256 devices in a mesh: exp: 64 (over z, x, core), sub: 4 (over y).
Axes of the slice: x: 4, y: 4, z: 8, core: 2. Of those that a mesh axis runs over, the one named last changes fastest.
Arguments:
- sky_map: float32 [256, 8, 8, 128], P(('exp', 'sub')), may hold values from -6 to 6
- coeffs: bfloat16 [128, 12, 512, 512], P('exp', None, 'sub'), may hold values from -1.75 to 1.75
- observed: float32 [128, 512, 512], P('exp', 'sub'), may hold values from -6 to 6
- vert_taps: bfloat16 [12, 21], replicated, may hold values from -1.25 to 1.25
- horiz_taps: bfloat16 [12, 21], replicated, may hold values from -1.25 to 1.25
- owner_ids: int32 [128, 64, 4, 1], P('exp', 'sub'), may hold values from 0 to 63; in each aligned block of 64 rows (0 to 63, 64 to 127, ..., all dimensions but the last counted through in order) at most 2 rows name the same one
- offset: int32 [128, 64, 4], P('exp', 'sub'), may hold values from 0 to 7
Outputs:
- sky_final: float32 [256, 8, 8, 128], P(('exp', 'sub'))
- clipped: float32 [128, 512, 512], P('exp', 'sub')
The draws below stay inside these ranges and needn't reach their ends.
Inputs may be any that keep to these rules, and one draw needn't show every extreme that they name: Patch (e, r, q) reads sky tile owner_ids[e, r, q, 0] * 4 + r // 16. Among the 64 patches of one band of one piece (the rows of one device's piece) no owner is named more than 2 times, and in every draw some band names one owner exactly 2 times.
All inputs are finite; a program needn't handle non-finite values.
Results may differ from the reference program's by a relative error of at most 0.0035.
Values may be sent and summed in bfloat16 or wider, within the bound.
A program may use at most 64 MiB of HBM per device.

```python
import math
from functools import partial
import jax
import jax.numpy as jnp
import numpy as np
from jax import lax

PIX = 512
MODES = 12
TAPS = 21
PH = 8
PW = 128
SKY_DEV = 8
STEPS = 2
BANDS = 4
PROWS = 64
PCOLS = 4
BANDP = 64
CAP = 2
PIECES = 128
TILES = 256
N_EXP = 64


def touch_ends(array, own_key, smallest, largest):
    index_at = [jax.random.randint(jax.random.fold_in(own_key, axis), (), 0, length) for axis, length in enumerate(array.shape)]
    main_axis = array.shape.index(max(array.shape))
    neighbour = index_at[:main_axis] + [(index_at[main_axis] + 1) % array.shape[main_axis]] + index_at[main_axis + 1:]
    return array.at[tuple(index_at)].set(smallest).at[tuple(neighbour)].set(largest)


def level_of(key, extent, shards, smallest, largest):
    def one(position, parts):
        steps = jax.random.uniform(jax.random.fold_in(jax.random.fold_in(key, 6), position), (parts,), jnp.float32, smallest / len(shards), largest / len(shards))
        return jnp.repeat(jnp.exp(steps), extent[position] // parts).reshape((-1,) + (1,) * (len(extent) - position - 1))

    loudness = one(*shards[0])
    for cut in shards[1:]:
        loudness = loudness * one(*cut)
    return loudness


def shared_out(stream_key, own, number, rows, amount, top, bound, lean):
    ranking = jax.random.permutation(stream_key, amount)
    heavy_load, ordinary = load_shares(amount, rows * top, bound, lean, True), load_shares(amount, rows * top, bound, lean, False)
    places = jnp.arange(amount)

    def named(lengths, offset_by):
        used = int((lengths > 0).sum())
        fixed = max(1, used // 4)
        moved = fixed + (places - fixed + offset_by * (used - fixed)) % max(1, amount - fixed)
        return jnp.zeros((amount,), jnp.int32).at[ranking[jnp.where(places < fixed, places, moved)]].set(jnp.asarray(lengths, jnp.int32))

    lengths = jnp.where(number % 4 == 0, named(heavy_load, number // 4), named(ordinary, number - number // 4 - 1))
    mixed = jax.random.permutation(jax.random.fold_in(own, 3), amount)
    source_of, sink = mixed[0:amount // 2 * 2:2], mixed[1:amount // 2 * 2:2]
    room = jnp.minimum(lengths[source_of] - 1, bound - lengths[sink]) // 2
    room = jnp.where((source_of == ranking[0]) | (sink == ranking[0]) | (lengths[sink] == 0), 0, jnp.maximum(room, 0))
    moved = jax.random.randint(jax.random.fold_in(own, 4), (amount // 2,), 0, 1 << 20) % (room + 1)
    lengths = lengths.at[source_of].add(-moved).at[sink].add(moved)
    members = jnp.searchsorted(jnp.cumsum(lengths), jnp.arange(rows * top), side="right").astype(jnp.int32)
    listing = members.reshape(top, rows).T
    listing = listing[jax.random.permutation(jax.random.fold_in(own, 1), rows)]
    offset_by = jax.random.randint(jax.random.fold_in(own, 2), (rows, 1), 0, top)
    return jnp.take_along_axis(listing, (jnp.arange(top)[None, :] + offset_by) % top, axis=1)


def load_shares(count, total, bound, lean, full):
    loads = [(1 << 20) // math.isqrt(rank ** lean) + 1 for rank in range(1, count + 1)]
    largest = bound if full else min(bound, max(-(-total // count), total * loads[0] // sum(loads)))
    least = 1 if total - largest >= count - 1 else 0
    holding, rest = [largest] + [least] * (count - 1), total - largest - least * (count - 1)
    while rest > 0:
        movable = [i for i in range(1, count) if holding[i] < largest] or [i for i in range(1, count) if holding[i] < bound]
        mass, budget = sum([loads[i] for i in movable]), rest
        for i in movable:
            addition = min(bound - holding[i], max(1, budget * loads[i] // mass), rest)
            holding[i] = holding[i] + addition
            rest = rest - addition
    return np.array(holding)


def gaussian(own_key, dims, width, limit, pieces=(), kind=jnp.bfloat16):
    entries = jax.random.normal(own_key, dims, jnp.float32) * width
    if len(pieces) > 0:
        entries = level_of(own_key, dims, pieces, -0.22, 0.18) * entries
    return jnp.clip(entries, min=-limit, max=limit).astype(kind)


def setup_inputs(seed: int = 0) -> dict:
    key_list = jax.random.split(jax.random.key(seed), 8)
    sky_map = gaussian(key_list[0], (TILES, SKY_DEV, PH, PW), 1.0, 6.0, ((0, 256),), jnp.float32)
    coeffs = gaussian(key_list[1], (PIECES, MODES, PIX, PIX), MODES ** -0.5, 1.75, ((0, 64), (2, 4)))
    observed = gaussian(key_list[2], (PIECES, PIX, PIX), 1.0, 6.0, ((0, 64), (1, 4)), jnp.float32)
    vert_taps = gaussian(key_list[3], (MODES, TAPS), TAPS ** -0.5, 1.25)
    horiz_taps = gaussian(key_list[4], (MODES, TAPS), TAPS ** -0.5, 1.25)
    owner_ids_keys = jax.random.split(jax.random.fold_in(key_list[5], 1), PIECES * PROWS * PCOLS // BANDP)
    owner_ids_turns = jax.random.permutation(jax.random.fold_in(key_list[5], 3), PIECES * PROWS * PCOLS // BANDP)
    owner_ids = jax.vmap(lambda own, number: shared_out(jax.random.fold_in(key_list[5], 2), own, number, BANDP, N_EXP, 1, CAP, 2))(owner_ids_keys, owner_ids_turns).reshape((PIECES, PROWS, PCOLS, 1))
    offset = touch_ends(jax.random.randint(key_list[6], (PIECES, PROWS, PCOLS), 0, SKY_DEV), jax.random.fold_in(key_list[6], 1), 0, SKY_DEV - 1).astype(jnp.int32)
    return dict(sky_map=sky_map, coeffs=coeffs, observed=observed, vert_taps=vert_taps, horiz_taps=horiz_taps, owner_ids=owner_ids, offset=offset)


ETA = 0.5
DELTA = 1.0


def correlate(filters, picture, axis_dim, reverse):
    margin = (filters.shape[1] - 1) // 2
    widths = [(0, 0), (0, 0), (0, 0)]
    widths[axis_dim] = (margin, margin)
    padded = jnp.pad(picture, widths)
    length = picture.shape[axis_dim]
    result = jnp.zeros(picture.shape, jnp.float32)
    for lag_index in range(filters.shape[1]):
        start_at = 2 * margin - lag_index if reverse else lag_index
        window = lax.slice_in_dim(padded, start_at, start_at + length, axis=axis_dim)
        result = result + filters[:, lag_index][:, None, None] * window
    return result


def patch_ids(owner_ids, offset):
    rows_band = PROWS // BANDS
    row_index = lax.broadcasted_iota(jnp.int32, offset.shape, 1)
    tile_index = owner_ids[..., 0] * BANDS + row_index // rows_band
    return (tile_index * SKY_DEV + offset).astype(jnp.int32).reshape(-1)


def to_image(patches):
    stacked = patches.reshape(PIECES, PROWS, PCOLS, PH, PW)
    return stacked.transpose(0, 1, 3, 2, 4).reshape(PIECES, PIX, PIX)


def to_patches(picture):
    stacked = picture.reshape(PIECES, PROWS, PH, PCOLS, PW)
    return stacked.transpose(0, 1, 3, 2, 4).reshape(PIECES * PROWS * PCOLS, PH * PW)


def piece_step(vertical, horizontal, inputs):
    picture, coeff_piece, observed_piece = inputs
    coeff_f = coeff_piece.astype(jnp.float32)
    stacked = jnp.broadcast_to(picture.astype(jnp.float32)[None], (MODES, PIX, PIX))
    smoothed = lax.optimization_barrier(correlate(vertical, stacked, 1, False).astype(jnp.bfloat16))
    blurred = correlate(horizontal, smoothed.astype(jnp.float32), 2, False)
    modeled = jnp.sum(coeff_f * blurred, axis=0)
    clipped = jnp.clip(modeled - observed_piece, -DELTA, DELTA)
    weighted = lax.optimization_barrier((coeff_f * clipped[None]).astype(jnp.bfloat16))
    back_rows = lax.optimization_barrier(correlate(horizontal, weighted.astype(jnp.float32), 2, True).astype(jnp.bfloat16))
    gradient = jnp.sum(correlate(vertical, back_rows.astype(jnp.float32), 1, True), axis=0)
    return clipped, gradient


def reference(sky_map, coeffs, observed, vert_taps, horiz_taps, owner_ids, offset):
    vertical = vert_taps.astype(jnp.float32)
    horizontal = horiz_taps.astype(jnp.float32)
    indices = patch_ids(owner_ids, offset)
    segments = TILES * SKY_DEV
    counts = jax.ops.segment_sum(jnp.ones(indices.shape, jnp.float32), indices, num_segments=segments)
    current = sky_map.reshape(segments, PH * PW)
    clipped = jnp.zeros(observed.shape, jnp.float32)
    for step_index in range(STEPS):
        rounded = lax.optimization_barrier(current.astype(jnp.bfloat16))
        pictures = to_image(rounded[indices])
        clipped, gradient = lax.map(partial(piece_step, vertical, horizontal), (pictures, coeffs, observed))
        summed = jax.ops.segment_sum(to_patches(gradient), indices, num_segments=segments)
        current = current - ETA * summed / jnp.maximum(counts, 1.0)[:, None]
    return current.reshape(TILES, SKY_DEV, PH, PW), clipped
```

```python
import jax
import jax.numpy as jnp
from jax import lax
from jax.experimental import pallas as pl
from jax.experimental.pallas import tpu as pltpu
from jax.sharding import PartitionSpec as P

ETA = 0.5
DELTA = 1.0

NZ, NX, NC = 8, 4, 2
COLS = NX * NC
MODES = 12
TAPS = 21
MARGIN = 10
PIECES = 2
HEIGHT = 128
BREADTH = 512
HALO = 16
EXT = HEIGHT + 2 * HALO
PER_TILE = 8
PH = 8
PW = 128
ROWS = HEIGHT // PH
QCOLS = BREADTH // PW
SIZE = PH * PW
WIDE = SIZE + PW
NEAR_ORDER = (0, 1, 7, 2, 6, 3, 5, 4)
FAR_ORDER = (4, 3, 5, 2, 6, 1, 7)
VMEM_LIMIT = 60 * 1024 * 1024


def place():
    e = lax.axis_index("exp")
    y = lax.axis_index("sub")
    return e // COLS, lax.rem(e // NC, NX), lax.rem(e, NC), y


def at_exp(z, x, c):
    return {"exp": (z * NX + x) * NC + c}


def remote(src, dst, send_sem, recv_sem, device):
    return pltpu.make_async_remote_copy(
        src_ref=src, dst_ref=dst, send_sem=send_sem, recv_sem=recv_sem,
        device_id=device, device_id_type=pl.DeviceIdType.MESH,
    )


def greet(across):
    z, x, c, y = place()
    barrier = pltpu.get_barrier_semaphore()
    many = 0
    for dz in range(1, NZ):
        pl.semaphore_signal(barrier, inc=1, device_id=at_exp(lax.rem(z + dz, NZ), x, c))
        many += 1
    for dx in range(NX):
        for dc in range(NC):
            if dx + dc > 0 and (dc == 0 or dx == 0 or across):
                pl.semaphore_signal(
                    barrier, inc=1, device_id=at_exp(z, lax.rem(x + dx, NX), lax.rem(c + dc, NC))
                )
                many += 1
    bands = lax.axis_size("sub")

    @pl.when(y > 0)
    def _():
        pl.semaphore_signal(barrier, inc=1, device_id={"sub": y - 1})

    @pl.when(y < bands - 1)
    def _():
        pl.semaphore_signal(barrier, inc=1, device_id={"sub": y + 1})

    pl.semaphore_wait(barrier, many + jnp.minimum(y, 1) + jnp.minimum(bands - 1 - y, 1))


def spread_tiles(table, sems):
    (zs, zr, xs, xr, cs, cr) = sems
    z, x, c, _ = place()
    col = x * NC + c

    def tile(col_at, z_at):
        return table.at[pl.ds((col_at * NZ + z_at) * PER_TILE, PER_TILE)]

    def along_z(dz, back):
        z_from = lax.rem(z - dz + NZ, NZ) if back else z
        block = tile(col, z_from)
        return remote(block, block, zs.at[dz], zr.at[dz], at_exp(lax.rem(z + dz, NZ), x, c))

    def along_x(dz, dx, back):
        x_from = lax.rem(x - dx + NX, NX) if back else x
        block = tile(x_from * NC + c, lax.rem(z - dz + NZ, NZ))
        return remote(block, block, xs.at[dz, dx], xr.at[dz, dx], at_exp(z, lax.rem(x + dx, NX), c))

    def to_twin(dz, dx, back):
        c_from = 1 - c if back else c
        block = tile(lax.rem(x - dx + NX, NX) * NC + c_from, lax.rem(z - dz + NZ, NZ))
        return remote(block, block, cs.at[dz, dx], cr.at[dz, dx], at_exp(z, x, 1 - c))

    for dz in FAR_ORDER:
        along_z(dz, False).start()
    for dz in NEAR_ORDER:
        if dz > 0:
            along_z(dz, True).wait_recv()
        for dx in (2, 1, 3):
            along_x(dz, dx, False).start()
        to_twin(dz, 0, False).start()
    for dz in NEAR_ORDER:
        for dx in (1, 3, 2):
            along_x(dz, dx, True).wait_recv()
            to_twin(dz, dx, False).start()
    for dz in NEAR_ORDER:
        for dx in range(NX):
            to_twin(dz, dx, True).wait_recv()
    for dz in range(NZ):
        if dz > 0:
            along_z(dz, False).wait_send()
        for dx in range(NX):
            if dx > 0:
                along_x(dz, dx, False).wait_send()
            to_twin(dz, dx, False).wait_send()


def gather_rows(wanted, table, ext, pair):
    for p in range(PIECES):
        for q in range(QCOLS):
            both = []
            for half in range(2):
                n = wanted[(p * ROWS + pair * 2 + half) * QCOLS + q]
                both.append(table[n].astype(jnp.float32))
            block = jnp.concatenate(both, axis=0).astype(jnp.bfloat16)
            if isinstance(pair, int):
                start = HALO + pair * 2 * PH
            else:
                start = pl.multiple_of(HALO + pair * 2 * PH, 2 * PH)
            ext[p, pl.ds(start, 2 * PH), q * PW:(q + 1) * PW] = block


def fetch_image(wanted, table, ext, rim_out, rim_in, hs, hr):
    _, _, _, y = place()
    bands = lax.axis_size("sub")
    pairs = ROWS // 2
    gather_rows(wanted, table, ext, 0)
    gather_rows(wanted, table, ext, pairs - 1)
    rim_out[0] = ext[:, HALO:2 * HALO, :]
    rim_out[1] = ext[:, HEIGHT:HEIGHT + HALO, :]
    up = remote(rim_out.at[0], rim_in.at[1], hs.at[0], hr.at[1], {"sub": y - 1})
    down = remote(rim_out.at[1], rim_in.at[0], hs.at[1], hr.at[0], {"sub": y + 1})

    @pl.when(y > 0)
    def _():
        up.start()

    @pl.when(y < bands - 1)
    def _():
        down.start()

    def more(pair, carry):
        gather_rows(wanted, table, ext, pair)
        return carry

    lax.fori_loop(1, pairs - 1, more, 0)
    none = jnp.zeros((PIECES, HALO, BREADTH), jnp.bfloat16)

    @pl.when(y > 0)
    def _():
        down.wait_recv()
        ext[:, 0:HALO, :] = rim_in[0]

    @pl.when(y == 0)
    def _():
        ext[:, 0:HALO, :] = none

    @pl.when(y < bands - 1)
    def _():
        up.wait_recv()
        ext[:, HALO + HEIGHT:EXT, :] = rim_in[1]

    @pl.when(y == bands - 1)
    def _():
        ext[:, HALO + HEIGHT:EXT, :] = none

    @pl.when(y > 0)
    def _():
        up.wait_send()

    @pl.when(y < bands - 1)
    def _():
        down.wait_send()


def reduce_patches(rows, select, extra, sky, sky_new, scratch):
    (rim_in, grad, stacked, outgoing, incoming, line_out, line_in, hs, hr, axs, axr, bzs, bzr) = scratch
    z, x, c, y = place()
    bands = lax.axis_size("sub")
    col = x * NC + c
    up = remote(rows.at[:, pl.ds(0, HALO), :], rim_in.at[1], hs.at[0], hr.at[1], {"sub": y - 1})
    down = remote(
        rows.at[:, pl.ds(HALO + HEIGHT, HALO), :], rim_in.at[0], hs.at[1], hr.at[0], {"sub": y + 1}
    )

    @pl.when(y > 0)
    def _():
        up.start()

    @pl.when(y < bands - 1)
    def _():
        down.start()

    strips = [(p, q, (p * QCOLS + q) * HEIGHT) for p in range(PIECES) for q in range(QCOLS)]
    for p, q, at in strips:
        grad[at:at + HEIGHT, :] = rows[p, HALO:HALO + HEIGHT, q * PW:(q + 1) * PW]

    @pl.when(y > 0)
    def _():
        down.wait_recv()
        for p, q, at in strips:
            grad[at:at + HALO, :] += rim_in[0, p, :, q * PW:(q + 1) * PW]

    @pl.when(y < bands - 1)
    def _():
        up.wait_recv()
        for p, q, at in strips:
            grad[at + HEIGHT - HALO:at + HEIGHT, :] += rim_in[1, p, :, q * PW:(q + 1) * PW]

    for p, q, at in strips:
        for i in range(PH):
            lines = grad[pl.ds(at + i, ROWS, stride=PH), :]
            stacked[at // PH:at // PH + ROWS, i * PW:(i + 1) * PW] = lines.astype(jnp.bfloat16)
    stacked[:, SIZE:] = extra[...]

    def across(half, dx, dc, back):
        x_to, c_to = lax.rem(x + dx, NX), lax.rem(c + dc, NC)
        x_from, c_from = lax.rem(x - dx + NX, NX), lax.rem(c + dc, NC)
        source = x_from * NC + c_from if back else col
        return remote(
            outgoing.at[half, x_to * NC + c_to], incoming.at[half, source],
            axs.at[half, dx, dc], axr.at[half, dx, dc], at_exp(z, x_to, c_to),
        )

    peers = [(2, 0), (2, 1), (1, 0), (1, 1), (3, 0), (3, 1), (0, 1)]
    for half in range(2):
        picked = jnp.dot(
            select[half], stacked[...], preferred_element_type=jnp.float32
        ).astype(jnp.bfloat16)
        outgoing[half] = picked.reshape(COLS, HALO, WIDE)
        for dx, dc in peers:
            across(half, dx, dc, False).start()
        incoming[half, col] = outgoing[half, col]

    def along_z(rel, start_at):
        return remote(
            line_out.at[rel], line_in.at[rel], bzs.at[rel], bzr.at[rel],
            at_exp(lax.rem(z + rel, NZ), x, c),
        )

    for half in range(2):
        for dx, dc in peers[::-1]:
            across(half, dx, dc, True).wait_recv()
        arrived = incoming[half].reshape(COLS * HALO, WIDE)
        marks = arrived[:, SIZE:].astype(jnp.float32).T[0:4 * PER_TILE].astype(jnp.bfloat16)
        totals = jnp.dot(marks, arrived[:, :SIZE], preferred_element_type=jnp.float32)
        many = jnp.dot(
            marks, jnp.ones((COLS * HALO, PW), jnp.bfloat16), preferred_element_type=jnp.float32
        )
        for pos in (2, 1, 3, 0) if half == 0 else (0, 3, 1, 2):
            rel = (pos + 4 * (1 - half) + NZ - 2) % NZ
            line = slice(pos * PER_TILE, (pos + 1) * PER_TILE)
            line_out[rel, :, 0:SIZE] = totals[line].astype(jnp.bfloat16)
            line_out[rel, :, SIZE:] = many[line].astype(jnp.bfloat16)
            if rel > 0:
                along_z(rel, True).start()
    total = line_out[0].astype(jnp.float32)
    for rel in NEAR_ORDER[1:]:
        along_z(rel, False).wait_recv()
        total = total + line_in[rel].astype(jnp.float32)
    scale = ETA / jnp.maximum(total[:, SIZE:], 1.0)
    for i in range(PH):
        old = sky[pl.ds(i, PER_TILE, stride=PH), :]
        sky_new[pl.ds(i, PER_TILE, stride=PH), :] = old - scale * total[:, i * PW:(i + 1) * PW]
    for half in range(2):
        for dx, dc in peers:
            across(half, dx, dc, False).wait_send()
    for rel in range(1, NZ):
        along_z(rel, False).wait_send()

    @pl.when(y > 0)
    def _():
        up.wait_send()

    @pl.when(y < bands - 1)
    def _():
        down.wait_send()


def own_tile(sky, table):
    z, x, c, _ = place()
    start = ((x * NC + c) * NZ + z) * PER_TILE
    for k in range(PER_TILE):
        table[start + k] = sky[k * PH:(k + 1) * PH, :].astype(jnp.bfloat16)


def fetch_scratch():
    return [
        pltpu.VMEM((COLS * NZ * PER_TILE, PH, PW), jnp.bfloat16),
        pltpu.VMEM((2, PIECES, HALO, BREADTH), jnp.bfloat16),
        pltpu.VMEM((2, PIECES, HALO, BREADTH), jnp.bfloat16),
        pltpu.SemaphoreType.DMA((NZ,)),
        pltpu.SemaphoreType.DMA((NZ,)),
        pltpu.SemaphoreType.DMA((NZ, NX)),
        pltpu.SemaphoreType.DMA((NZ, NX)),
        pltpu.SemaphoreType.DMA((NZ, NX)),
        pltpu.SemaphoreType.DMA((NZ, NX)),
        pltpu.SemaphoreType.DMA((2,)),
        pltpu.SemaphoreType.DMA((2,)),
    ]


def reduce_scratch():
    return [
        pltpu.VMEM((2, PIECES, HALO, BREADTH), jnp.float32),
        pltpu.VMEM((PIECES * QCOLS * HEIGHT, PW), jnp.float32),
        pltpu.VMEM((PIECES * ROWS * QCOLS, WIDE), jnp.bfloat16),
        pltpu.VMEM((2, COLS, HALO, WIDE), jnp.bfloat16),
        pltpu.VMEM((2, COLS, HALO, WIDE), jnp.bfloat16),
        pltpu.VMEM((NZ, PER_TILE, WIDE), jnp.bfloat16),
        pltpu.VMEM((NZ, PER_TILE, WIDE), jnp.bfloat16),
        pltpu.SemaphoreType.DMA((2,)),
        pltpu.SemaphoreType.DMA((2,)),
        pltpu.SemaphoreType.DMA((2, NX, NC)),
        pltpu.SemaphoreType.DMA((2, NX, NC)),
        pltpu.SemaphoreType.DMA((NZ,)),
        pltpu.SemaphoreType.DMA((NZ,)),
    ]


N_FETCH = 11
N_REDUCE = 13


def first_kernel(wanted, sky, ext, *scratch):
    table, rim_out, rim_in = scratch[:3]
    greet(False)
    own_tile(sky, table)
    spread_tiles(table, scratch[3:9])
    fetch_image(wanted, table, ext, rim_out, rim_in, *scratch[9:11])


def middle_kernel(wanted, sky, rows, select, extra, sky_new, ext, *scratch):
    table, rim_out, rim_in = scratch[:3]
    greet(True)
    reduce_patches(rows, select, extra, sky, sky_new, scratch[N_FETCH:])
    own_tile(sky_new, table)
    spread_tiles(table, scratch[3:9])
    fetch_image(wanted, table, ext, rim_out, rim_in, *scratch[9:11])


def last_kernel(sky, rows, select, extra, sky_new, *scratch):
    greet(True)
    reduce_patches(rows, select, extra, sky, sky_new, scratch)


def convolve(block, centre, edge, transposed):
    dims = (((1,), (1 if transposed else 0,)), ((), ()))
    half = BREADTH // 2

    def product(a, b):
        return lax.dot_general(a, b, dims, preferred_element_type=jnp.float32)

    left = product(block[:, :half], centre)
    right = product(block[:, half:], centre)
    seam = product(block[:, PW:PW + half], edge)
    return [left[:, :PW], left[:, PW:] + seam[:, :PW], right[:, :PW] + seam[:, PW:], right[:, PW:]]


def compute_kernel(ext, coeffs, observed, tall, wide, bands, seams, clipped, rows, smooth, back, model):
    for p in range(PIECES):
        for m in range(MODES):
            smooth[m, p * HEIGHT:(p + 1) * HEIGHT, :] = jnp.dot(
                tall[m * HEIGHT:(m + 1) * HEIGHT, :], ext[p], preferred_element_type=jnp.float32
            ).astype(jnp.bfloat16)
    model[...] = -observed[...]

    def forward(m, carry):
        parts = convolve(smooth[m], bands[m], seams[m], False)
        for q in range(QCOLS):
            cols = slice(q * PW, (q + 1) * PW)
            for p in range(PIECES):
                model[p, :, cols] += (
                    coeffs[p, m, :, cols].astype(jnp.float32) * parts[q][p * HEIGHT:(p + 1) * HEIGHT]
                )
        return carry

    lax.fori_loop(0, MODES, forward, 0)
    clipped[...] = jnp.clip(model[...], -DELTA, DELTA)

    def adjoint(m, carry):
        weighted = jnp.concatenate(
            [
                (coeffs[p, m].astype(jnp.float32) * clipped[p]).astype(jnp.bfloat16)
                for p in range(PIECES)
            ],
            axis=0,
        )
        parts = convolve(weighted, bands[m], seams[m], True)
        start = pl.multiple_of(m * HEIGHT, HEIGHT)
        for q in range(QCOLS):
            cols = slice(q * PW, (q + 1) * PW)
            for p in range(PIECES):
                back[p, pl.ds(start, HEIGHT), cols] = parts[q][p * HEIGHT:(p + 1) * HEIGHT].astype(
                    jnp.bfloat16
                )
        return carry

    lax.fori_loop(0, MODES, adjoint, 0)
    for p in range(PIECES):
        rows[p] = jnp.dot(wide[...], back[p], preferred_element_type=jnp.float32)


def whole(count, smem=()):
    return [
        pl.BlockSpec(memory_space=pltpu.SMEM if i in smem else pltpu.VMEM) for i in range(count)
    ]


def call(kernel, outs, scratch, smem, collective, *args):
    params = dict(vmem_limit_bytes=VMEM_LIMIT)
    if collective is not None:
        params.update(collective_id=collective, has_side_effects=True)
    return pl.pallas_call(
        kernel,
        out_shape=outs,
        in_specs=whole(len(args), smem),
        out_specs=jax.tree.map(lambda _: pl.BlockSpec(memory_space=pltpu.VMEM), outs),
        scratch_shapes=scratch,
        compiler_params=pltpu.CompilerParams(**params),
    )(*args)


def lag_table(filters, shape, lag):
    lags = lax.broadcasted_iota(jnp.int32, (TAPS,) + shape, 0)
    chosen = (lags == lag[None]).astype(jnp.bfloat16)
    return jnp.tensordot(filters, chosen, axes=1, preferred_element_type=jnp.float32).astype(jnp.bfloat16)


def per_device(sky_map, coeffs, observed, vert_taps, horiz_taps, owner_ids, offset):
    z = lax.axis_index("exp") // COLS
    sky = sky_map.reshape(PER_TILE * PH, PW)

    owner = owner_ids[..., 0]
    col, tile_z = owner % COLS, owner // COLS
    wanted = ((col * NZ + tile_z) * PER_TILE + offset).reshape(-1)

    ranked = owner.transpose(0, 2, 1).reshape(PIECES, QCOLS * ROWS)
    places = jnp.arange(QCOLS * ROWS)
    earlier = (ranked[:, :, None] == ranked[:, None, :]) & (places[None, :] < places[:, None])[None]
    rank = jnp.sum(earlier.astype(jnp.int32), axis=2)
    turned = (ranked // COLS - z + NZ + 2) % NZ
    half, pos = 1 - turned // 4, turned % 4
    piece = jnp.arange(PIECES)[:, None]
    slot = ((half * COLS + ranked % COLS) * 4 + pos) * 4 + piece * 2 + rank
    slots = 2 * COLS * HALO
    select = (
        lax.broadcasted_iota(jnp.int32, (slots, 1), 0) == slot.reshape(1, -1)
    ).astype(jnp.bfloat16).reshape(2, COLS * HALO, PIECES * QCOLS * ROWS)
    mark = pos * PER_TILE + offset.transpose(0, 2, 1).reshape(PIECES, QCOLS * ROWS)
    extra = (mark.reshape(-1, 1) == lax.broadcasted_iota(jnp.int32, (1, PW), 1)).astype(jnp.bfloat16)

    i = lax.broadcasted_iota(jnp.int32, (HEIGHT, EXT), 0)
    a = lax.broadcasted_iota(jnp.int32, (HEIGHT, EXT), 1)
    tall = lag_table(vert_taps, (HEIGHT, EXT), a - HALO - i + MARGIN).reshape(MODES * HEIGHT, EXT)
    wide = tall.T
    side = BREADTH // 2
    w = lax.broadcasted_iota(jnp.int32, (side, side), 0)
    j = lax.broadcasted_iota(jnp.int32, (side, side), 1)
    bands = lag_table(horiz_taps, (side, side), w - j + MARGIN)
    seams = jnp.where((w < PW) != (j < PW), bands, jnp.zeros((), jnp.bfloat16))

    sky_shape = jax.ShapeDtypeStruct(sky.shape, jnp.float32)
    ext_shape = jax.ShapeDtypeStruct((PIECES, EXT, BREADTH), jnp.bfloat16)
    clip_shape = jax.ShapeDtypeStruct(observed.shape, jnp.float32)
    rows_shape = jax.ShapeDtypeStruct((PIECES, EXT, BREADTH), jnp.float32)
    compute_scratch = [
        pltpu.VMEM((MODES, PIECES * HEIGHT, BREADTH), jnp.bfloat16),
        pltpu.VMEM((PIECES, MODES * HEIGHT, BREADTH), jnp.bfloat16),
        pltpu.VMEM((PIECES, HEIGHT, BREADTH), jnp.float32),
    ]

    def compute(ext):
        return call(
            compute_kernel, (clip_shape, rows_shape), compute_scratch, (), None,
            ext, coeffs, observed, tall, wide, bands, seams,
        )

    ext = call(first_kernel, ext_shape, fetch_scratch(), (0,), 0, wanted, sky)
    _, rows = compute(ext)
    sky, ext = call(
        middle_kernel, (sky_shape, ext_shape), fetch_scratch() + reduce_scratch(), (0,), 1,
        wanted, sky, rows, select, extra,
    )
    clipped, rows = compute(ext)
    sky = call(last_kernel, sky_shape, reduce_scratch(), (), 2, sky, rows, select, extra)
    return sky.reshape(sky_map.shape), clipped


def solution(mesh):
    return jax.shard_map(
        per_device,
        mesh=mesh,
        in_specs=(
            P(("exp", "sub"), None, None, None),
            P("exp", None, "sub", None),
            P("exp", "sub", None),
            P(),
            P(),
            P("exp", "sub", None, None),
            P("exp", "sub", None),
        ),
        out_specs=(P(("exp", "sub"), None, None, None), P("exp", "sub", None)),
        check_vma=False,
    )
```

```python
import jax
import jax.numpy as jnp
from jax import lax
from jax.experimental import pallas as pl
from jax.experimental.pallas import tpu as pltpu
from jax.sharding import PartitionSpec as P

STEPS = 2
ETA = 0.5
DELTA = 1.0

NZ, NX, NC = 8, 4, 2
COLS = NX * NC
MODES = 12
TAPS = 21
MARGIN = 10
PIECES = 2
HEIGHT = 128
BREADTH = 512
HALO = 16
EXT = HEIGHT + 2 * HALO
PER_TILE = 8
PH = 8
PW = 128
ROWS = HEIGHT // PH
QCOLS = BREADTH // PW
SIZE = PH * PW
WIDE = SIZE + PW
NEAR_ORDER = (0, 1, 7, 2, 6, 3, 5, 4)
FAR_ORDER = (4, 3, 5, 2, 6, 1, 7)
VMEM_LIMIT = 60 * 1024 * 1024


def place():
    e = lax.axis_index("exp")
    y = lax.axis_index("sub")
    return e // COLS, lax.rem(e // NC, NX), lax.rem(e, NC), y


def at_exp(z, x, c):
    return {"exp": (z * NX + x) * NC + c}


def remote(src, dst, send_sem, recv_sem, device):
    return pltpu.make_async_remote_copy(
        src_ref=src, dst_ref=dst, send_sem=send_sem, recv_sem=recv_sem,
        device_id=device, device_id_type=pl.DeviceIdType.MESH,
    )


def greet():
    z, x, c, y = place()
    barrier = pltpu.get_barrier_semaphore()
    many = 0
    for dz in range(1, NZ):
        pl.semaphore_signal(barrier, inc=1, device_id=at_exp(lax.rem(z + dz, NZ), x, c))
        many += 1
    for dx in range(NX):
        for dc in range(NC):
            if dx + dc > 0:
                pl.semaphore_signal(
                    barrier, inc=1, device_id=at_exp(z, lax.rem(x + dx, NX), lax.rem(c + dc, NC))
                )
                many += 1
    bands = lax.axis_size("sub")

    @pl.when(y > 0)
    def _():
        pl.semaphore_signal(barrier, inc=1, device_id={"sub": y - 1})

    @pl.when(y < bands - 1)
    def _():
        pl.semaphore_signal(barrier, inc=1, device_id={"sub": y + 1})

    return lambda: pl.semaphore_wait(
        barrier, many + jnp.minimum(y, 1) + jnp.minimum(bands - 1 - y, 1)
    )


def spread_tiles(table, sems, early, late):
    (zs, zr, xs, xr, cs, cr) = sems
    z, x, c, _ = place()
    col = x * NC + c

    def tile(col_at, z_at):
        return table.at[pl.ds((col_at * NZ + z_at) * PER_TILE, PER_TILE)]

    def along_z(dz, back):
        z_from = lax.rem(z - dz + NZ, NZ) if back else z
        block = tile(col, z_from)
        return remote(block, block, zs.at[dz], zr.at[dz], at_exp(lax.rem(z + dz, NZ), x, c))

    def along_x(dz, dx, back):
        x_from = lax.rem(x - dx + NX, NX) if back else x
        block = tile(x_from * NC + c, lax.rem(z - dz + NZ, NZ))
        return remote(block, block, xs.at[dz, dx], xr.at[dz, dx], at_exp(z, lax.rem(x + dx, NX), c))

    def to_twin(dz, dx, back):
        c_from = 1 - c if back else c
        block = tile(lax.rem(x - dx + NX, NX) * NC + c_from, lax.rem(z - dz + NZ, NZ))
        return remote(block, block, cs.at[dz, dx], cr.at[dz, dx], at_exp(z, x, 1 - c))

    for dz in FAR_ORDER:
        along_z(dz, False).start()
    early()
    for dz in NEAR_ORDER:
        if dz > 0:
            along_z(dz, True).wait_recv()
        for dx in (2, 1, 3):
            along_x(dz, dx, False).start()
        to_twin(dz, 0, False).start()
    late()
    for dz in NEAR_ORDER:
        for dx in (1, 3, 2):
            along_x(dz, dx, True).wait_recv()
            to_twin(dz, dx, False).start()
    for dz in NEAR_ORDER:
        for dx in range(NX):
            to_twin(dz, dx, True).wait_recv()
    for dz in range(NZ):
        if dz > 0:
            along_z(dz, False).wait_send()
        for dx in range(NX):
            if dx > 0:
                along_x(dz, dx, False).wait_send()
            to_twin(dz, dx, False).wait_send()


def gather_rows(owners, offsets, table, ext, pair):
    for p in range(PIECES):
        for q in range(QCOLS):
            both = []
            for half in range(2):
                r = pair * 2 + half
                owner = owners[p, q, 0, r]
                tile = lax.rem(owner, COLS) * NZ + owner // COLS
                both.append(table[tile * PER_TILE + offsets[p, q, r]].astype(jnp.float32))
            block = jnp.concatenate(both, axis=0).astype(jnp.bfloat16)
            if isinstance(pair, int):
                start = HALO + pair * 2 * PH
            else:
                start = pl.multiple_of(HALO + pair * 2 * PH, 2 * PH)
            ext[p, pl.ds(start, 2 * PH), q * PW:(q + 1) * PW] = block


def fetch_image(owners, offsets, table, ext, rim_out, rim_in, hs, hr):
    _, _, _, y = place()
    bands = lax.axis_size("sub")
    pairs = ROWS // 2
    gather_rows(owners, offsets, table, ext, 0)
    gather_rows(owners, offsets, table, ext, pairs - 1)
    rim_out[0] = ext[:, HALO:2 * HALO, :]
    rim_out[1] = ext[:, HEIGHT:HEIGHT + HALO, :]
    up = remote(rim_out.at[0], rim_in.at[1], hs.at[0], hr.at[1], {"sub": y - 1})
    down = remote(rim_out.at[1], rim_in.at[0], hs.at[1], hr.at[0], {"sub": y + 1})

    @pl.when(y > 0)
    def _():
        up.start()

    @pl.when(y < bands - 1)
    def _():
        down.start()

    def more(pair, carry):
        gather_rows(owners, offsets, table, ext, pair)
        return carry

    lax.fori_loop(1, pairs - 1, more, 0)
    none = jnp.zeros((PIECES, HALO, BREADTH), jnp.bfloat16)

    @pl.when(y > 0)
    def _():
        down.wait_recv()
        ext[:, 0:HALO, :] = rim_in[0]

    @pl.when(y == 0)
    def _():
        ext[:, 0:HALO, :] = none

    @pl.when(y < bands - 1)
    def _():
        up.wait_recv()
        ext[:, HALO + HEIGHT:EXT, :] = rim_in[1]

    @pl.when(y == bands - 1)
    def _():
        ext[:, HALO + HEIGHT:EXT, :] = none

    @pl.when(y > 0)
    def _():
        up.wait_send()

    @pl.when(y < bands - 1)
    def _():
        down.wait_send()


def reduce_patches(rows, select, extra, sky, sky_new, scratch):
    (rim_in, grad, stacked, outgoing, incoming, line_out, line_in), sems = scratch
    hs, hr, axs, axr, bzs, bzr = sems
    z, x, c, y = place()
    bands = lax.axis_size("sub")
    col = x * NC + c
    up = remote(rows.at[:, pl.ds(0, HALO), :], rim_in.at[1], hs.at[0], hr.at[1], {"sub": y - 1})
    down = remote(
        rows.at[:, pl.ds(HALO + HEIGHT, HALO), :], rim_in.at[0], hs.at[1], hr.at[0], {"sub": y + 1}
    )

    @pl.when(y > 0)
    def _():
        up.start()

    @pl.when(y < bands - 1)
    def _():
        down.start()

    strips = [(p, q, (p * QCOLS + q) * HEIGHT) for p in range(PIECES) for q in range(QCOLS)]
    for p, q, at in strips:
        grad[at:at + HEIGHT, :] = rows[p, HALO:HALO + HEIGHT, q * PW:(q + 1) * PW]

    @pl.when(y > 0)
    def _():
        down.wait_recv()
        for p, q, at in strips:
            grad[at:at + HALO, :] += rim_in[0, p, :, q * PW:(q + 1) * PW]

    @pl.when(y < bands - 1)
    def _():
        up.wait_recv()
        for p, q, at in strips:
            grad[at + HEIGHT - HALO:at + HEIGHT, :] += rim_in[1, p, :, q * PW:(q + 1) * PW]

    for p, q, at in strips:
        for i in range(PH):
            lines = grad[pl.ds(at + i, ROWS, stride=PH), :]
            stacked[at // PH:at // PH + ROWS, i * PW:(i + 1) * PW] = lines.astype(jnp.bfloat16)
    stacked[:, SIZE:] = extra[...]

    def across(half, dx, dc, back):
        x_to, c_to = lax.rem(x + dx, NX), lax.rem(c + dc, NC)
        x_from, c_from = lax.rem(x - dx + NX, NX), lax.rem(c + dc, NC)
        source = x_from * NC + c_from if back else col
        return remote(
            outgoing.at[half, x_to * NC + c_to], incoming.at[half, source],
            axs.at[half, dx, dc], axr.at[half, dx, dc], at_exp(z, x_to, c_to),
        )

    peers = [(2, 0), (2, 1), (1, 0), (1, 1), (3, 0), (3, 1), (0, 1)]
    for half in range(2):
        picked = jnp.dot(
            select[half], stacked[...], preferred_element_type=jnp.float32
        ).astype(jnp.bfloat16)
        outgoing[half] = picked.reshape(COLS, HALO, WIDE)
        for dx, dc in peers:
            across(half, dx, dc, False).start()
        incoming[half, col] = outgoing[half, col]

    def along_z(rel, start_at):
        return remote(
            line_out.at[rel], line_in.at[rel], bzs.at[rel], bzr.at[rel],
            at_exp(lax.rem(z + rel, NZ), x, c),
        )

    for half in range(2):
        for dx, dc in peers[::-1]:
            across(half, dx, dc, True).wait_recv()
        arrived = incoming[half].reshape(COLS * HALO, WIDE)
        marks = arrived[:, SIZE:].astype(jnp.float32).T[0:4 * PER_TILE].astype(jnp.bfloat16)
        totals = jnp.dot(marks, arrived[:, :SIZE], preferred_element_type=jnp.float32)
        many = jnp.dot(
            marks, jnp.ones((COLS * HALO, PW), jnp.bfloat16), preferred_element_type=jnp.float32
        )
        for pos in (2, 1, 3, 0) if half == 0 else (0, 3, 1, 2):
            rel = (pos + 4 * (1 - half) + NZ - 2) % NZ
            line = slice(pos * PER_TILE, (pos + 1) * PER_TILE)
            line_out[rel, :, 0:SIZE] = totals[line].astype(jnp.bfloat16)
            line_out[rel, :, SIZE:] = many[line].astype(jnp.bfloat16)
            if rel > 0:
                along_z(rel, True).start()
    total = line_out[0].astype(jnp.float32)
    for rel in NEAR_ORDER[1:]:
        along_z(rel, False).wait_recv()
        total = total + line_in[rel].astype(jnp.float32)
    scale = ETA / jnp.maximum(total[:, SIZE:], 1.0)
    for i in range(PH):
        old = sky[pl.ds(i, PER_TILE, stride=PH), :]
        sky_new[pl.ds(i, PER_TILE, stride=PH), :] = old - scale * total[:, i * PW:(i + 1) * PW]
    for half in range(2):
        for dx, dc in peers:
            across(half, dx, dc, False).wait_send()
    for rel in range(1, NZ):
        along_z(rel, False).wait_send()

    @pl.when(y > 0)
    def _():
        up.wait_send()

    @pl.when(y < bands - 1)
    def _():
        down.wait_send()


def own_tile(sky, table):
    z, x, c, _ = place()
    start = ((x * NC + c) * NZ + z) * PER_TILE
    for k in range(PER_TILE):
        table[start + k] = sky[k * PH:(k + 1) * PH, :].astype(jnp.bfloat16)


def convolve(block, centre, edge, transposed):
    dims = (((1,), (1 if transposed else 0,)), ((), ()))
    half = BREADTH // 2

    def product(a, b):
        return lax.dot_general(a, b, dims, preferred_element_type=jnp.float32)

    left = product(block[:, :half], centre)
    right = product(block[:, half:], centre)
    seam = product(block[:, PW:PW + half], edge)
    return [left[:, :PW], left[:, PW:] + seam[:, :PW], right[:, :PW] + seam[:, PW:], right[:, PW:]]


def diagonals(row, height):
    return pltpu.roll(jnp.broadcast_to(row, (height, row.shape[1])), 0, 1, stride=1, stride_axis=0)


def lag_rows(taps, lag):
    tap = lax.broadcasted_iota(jnp.int32, (TAPS, 2 * PW), 0)
    lane = lax.broadcasted_iota(jnp.int32, (TAPS, 2 * PW), 1)
    chosen = (tap == lag(lane)).astype(jnp.bfloat16)
    return jnp.dot(taps[...], chosen, preferred_element_type=jnp.float32)


def wrapped(lane):
    return jnp.where(lane < PW, lane, lane - 2 * PW)


def build_tall(vert, base, tall):
    base[...] = lag_rows(vert, lambda lane: lane - HALO + MARGIN)

    def one(m, carry):
        rows = diagonals(base[pl.ds(m, 1), :], HEIGHT)
        tall[pl.ds(pl.multiple_of(m * HEIGHT, HEIGHT), HEIGHT), :] = rows[:, :EXT].astype(jnp.bfloat16)
        return carry

    lax.fori_loop(0, MODES, one, 0)


def build_wide(vert, base, wide):
    base[...] = lag_rows(vert, lambda lane: MARGIN - HALO - wrapped(lane))

    def one(m, carry):
        rows = diagonals(base[pl.ds(m, 1), :], EXT)
        wide[m] = rows[:, :HEIGHT].astype(jnp.bfloat16)
        return carry

    lax.fori_loop(0, MODES, one, 0)


def build_bands(horiz, base, bands, seams):
    base[...] = lag_rows(horiz, lambda lane: MARGIN - wrapped(lane))
    side = BREADTH // 2
    w = lax.broadcasted_iota(jnp.int32, (side, side), 0)
    c = lax.broadcasted_iota(jnp.int32, (side, side), 1)
    near = jnp.abs(w - c) <= MARGIN
    across = near & ((w < PW) != (c < PW))

    def one(m, carry):
        rows = diagonals(base[pl.ds(m, 1), :], side)
        bands[m] = jnp.where(near, rows, 0.0).astype(jnp.bfloat16)
        seams[m] = jnp.where(across, rows, 0.0).astype(jnp.bfloat16)
        return carry

    lax.fori_loop(0, MODES, one, 0)


def build_slots(owners, offsets, own_rows, off_rows, select, extra):
    z, _, _, _ = place()

    def one(r, carry):
        for p in range(PIECES):
            for q in range(QCOLS):
                n = (p * QCOLS + q) * ROWS + r
                own_rows[pl.ds(n, 1), :] = jnp.full((1, PW), owners[p, q, 0, r], jnp.int32)
                off_rows[pl.ds(n, 1), :] = jnp.full((1, PW), offsets[p, q, r], jnp.int32)
        return carry

    lax.fori_loop(0, ROWS, one, 0)
    count = PIECES * QCOLS * ROWS
    down = lax.broadcasted_iota(jnp.int32, (count, count), 0)
    along = lax.broadcasted_iota(jnp.int32, (count, count), 1)
    per_piece = QCOLS * ROWS
    own = own_rows[...]
    own_along = own.T
    earlier = (own == own_along) & (down < along) & ((down < per_piece) == (along < per_piece))
    rank = jnp.sum(earlier.astype(jnp.int32), axis=0, keepdims=True)
    across = own_along[0:1, :]

    def turned(owner):
        return lax.rem(owner // COLS - z + NZ + 2, NZ)

    spin = turned(across)
    half, pos = 1 - spin // 4, lax.rem(spin, 4)
    piece = along[0:1, :] // per_piece
    slot = ((half * COLS + lax.rem(across, COLS)) * 4 + pos) * 4 + piece * 2 + rank
    for h in range(2):
        select[h] = (down + h * count == slot).astype(jnp.bfloat16)
    mark = lax.rem(turned(own), 4) * PER_TILE + off_rows[...]
    extra[...] = (mark == along).astype(jnp.bfloat16)


def compute(ext, coeffs, observed, tables, clipped, rows, scratch):
    tall, wide, bands, seams = tables
    smooth, back, model = scratch
    for p in range(PIECES):
        for m in range(MODES):
            smooth[m, p * HEIGHT:(p + 1) * HEIGHT, :] = jnp.dot(
                tall[m * HEIGHT:(m + 1) * HEIGHT, :], ext[p], preferred_element_type=jnp.float32
            ).astype(jnp.bfloat16)
    model[...] = -observed[...]

    def forward(m, carry):
        parts = convolve(smooth[m], bands[m], seams[m], False)
        for q in range(QCOLS):
            cols = slice(q * PW, (q + 1) * PW)
            for p in range(PIECES):
                model[p, :, cols] += (
                    coeffs[p, m, :, cols].astype(jnp.float32) * parts[q][p * HEIGHT:(p + 1) * HEIGHT]
                )
        return carry

    lax.fori_loop(0, MODES, forward, 0)
    clipped[...] = jnp.clip(model[...], -DELTA, DELTA)

    def adjoint(m, carry):
        weighted = jnp.concatenate(
            [
                (coeffs[p, m].astype(jnp.float32) * clipped[p]).astype(jnp.bfloat16)
                for p in range(PIECES)
            ],
            axis=0,
        )
        parts = convolve(weighted, bands[m], seams[m], True)
        start = pl.multiple_of(m * HEIGHT, HEIGHT)
        for q in range(QCOLS):
            cols = slice(q * PW, (q + 1) * PW)
            for p in range(PIECES):
                back[p, pl.ds(start, HEIGHT), cols] = parts[q][p * HEIGHT:(p + 1) * HEIGHT].astype(
                    jnp.bfloat16
                )
        return carry

    lax.fori_loop(0, MODES, adjoint, 0)
    turned = jnp.concatenate([wide[m] for m in range(MODES)], axis=1)
    for p in range(PIECES):
        rows[p] = jnp.dot(turned, back[p], preferred_element_type=jnp.float32)


def kernel(owners, offsets, sky, coeffs_far, observed_far, vert, horiz, sky_out, clipped, *scratch):
    (
        coeffs, observed, base, tall, wide, bands, seams, own_rows, off_rows, select, extra,
        table, rim_out, rim_in, ext, smooth, back, model, rows, sky_mid, *scratch
    ) = scratch
    load, fetch_sems, reduce_refs, reduce_sems = scratch[0], scratch[1:9], scratch[9:16], scratch[16:]
    loads = [
        pltpu.make_async_copy(coeffs_far, coeffs, load.at[0]),
        pltpu.make_async_copy(observed_far, observed, load.at[1]),
    ]
    all_here = greet()
    for copy in loads:
        copy.start()
    own_tile(sky, table)
    build_tall(vert, base, tall)
    all_here()

    def early():
        build_wide(vert, base, wide)

    def late():
        build_bands(horiz, base, bands, seams)
        build_slots(owners, offsets, own_rows, off_rows, select, extra)

    def nothing():
        pass

    for step in range(STEPS):
        first = step == 0
        sems = [ref.at[step] for ref in fetch_sems]
        spread_tiles(table, sems[:6], early if first else nothing, late if first else nothing)
        fetch_image(owners, offsets, table, ext, rim_out, rim_in, *sems[6:])
        if first:
            for copy in loads:
                copy.wait()
        compute(ext, coeffs, observed, (tall, wide, bands, seams), clipped, rows, (smooth, back, model))
        sems = [ref.at[step] for ref in reduce_sems]
        before, after = (sky, sky_mid) if first else (sky_mid, sky_out)
        reduce_patches(rows, select, extra, before, after, (reduce_refs, sems))
        if first:
            own_tile(sky_mid, table)


def per_device(sky_map, coeffs, observed, vert_taps, horiz_taps, owner_ids, offset):
    sky = sky_map.reshape(PER_TILE * PH, PW)
    bf16, f32, i32 = jnp.bfloat16, jnp.float32, jnp.int32
    side = BREADTH // 2
    count = PIECES * QCOLS * ROWS
    dma = pltpu.SemaphoreType.DMA
    scratch = [
        pltpu.VMEM(coeffs.shape, bf16),
        pltpu.VMEM(observed.shape, f32),
        pltpu.VMEM((MODES, side), f32),
        pltpu.VMEM((MODES * HEIGHT, EXT), bf16),
        pltpu.VMEM((MODES, EXT, HEIGHT), bf16),
        pltpu.VMEM((MODES, side, side), bf16),
        pltpu.VMEM((MODES, side, side), bf16),
        pltpu.VMEM((count, PW), i32),
        pltpu.VMEM((count, PW), i32),
        pltpu.VMEM((2, count, count), bf16),
        pltpu.VMEM((count, PW), bf16),
        pltpu.VMEM((COLS * NZ * PER_TILE, PH, PW), bf16),
        pltpu.VMEM((2, PIECES, HALO, BREADTH), bf16),
        pltpu.VMEM((2, PIECES, HALO, BREADTH), bf16),
        pltpu.VMEM((PIECES, EXT, BREADTH), bf16),
        pltpu.VMEM((MODES, PIECES * HEIGHT, BREADTH), bf16),
        pltpu.VMEM((PIECES, MODES * HEIGHT, BREADTH), bf16),
        pltpu.VMEM((PIECES, HEIGHT, BREADTH), f32),
        pltpu.VMEM((PIECES, EXT, BREADTH), f32),
        pltpu.VMEM((PER_TILE * PH, PW), f32),
        dma((2,)),
        dma((STEPS, NZ)),
        dma((STEPS, NZ)),
        dma((STEPS, NZ, NX)),
        dma((STEPS, NZ, NX)),
        dma((STEPS, NZ, NX)),
        dma((STEPS, NZ, NX)),
        dma((STEPS, 2)),
        dma((STEPS, 2)),
        pltpu.VMEM((2, PIECES, HALO, BREADTH), f32),
        pltpu.VMEM((PIECES * QCOLS * HEIGHT, PW), f32),
        pltpu.VMEM((count, WIDE), bf16),
        pltpu.VMEM((2, COLS, HALO, WIDE), bf16),
        pltpu.VMEM((2, COLS, HALO, WIDE), bf16),
        pltpu.VMEM((NZ, PER_TILE, WIDE), bf16),
        pltpu.VMEM((NZ, PER_TILE, WIDE), bf16),
        dma((STEPS, 2)),
        dma((STEPS, 2)),
        dma((STEPS, 2, NX, NC)),
        dma((STEPS, 2, NX, NC)),
        dma((STEPS, NZ)),
        dma((STEPS, NZ)),
    ]
    smem, vmem, far = pltpu.SMEM, pltpu.VMEM, pl.ANY
    sky_new, clipped = pl.pallas_call(
        kernel,
        out_shape=(
            jax.ShapeDtypeStruct(sky.shape, f32),
            jax.ShapeDtypeStruct(observed.shape, f32),
        ),
        in_specs=[pl.BlockSpec(memory_space=m) for m in (smem, smem, vmem, far, far, vmem, vmem)],
        out_specs=(pl.BlockSpec(memory_space=vmem), pl.BlockSpec(memory_space=vmem)),
        scratch_shapes=scratch,
        compiler_params=pltpu.CompilerParams(
            vmem_limit_bytes=VMEM_LIMIT, collective_id=0, has_side_effects=True
        ),
    )(owner_ids.transpose(0, 2, 3, 1), offset.transpose(0, 2, 1), sky, coeffs, observed, vert_taps, horiz_taps)
    return sky_new.reshape(sky_map.shape), clipped


def solution(mesh):
    return jax.shard_map(
        per_device,
        mesh=mesh,
        in_specs=(
            P(("exp", "sub"), None, None, None),
            P("exp", None, "sub", None),
            P("exp", "sub", None),
            P(),
            P(),
            P("exp", "sub", None, None),
            P("exp", "sub", None),
        ),
        out_specs=(P(("exp", "sub"), None, None, None), P("exp", "sub", None)),
        check_vma=False,
    )
```

```python
import jax
import jax.numpy as jnp
from jax import lax
from jax.experimental import pallas as pl
from jax.experimental.pallas import tpu as pltpu
from jax.sharding import PartitionSpec as P

STEPS = 2
ETA = 0.5
DELTA = 1.0

NZ, NX, NC = 8, 4, 2
COLS = NX * NC
MODES = 12
TAPS = 21
MARGIN = 10
PIECES = 2
HEIGHT = 128
BREADTH = 512
HALO = 16
EXT = HEIGHT + 2 * HALO
PER_TILE = 8
PH = 8
PW = 128
ROWS = HEIGHT // PH
QCOLS = BREADTH // PW
SIZE = PH * PW
NEAR_ORDER = (0, 1, 7, 2, 6, 3, 5, 4)
FAR_ORDER = (4, 3, 5, 2, 6, 1, 7)
RELAYED = (0, 1, 7, 2, 6)
PEERS = ((2, 0), (2, 1), (1, 0), (1, 1), (3, 0), (3, 1), (0, 1))
VMEM_LIMIT = 60 * 1024 * 1024


def place():
    e = lax.axis_index("exp")
    y = lax.axis_index("sub")
    return e // COLS, lax.rem(e // NC, NX), lax.rem(e, NC), y


def at_exp(z, x, c):
    return {"exp": (z * NX + x) * NC + c}


def remote(src, dst, send_sem, recv_sem, device):
    return pltpu.make_async_remote_copy(
        src_ref=src, dst_ref=dst, send_sem=send_sem, recv_sem=recv_sem,
        device_id=device, device_id_type=pl.DeviceIdType.MESH,
    )


def greet():
    z, x, c, y = place()
    barrier = pltpu.get_barrier_semaphore()
    many = 0
    for dz in range(1, NZ):
        pl.semaphore_signal(barrier, inc=1, device_id=at_exp(lax.rem(z + dz, NZ), x, c))
        many += 1
    for dx in range(NX):
        for dc in range(NC):
            if dx + dc > 0:
                pl.semaphore_signal(
                    barrier, inc=1, device_id=at_exp(z, lax.rem(x + dx, NX), lax.rem(c + dc, NC))
                )
                many += 1
    bands = lax.axis_size("sub")

    @pl.when(y > 0)
    def _():
        pl.semaphore_signal(barrier, inc=1, device_id={"sub": y - 1})

    @pl.when(y < bands - 1)
    def _():
        pl.semaphore_signal(barrier, inc=1, device_id={"sub": y + 1})

    return lambda: pl.semaphore_wait(
        barrier, many + jnp.minimum(y, 1) + jnp.minimum(bands - 1 - y, 1)
    )


def spread_tiles(table, sems, early, late):
    (zs, zr, xs, xr, cs, cr) = sems
    z, x, c, _ = place()
    col = x * NC + c

    def tile(col_at, z_at):
        return table.at[pl.ds((col_at * NZ + z_at) * PER_TILE, PER_TILE)]

    def along_z(dz, back):
        z_from = lax.rem(z - dz + NZ, NZ) if back else z
        block = tile(col, z_from)
        return remote(block, block, zs.at[dz], zr.at[dz], at_exp(lax.rem(z + dz, NZ), x, c))

    def along_x(dz, dx, back):
        x_from = lax.rem(x - dx + NX, NX) if back else x
        block = tile(x_from * NC + c, lax.rem(z - dz + NZ, NZ))
        return remote(block, block, xs.at[dz, dx], xr.at[dz, dx], at_exp(z, lax.rem(x + dx, NX), c))

    def to_twin(dz, dx, back):
        c_from = 1 - c if back else c
        block = tile(lax.rem(x - dx + NX, NX) * NC + c_from, lax.rem(z - dz + NZ, NZ))
        return remote(block, block, cs.at[dz, dx], cr.at[dz, dx], at_exp(z, x, 1 - c))

    def pass_on(dz, step):
        block = tile(lax.rem(x - step + NX, NX) * NC + c, lax.rem(z - dz + NZ, NZ))
        return remote(
            block, block, xs.at[dz, 2], xr.at[dz, 2], at_exp(z, lax.rem(x + step, NX), c)
        )

    for dz in FAR_ORDER:
        along_z(dz, False).start()
    early()
    for dz in NEAR_ORDER:
        if dz > 0:
            along_z(dz, True).wait_recv()
        for dx in (1, 3) if dz in RELAYED else (2, 1, 3):
            along_x(dz, dx, False).start()
        to_twin(dz, 0, False).start()
    late()
    for place_at in range(NZ + 2):
        if place_at < NZ:
            dz = NEAR_ORDER[place_at]
            for dx in (1, 3):
                along_x(dz, dx, True).wait_recv()
                if dz in RELAYED and dx == (1 if dz % 2 == 0 else NX - 1):
                    pass_on(dz, dx).start()
                to_twin(dz, dx, False).start()
        if place_at >= 2:
            dz = NEAR_ORDER[place_at - 2]
            along_x(dz, 2, True).wait_recv()
            to_twin(dz, 2, False).start()
    for dz in NEAR_ORDER:
        for dx in range(NX):
            to_twin(dz, dx, True).wait_recv()
    for dz in range(NZ):
        if dz > 0:
            along_z(dz, False).wait_send()
        for dx in range(NX):
            if dx > 0:
                along_x(dz, dx, False).wait_send()
            to_twin(dz, dx, False).wait_send()


def gather_rows(owners, offsets, table, ext, pair):
    for p in range(PIECES):
        for q in range(QCOLS):
            both = []
            for half in range(2):
                r = pair * 2 + half
                owner = owners[p, q, 0, r]
                tile = lax.rem(owner, COLS) * NZ + owner // COLS
                both.append(table[tile * PER_TILE + offsets[p, q, r]].astype(jnp.float32))
            block = jnp.concatenate(both, axis=0).astype(jnp.bfloat16)
            if isinstance(pair, int):
                start = HALO + pair * 2 * PH
            else:
                start = pl.multiple_of(HALO + pair * 2 * PH, 2 * PH)
            ext[p, pl.ds(start, 2 * PH), q * PW:(q + 1) * PW] = block


def fetch_image(owners, offsets, table, ext, rim_out, rim_in, hs, hr):
    _, _, _, y = place()
    bands = lax.axis_size("sub")
    pairs = ROWS // 2
    gather_rows(owners, offsets, table, ext, 0)
    gather_rows(owners, offsets, table, ext, pairs - 1)
    rim_out[0] = ext[:, HALO:2 * HALO, :]
    rim_out[1] = ext[:, HEIGHT:HEIGHT + HALO, :]
    up = remote(rim_out.at[0], rim_in.at[1], hs.at[0], hr.at[1], {"sub": y - 1})
    down = remote(rim_out.at[1], rim_in.at[0], hs.at[1], hr.at[0], {"sub": y + 1})

    @pl.when(y > 0)
    def _():
        up.start()

    @pl.when(y < bands - 1)
    def _():
        down.start()

    def more(pair, carry):
        gather_rows(owners, offsets, table, ext, pair)
        return carry

    lax.fori_loop(1, pairs - 1, more, 0)
    none = jnp.zeros((PIECES, HALO, BREADTH), jnp.bfloat16)

    @pl.when(y > 0)
    def _():
        down.wait_recv()
        ext[:, 0:HALO, :] = rim_in[0]

    @pl.when(y == 0)
    def _():
        ext[:, 0:HALO, :] = none

    @pl.when(y < bands - 1)
    def _():
        up.wait_recv()
        ext[:, HALO + HEIGHT:EXT, :] = rim_in[1]

    @pl.when(y == bands - 1)
    def _():
        ext[:, HALO + HEIGHT:EXT, :] = none

    @pl.when(y > 0)
    def _():
        up.wait_send()

    @pl.when(y < bands - 1)
    def _():
        down.wait_send()


def across(outgoing, incoming, send_sem, recv_sem, dx, dc, back):
    z, x, c, _ = place()
    x_to, c_to = lax.rem(x + dx, NX), lax.rem(c + dc, NC)
    x_from, c_from = (lax.rem(x - dx + NX, NX), c_to) if back else (x, c)
    return remote(
        outgoing.at[x_to * NC + c_to], incoming.at[x_from * NC + c_from],
        send_sem.at[dx, dc], recv_sem.at[dx, dc], at_exp(z, x_to, c_to),
    )


def along_line(outgoing, incoming, send_sem, recv_sem, rel):
    z, x, c, _ = place()
    return remote(
        outgoing.at[rel], incoming.at[rel], send_sem.at[rel], recv_sem.at[rel],
        at_exp(lax.rem(z + rel, NZ), x, c),
    )


def send_marks(select, extra, marks_out, marks_in, send_sem, recv_sem):
    z, x, c, _ = place()
    col = x * NC + c
    for half in range(2):
        picked = jnp.dot(select[half], extra[...], preferred_element_type=jnp.float32)
        marks_out[:, half * HALO:(half + 1) * HALO, :] = picked.astype(jnp.bfloat16).reshape(
            COLS, HALO, PW
        )
    for dx, dc in PEERS:
        across(marks_out, marks_in, send_sem, recv_sem, dx, dc, False).start()
    marks_in[col] = marks_out[col]


def take_marks(marks_out, marks_in, marks, count_out, count_in, sems):
    send_sem, recv_sem, line_send, line_recv = sems
    for dx, dc in PEERS:
        across(marks_out, marks_in, send_sem, recv_sem, dx, dc, True).wait_recv()
    for half in range(2):
        arrived = marks_in[:, half * HALO:(half + 1) * HALO, :].reshape(COLS * HALO, PW)
        turned = arrived.astype(jnp.float32).T[0:4 * PER_TILE].astype(jnp.bfloat16)
        marks[half] = turned
        many = jnp.dot(
            turned, jnp.ones((COLS * HALO, PW), jnp.bfloat16), preferred_element_type=jnp.float32
        )
        for pos in range(4):
            rel = (pos + 4 * (1 - half) + NZ - 2) % NZ
            count_out[rel] = many[pos * PER_TILE:(pos + 1) * PER_TILE]
    for rel in FAR_ORDER:
        along_line(count_out, count_in, line_send, line_recv, rel).start()
    for dx, dc in PEERS:
        across(marks_out, marks_in, send_sem, recv_sem, dx, dc, False).wait_send()


def take_counts(count_out, count_in, scale, sems):
    _, _, line_send, line_recv = sems
    total = count_out[0]
    for rel in NEAR_ORDER[1:]:
        along_line(count_out, count_in, line_send, line_recv, rel).wait_recv()
        total = total + count_in[rel]
    scale[...] = ETA / jnp.maximum(total, 1.0)
    for rel in FAR_ORDER:
        along_line(count_out, count_in, line_send, line_recv, rel).wait_send()


def send_rims(rows, rim_out, rim_in, hs, hr):
    _, _, _, y = place()
    bands = lax.axis_size("sub")
    rim_out[0] = rows[:, 0:HALO, :].astype(jnp.bfloat16)
    rim_out[1] = rows[:, HALO + HEIGHT:EXT, :].astype(jnp.bfloat16)
    up = remote(rim_out.at[0], rim_in.at[1], hs.at[0], hr.at[1], {"sub": y - 1})
    down = remote(rim_out.at[1], rim_in.at[0], hs.at[1], hr.at[0], {"sub": y + 1})

    @pl.when(y > 0)
    def _():
        up.start()

    @pl.when(y < bands - 1)
    def _():
        down.start()

    return up, down


def reduce_patches(rows, rims, select, marks, get_scale, sky, sky_new, scratch):
    (rim_in, grad, stacked, outgoing, incoming, line_out, line_in), sems = scratch
    axs, axr, bzs, bzr = sems
    up, down = rims
    _, x, c, y = place()
    bands = lax.axis_size("sub")
    col = x * NC + c
    strips = [(p, q, (p * QCOLS + q) * HEIGHT) for p in range(PIECES) for q in range(QCOLS)]
    for p, q, at in strips:
        grad[at:at + HEIGHT, :] = rows[p, HALO:HALO + HEIGHT, q * PW:(q + 1) * PW]

    @pl.when(y > 0)
    def _():
        down.wait_recv()
        for p, q, at in strips:
            grad[at:at + HALO, :] += rim_in[0, p, :, q * PW:(q + 1) * PW].astype(jnp.float32)

    @pl.when(y < bands - 1)
    def _():
        up.wait_recv()
        for p, q, at in strips:
            end = at + HEIGHT
            grad[end - HALO:end, :] += rim_in[1, p, :, q * PW:(q + 1) * PW].astype(jnp.float32)

    for p, q, at in strips:
        for i in range(PH):
            lines = grad[pl.ds(at + i, ROWS, stride=PH), :]
            stacked[at // PH:at // PH + ROWS, i * PW:(i + 1) * PW] = lines.astype(jnp.bfloat16)

    def exchange(half, dx, dc, back):
        return across(
            outgoing.at[half], incoming.at[half], axs.at[half], axr.at[half], dx, dc, back
        )

    for half in range(2):
        picked = jnp.dot(
            select[half], stacked[...], preferred_element_type=jnp.float32
        ).astype(jnp.bfloat16)
        outgoing[half] = picked.reshape(COLS, HALO, SIZE)
        for dx, dc in PEERS:
            exchange(half, dx, dc, False).start()
        incoming[half, col] = outgoing[half, col]
    for half in range(2):
        for dx, dc in PEERS[::-1]:
            exchange(half, dx, dc, True).wait_recv()
        arrived = incoming[half].reshape(COLS * HALO, SIZE)
        totals = jnp.dot(marks[half], arrived, preferred_element_type=jnp.float32)
        for pos in (2, 1, 3, 0) if half == 0 else (0, 3, 1, 2):
            rel = (pos + 4 * (1 - half) + NZ - 2) % NZ
            line_out[rel] = totals[pos * PER_TILE:(pos + 1) * PER_TILE].astype(jnp.bfloat16)
            if rel > 0:
                along_line(line_out, line_in, bzs, bzr, rel).start()
    scale = get_scale()
    total = line_out[0].astype(jnp.float32)
    for rel in NEAR_ORDER[1:]:
        along_line(line_out, line_in, bzs, bzr, rel).wait_recv()
        total = total + line_in[rel].astype(jnp.float32)
    for i in range(PH):
        old = sky[pl.ds(i, PER_TILE, stride=PH), :]
        sky_new[pl.ds(i, PER_TILE, stride=PH), :] = old - scale * total[:, i * PW:(i + 1) * PW]
    for half in range(2):
        for dx, dc in PEERS:
            exchange(half, dx, dc, False).wait_send()
    for rel in range(1, NZ):
        along_line(line_out, line_in, bzs, bzr, rel).wait_send()

    @pl.when(y > 0)
    def _():
        up.wait_send()

    @pl.when(y < bands - 1)
    def _():
        down.wait_send()


def own_tile(sky, table):
    z, x, c, _ = place()
    start = ((x * NC + c) * NZ + z) * PER_TILE
    for k in range(PER_TILE):
        table[start + k] = sky[k * PH:(k + 1) * PH, :].astype(jnp.bfloat16)


def convolve(block, centre, edge, transposed):
    dims = (((1,), (1 if transposed else 0,)), ((), ()))
    half = BREADTH // 2

    def product(a, b):
        return lax.dot_general(a, b, dims, preferred_element_type=jnp.float32)

    left = product(block[:, :half], centre)
    right = product(block[:, half:], centre)
    seam = product(block[:, PW:PW + half], edge)
    return [left[:, :PW], left[:, PW:] + seam[:, :PW], right[:, :PW] + seam[:, PW:], right[:, PW:]]


def diagonals(row, height):
    return pltpu.roll(jnp.broadcast_to(row, (height, row.shape[1])), 0, 1, stride=1, stride_axis=0)


def lag_rows(taps, lag):
    tap = lax.broadcasted_iota(jnp.int32, (TAPS, 2 * PW), 0)
    lane = lax.broadcasted_iota(jnp.int32, (TAPS, 2 * PW), 1)
    chosen = (tap == lag(lane)).astype(jnp.bfloat16)
    return jnp.dot(taps[...], chosen, preferred_element_type=jnp.float32)


def wrapped(lane):
    return jnp.where(lane < PW, lane, lane - 2 * PW)


def build_tall(vert, base, tall):
    base[...] = lag_rows(vert, lambda lane: lane - HALO + MARGIN)

    def one(m, carry):
        rows = diagonals(base[pl.ds(m, 1), :], HEIGHT)
        tall[pl.ds(pl.multiple_of(m * HEIGHT, HEIGHT), HEIGHT), :] = rows[:, :EXT].astype(jnp.bfloat16)
        return carry

    lax.fori_loop(0, MODES, one, 0)


def build_wide(vert, base, wide):
    base[...] = lag_rows(vert, lambda lane: MARGIN - HALO - wrapped(lane))

    def one(m, carry):
        rows = diagonals(base[pl.ds(m, 1), :], EXT)
        wide[m] = rows[:, :HEIGHT].astype(jnp.bfloat16)
        return carry

    lax.fori_loop(0, MODES, one, 0)


def build_bands(horiz, base, bands, seams):
    base[...] = lag_rows(horiz, lambda lane: MARGIN - wrapped(lane))
    side = BREADTH // 2
    w = lax.broadcasted_iota(jnp.int32, (side, side), 0)
    c = lax.broadcasted_iota(jnp.int32, (side, side), 1)
    near = jnp.abs(w - c) <= MARGIN
    across = near & ((w < PW) != (c < PW))

    def one(m, carry):
        rows = diagonals(base[pl.ds(m, 1), :], side)
        bands[m] = jnp.where(near, rows, 0.0).astype(jnp.bfloat16)
        seams[m] = jnp.where(across, rows, 0.0).astype(jnp.bfloat16)
        return carry

    lax.fori_loop(0, MODES, one, 0)


def build_slots(owners, offsets, own_rows, off_rows, select, extra):
    z, _, _, _ = place()

    def one(r, carry):
        for p in range(PIECES):
            for q in range(QCOLS):
                n = (p * QCOLS + q) * ROWS + r
                own_rows[pl.ds(n, 1), :] = jnp.full((1, PW), owners[p, q, 0, r], jnp.int32)
                off_rows[pl.ds(n, 1), :] = jnp.full((1, PW), offsets[p, q, r], jnp.int32)
        return carry

    lax.fori_loop(0, ROWS, one, 0)
    count = PIECES * QCOLS * ROWS
    down = lax.broadcasted_iota(jnp.int32, (count, count), 0)
    along = lax.broadcasted_iota(jnp.int32, (count, count), 1)
    per_piece = QCOLS * ROWS
    own = own_rows[...]
    own_along = own.T
    earlier = (own == own_along) & (down < along) & ((down < per_piece) == (along < per_piece))
    rank = jnp.sum(earlier.astype(jnp.int32), axis=0, keepdims=True)
    across = own_along[0:1, :]

    def turned(owner):
        return lax.rem(owner // COLS - z + NZ + 2, NZ)

    spin = turned(across)
    half, pos = 1 - spin // 4, lax.rem(spin, 4)
    piece = along[0:1, :] // per_piece
    slot = ((half * COLS + lax.rem(across, COLS)) * 4 + pos) * 4 + piece * 2 + rank
    for h in range(2):
        select[h] = (down + h * count == slot).astype(jnp.bfloat16)
    mark = lax.rem(turned(own), 4) * PER_TILE + off_rows[...]
    extra[...] = (mark == along).astype(jnp.bfloat16)


def compute(ext, coeffs, observed, tables, clipped, rows, scratch):
    tall, wide, bands, seams = tables
    smooth, back, model = scratch
    for p in range(PIECES):
        for m in range(MODES):
            smooth[m, p * HEIGHT:(p + 1) * HEIGHT, :] = jnp.dot(
                tall[m * HEIGHT:(m + 1) * HEIGHT, :], ext[p], preferred_element_type=jnp.float32
            ).astype(jnp.bfloat16)
    model[...] = -observed[...]

    def forward(m, carry):
        parts = convolve(smooth[m], bands[m], seams[m], False)
        for q in range(QCOLS):
            cols = slice(q * PW, (q + 1) * PW)
            for p in range(PIECES):
                model[p, :, cols] += (
                    coeffs[p, m, :, cols].astype(jnp.float32) * parts[q][p * HEIGHT:(p + 1) * HEIGHT]
                )
        return carry

    lax.fori_loop(0, MODES, forward, 0, unroll=MODES)
    clipped[...] = jnp.clip(model[...], -DELTA, DELTA)

    def adjoint(m, carry):
        weighted = jnp.concatenate(
            [
                (coeffs[p, m].astype(jnp.float32) * clipped[p]).astype(jnp.bfloat16)
                for p in range(PIECES)
            ],
            axis=0,
        )
        parts = convolve(weighted, bands[m], seams[m], True)
        start = pl.multiple_of(m * HEIGHT, HEIGHT)
        for q in range(QCOLS):
            cols = slice(q * PW, (q + 1) * PW)
            for p in range(PIECES):
                back[p, pl.ds(start, HEIGHT), cols] = parts[q][p * HEIGHT:(p + 1) * HEIGHT].astype(
                    jnp.bfloat16
                )
        return carry

    lax.fori_loop(0, MODES, adjoint, 0, unroll=MODES)
    turned = jnp.concatenate([wide[m] for m in range(MODES)], axis=1)
    for p in range(PIECES):
        rows[p] = jnp.dot(turned, back[p], preferred_element_type=jnp.float32)


def kernel(owners, offsets, sky, coeffs_far, observed_far, vert, horiz, sky_out, clipped, *scratch):
    (
        coeffs, observed, base, tall, wide, bands, seams, own_rows, off_rows, select, extra,
        table, rim_out, rim_in, ext, smooth, back, model, rows, sky_mid,
        marks_out, marks_in, marks, count_out, count_in, scale, adj_out, *scratch
    ) = scratch
    load, mark_sems, fetch_sems = scratch[0], scratch[1:5], scratch[5:13]
    adj_in, reduce_refs, reduce_sems = scratch[13], scratch[13:20], scratch[20:]
    loads = [
        pltpu.make_async_copy(coeffs_far, coeffs, load.at[0]),
        pltpu.make_async_copy(observed_far, observed, load.at[1]),
    ]
    all_here = greet()
    for copy in loads:
        copy.start()
    own_tile(sky, table)
    build_tall(vert, base, tall)
    all_here()

    def early():
        build_wide(vert, base, wide)

    def late():
        build_bands(horiz, base, bands, seams)
        build_slots(owners, offsets, own_rows, off_rows, select, extra)

    def nothing():
        pass

    for step in range(STEPS):
        first = step == 0
        sems = [ref.at[step] for ref in fetch_sems]
        spread_tiles(table, sems[:6], early if first else nothing, late if first else nothing)
        fetch_image(owners, offsets, table, ext, rim_out, rim_in, *sems[6:])
        if first:
            send_marks(select, extra, marks_out, marks_in, *mark_sems[:2])
            for copy in loads:
                copy.wait()
        compute(ext, coeffs, observed, (tall, wide, bands, seams), clipped, rows, (smooth, back, model))
        sems = [ref.at[step] for ref in reduce_sems]
        rims = send_rims(rows, adj_out, adj_in, *sems[:2])
        if first:
            take_marks(marks_out, marks_in, marks, count_out, count_in, mark_sems)

        def get_scale():
            if first:
                take_counts(count_out, count_in, scale, mark_sems)
            return scale[...]

        before, after = (sky, sky_mid) if first else (sky_mid, sky_out)
        reduce_patches(rows, rims, select, marks, get_scale, before, after, (reduce_refs, sems[2:]))
        if first:
            own_tile(sky_mid, table)


def copy_out(sky_far, clipped_far, sky_out, clipped_out, sky, clipped, load, store):
    pairs = ((clipped_far, clipped, clipped_out), (sky_far, sky, sky_out))
    inward = [pltpu.make_async_copy(a, b, load.at[i]) for i, (a, b, _) in enumerate(pairs)]
    outward = [pltpu.make_async_copy(b, c, store.at[i]) for i, (_, b, c) in enumerate(pairs)]
    for copy in inward:
        copy.start()
    for came, goes in zip(inward, outward):
        came.wait()
        goes.start()
    for copy in outward:
        copy.wait()


def per_device(sky_map, coeffs, observed, vert_taps, horiz_taps, owner_ids, offset):
    sky = sky_map.reshape(PER_TILE * PH, PW)
    bf16, f32, i32 = jnp.bfloat16, jnp.float32, jnp.int32
    side = BREADTH // 2
    count = PIECES * QCOLS * ROWS
    dma = pltpu.SemaphoreType.DMA
    scratch = [
        pltpu.VMEM(coeffs.shape, bf16),
        pltpu.VMEM(observed.shape, f32),
        pltpu.VMEM((MODES, side), f32),
        pltpu.VMEM((MODES * HEIGHT, EXT), bf16),
        pltpu.VMEM((MODES, EXT, HEIGHT), bf16),
        pltpu.VMEM((MODES, side, side), bf16),
        pltpu.VMEM((MODES, side, side), bf16),
        pltpu.VMEM((count, PW), i32),
        pltpu.VMEM((count, PW), i32),
        pltpu.VMEM((2, count, count), bf16),
        pltpu.VMEM((count, PW), bf16),
        pltpu.VMEM((COLS * NZ * PER_TILE, PH, PW), bf16),
        pltpu.VMEM((2, PIECES, HALO, BREADTH), bf16),
        pltpu.VMEM((2, PIECES, HALO, BREADTH), bf16),
        pltpu.VMEM((PIECES, EXT, BREADTH), bf16),
        pltpu.VMEM((MODES, PIECES * HEIGHT, BREADTH), bf16),
        pltpu.VMEM((PIECES, MODES * HEIGHT, BREADTH), bf16),
        pltpu.VMEM((PIECES, HEIGHT, BREADTH), f32),
        pltpu.VMEM((PIECES, EXT, BREADTH), f32),
        pltpu.VMEM((PER_TILE * PH, PW), f32),
        pltpu.VMEM((COLS, 2 * HALO, PW), bf16),
        pltpu.VMEM((COLS, 2 * HALO, PW), bf16),
        pltpu.VMEM((2, 4 * PER_TILE, COLS * HALO), bf16),
        pltpu.VMEM((NZ, PER_TILE, PW), f32),
        pltpu.VMEM((NZ, PER_TILE, PW), f32),
        pltpu.VMEM((PER_TILE, PW), f32),
        pltpu.VMEM((2, PIECES, HALO, BREADTH), bf16),
        dma((2,)),
        dma((NX, NC)),
        dma((NX, NC)),
        dma((NZ,)),
        dma((NZ,)),
        dma((STEPS, NZ)),
        dma((STEPS, NZ)),
        dma((STEPS, NZ, NX)),
        dma((STEPS, NZ, NX)),
        dma((STEPS, NZ, NX)),
        dma((STEPS, NZ, NX)),
        dma((STEPS, 2)),
        dma((STEPS, 2)),
        pltpu.VMEM((2, PIECES, HALO, BREADTH), bf16),
        pltpu.VMEM((PIECES * QCOLS * HEIGHT, PW), f32),
        pltpu.VMEM((count, SIZE), bf16),
        pltpu.VMEM((2, COLS, HALO, SIZE), bf16),
        pltpu.VMEM((2, COLS, HALO, SIZE), bf16),
        pltpu.VMEM((NZ, PER_TILE, SIZE), bf16),
        pltpu.VMEM((NZ, PER_TILE, SIZE), bf16),
        dma((STEPS, 2)),
        dma((STEPS, 2)),
        dma((STEPS, 2, NX, NC)),
        dma((STEPS, 2, NX, NC)),
        dma((STEPS, NZ)),
        dma((STEPS, NZ)),
    ]
    smem, vmem, far = pltpu.SMEM, pltpu.VMEM, pl.ANY
    sky_new, clipped = pl.pallas_call(
        kernel,
        out_shape=(
            jax.ShapeDtypeStruct(sky.shape, f32),
            jax.ShapeDtypeStruct(observed.shape, f32),
        ),
        in_specs=[pl.BlockSpec(memory_space=m) for m in (smem, smem, vmem, far, far, vmem, vmem)],
        out_specs=(pl.BlockSpec(memory_space=vmem), pl.BlockSpec(memory_space=vmem)),
        scratch_shapes=scratch,
        compiler_params=pltpu.CompilerParams(
            vmem_limit_bytes=VMEM_LIMIT, collective_id=0, has_side_effects=True
        ),
    )(owner_ids.transpose(0, 2, 3, 1), offset.transpose(0, 2, 1), sky, coeffs, observed, vert_taps, horiz_taps)
    sky_new, clipped = pl.pallas_call(
        copy_out,
        out_shape=(
            jax.ShapeDtypeStruct(sky.shape, f32),
            jax.ShapeDtypeStruct(observed.shape, f32),
        ),
        in_specs=[pl.BlockSpec(memory_space=far)] * 2,
        out_specs=(pl.BlockSpec(memory_space=far), pl.BlockSpec(memory_space=far)),
        scratch_shapes=[pltpu.VMEM(sky.shape, f32), pltpu.VMEM(observed.shape, f32), dma((2,)), dma((2,))],
        compiler_params=pltpu.CompilerParams(vmem_limit_bytes=VMEM_LIMIT),
    )(sky_new, clipped)
    return sky_new.reshape(sky_map.shape), clipped


def solution(mesh):
    return jax.shard_map(
        per_device,
        mesh=mesh,
        in_specs=(
            P(("exp", "sub"), None, None, None),
            P("exp", None, "sub", None),
            P("exp", "sub", None),
            P(),
            P(),
            P("exp", "sub", None, None),
            P("exp", "sub", None),
        ),
        out_specs=(P(("exp", "sub"), None, None, None), P("exp", "sub", None)),
        check_vma=False,
    )
```

```python
import jax
import jax.numpy as jnp
from jax import lax
from jax.experimental import pallas as pl
from jax.experimental.pallas import tpu as pltpu
from jax.sharding import PartitionSpec as P

STEPS = 2
ETA = 0.5
DELTA = 1.0

NZ, NX, NC = 8, 4, 2
COLS = NX * NC
MODES = 12
TAPS = 21
MARGIN = 10
PIECES = 2
HEIGHT = 128
BREADTH = 512
HALO = 16
EXT = HEIGHT + 2 * HALO
PER_TILE = 8
PH = 8
PW = 128
ROWS = HEIGHT // PH
QCOLS = BREADTH // PW
SIZE = PH * PW
NEAR_ORDER = (0, 1, 7, 2, 6, 3, 5, 4)
FAR_ORDER = (4, 3, 5, 2, 6, 1, 7)
CHUNKS = ((4, 3), (5, 2), (6, 1), (7, 0))
N_CHUNKS = len(CHUNKS)
CHUNK_ROWS = 4 * len(CHUNKS[0])
PEERS = ((2, 0), (2, 1), (1, 0), (1, 1), (3, 0), (3, 1), (0, 1))
VMEM_LIMIT = 60 * 1024 * 1024


def place():
    e = lax.axis_index("exp")
    y = lax.axis_index("sub")
    return e // COLS, lax.rem(e // NC, NX), lax.rem(e, NC), y


def at_exp(z, x, c):
    return {"exp": (z * NX + x) * NC + c}


def remote(src, dst, send_sem, recv_sem, device):
    return pltpu.make_async_remote_copy(
        src_ref=src, dst_ref=dst, send_sem=send_sem, recv_sem=recv_sem,
        device_id=device, device_id_type=pl.DeviceIdType.MESH,
    )


def greet():
    z, x, c, y = place()
    barrier = pltpu.get_barrier_semaphore()
    many = 0
    for dz in range(1, NZ):
        pl.semaphore_signal(barrier, inc=1, device_id=at_exp(lax.rem(z + dz, NZ), x, c))
        many += 1
    for dx in range(NX):
        for dc in range(NC):
            if dx + dc > 0:
                pl.semaphore_signal(
                    barrier, inc=1, device_id=at_exp(z, lax.rem(x + dx, NX), lax.rem(c + dc, NC))
                )
                many += 1
    bands = lax.axis_size("sub")

    @pl.when(y > 0)
    def _():
        pl.semaphore_signal(barrier, inc=1, device_id={"sub": y - 1})

    @pl.when(y < bands - 1)
    def _():
        pl.semaphore_signal(barrier, inc=1, device_id={"sub": y + 1})

    return lambda: pl.semaphore_wait(
        barrier, many + jnp.minimum(y, 1) + jnp.minimum(bands - 1 - y, 1)
    )


def spread_tiles(table, sems, early, late):
    (zs, zr, xs, xr, cs, cr) = sems
    z, x, c, _ = place()
    col = x * NC + c

    def tile(col_at, z_at):
        return table.at[pl.ds((col_at * NZ + z_at) * PER_TILE, PER_TILE)]

    def along_z(dz, back):
        z_from = lax.rem(z - dz + NZ, NZ) if back else z
        block = tile(col, z_from)
        return remote(block, block, zs.at[dz], zr.at[dz], at_exp(lax.rem(z + dz, NZ), x, c))

    def along_x(dz, dx, back):
        x_from = lax.rem(x - dx + NX, NX) if back else x
        block = tile(x_from * NC + c, lax.rem(z - dz + NZ, NZ))
        return remote(block, block, xs.at[dz, dx], xr.at[dz, dx], at_exp(z, lax.rem(x + dx, NX), c))

    def to_twin(dz, dx, back):
        c_from = 1 - c if back else c
        block = tile(lax.rem(x - dx + NX, NX) * NC + c_from, lax.rem(z - dz + NZ, NZ))
        return remote(block, block, cs.at[dz, dx], cr.at[dz, dx], at_exp(z, x, 1 - c))

    for dz in FAR_ORDER:
        along_z(dz, False).start()
    early()
    for dz in NEAR_ORDER:
        if dz > 0:
            along_z(dz, True).wait_recv()
        for dx in (2, 1, 3):
            along_x(dz, dx, False).start()
        to_twin(dz, 0, False).start()
    late()
    for dz in NEAR_ORDER:
        for dx in (1, 3, 2):
            along_x(dz, dx, True).wait_recv()
            to_twin(dz, dx, False).start()
    for dz in NEAR_ORDER:
        for dx in range(NX):
            to_twin(dz, dx, True).wait_recv()
    for dz in range(NZ):
        if dz > 0:
            along_z(dz, False).wait_send()
        for dx in range(NX):
            if dx > 0:
                along_x(dz, dx, False).wait_send()
            to_twin(dz, dx, False).wait_send()


def gather_rows(owners, offsets, table, ext, pair):
    for p in range(PIECES):
        for q in range(QCOLS):
            both = []
            for half in range(2):
                r = pair * 2 + half
                owner = owners[p, q, 0, r]
                tile = lax.rem(owner, COLS) * NZ + owner // COLS
                both.append(table[tile * PER_TILE + offsets[p, q, r]].astype(jnp.float32))
            block = jnp.concatenate(both, axis=0).astype(jnp.bfloat16)
            if isinstance(pair, int):
                start = HALO + pair * 2 * PH
            else:
                start = pl.multiple_of(HALO + pair * 2 * PH, 2 * PH)
            ext[p, pl.ds(start, 2 * PH), q * PW:(q + 1) * PW] = block


def fetch_image(owners, offsets, table, ext, rim_out, rim_in, hs, hr):
    _, _, _, y = place()
    bands = lax.axis_size("sub")
    pairs = ROWS // 2
    gather_rows(owners, offsets, table, ext, 0)
    gather_rows(owners, offsets, table, ext, pairs - 1)
    rim_out[0] = ext[:, HALO:2 * HALO, :]
    rim_out[1] = ext[:, HEIGHT:HEIGHT + HALO, :]
    up = remote(rim_out.at[0], rim_in.at[1], hs.at[0], hr.at[1], {"sub": y - 1})
    down = remote(rim_out.at[1], rim_in.at[0], hs.at[1], hr.at[0], {"sub": y + 1})

    @pl.when(y > 0)
    def _():
        up.start()

    @pl.when(y < bands - 1)
    def _():
        down.start()

    def more(pair, carry):
        gather_rows(owners, offsets, table, ext, pair)
        return carry

    lax.fori_loop(1, pairs - 1, more, 0)
    none = jnp.zeros((PIECES, HALO, BREADTH), jnp.bfloat16)

    @pl.when(y > 0)
    def _():
        down.wait_recv()
        ext[:, 0:HALO, :] = rim_in[0]

    @pl.when(y == 0)
    def _():
        ext[:, 0:HALO, :] = none

    @pl.when(y < bands - 1)
    def _():
        up.wait_recv()
        ext[:, HALO + HEIGHT:EXT, :] = rim_in[1]

    @pl.when(y == bands - 1)
    def _():
        ext[:, HALO + HEIGHT:EXT, :] = none

    @pl.when(y > 0)
    def _():
        up.wait_send()

    @pl.when(y < bands - 1)
    def _():
        down.wait_send()


def across(outgoing, incoming, send_sem, recv_sem, dx, dc, back, every=False):
    z, x, c, _ = place()
    x_to, c_to = lax.rem(x + dx, NX), lax.rem(c + dc, NC)
    x_from, c_from = (lax.rem(x - dx + NX, NX), c_to) if back else (x, c)
    to_at, from_at = x_to * NC + c_to, x_from * NC + c_from
    return remote(
        outgoing.at[:, to_at] if every else outgoing.at[to_at],
        incoming.at[:, from_at] if every else incoming.at[from_at],
        send_sem.at[dx, dc], recv_sem.at[dx, dc], at_exp(z, x_to, c_to),
    )


def along_line(outgoing, incoming, send_sem, recv_sem, rel):
    z, x, c, _ = place()
    return remote(
        outgoing.at[rel], incoming.at[rel], send_sem.at[rel], recv_sem.at[rel],
        at_exp(lax.rem(z + rel, NZ), x, c),
    )


def send_marks(select, extra, marks_out, marks_in, send_sem, recv_sem):
    z, x, c, _ = place()
    col = x * NC + c
    for chunk in range(N_CHUNKS):
        picked = jnp.dot(select[chunk], extra[...], preferred_element_type=jnp.float32)
        marks_out[chunk] = picked.reshape(COLS, CHUNK_ROWS, PW).astype(jnp.bfloat16)
    for dx, dc in PEERS:
        across(marks_out, marks_in, send_sem, recv_sem, dx, dc, False, True).start()
    marks_in[:, col] = marks_out[:, col]


def take_marks(marks_out, marks_in, marks, count_out, count_in, sems):
    send_sem, recv_sem, line_send, line_recv = sems
    for dx, dc in PEERS:
        across(marks_out, marks_in, send_sem, recv_sem, dx, dc, True, True).wait_recv()
    for chunk in range(N_CHUNKS):
        arrived = marks_in[chunk].astype(jnp.float32).reshape(COLS * CHUNK_ROWS, PW)
        turned = arrived.T[0:2 * PER_TILE].astype(jnp.bfloat16)
        marks[chunk] = turned
        many = jnp.dot(
            turned, jnp.ones((COLS * CHUNK_ROWS, PW), jnp.bfloat16), preferred_element_type=jnp.float32
        )
        for pos, rel in enumerate(CHUNKS[chunk]):
            count_out[rel] = many[pos * PER_TILE:(pos + 1) * PER_TILE]
    for rel in FAR_ORDER:
        along_line(count_out, count_in, line_send, line_recv, rel).start()
    for dx, dc in PEERS:
        across(marks_out, marks_in, send_sem, recv_sem, dx, dc, False, True).wait_send()


def take_counts(count_out, count_in, scale, sems):
    _, _, line_send, line_recv = sems
    total = count_out[0]
    for rel in NEAR_ORDER[1:]:
        along_line(count_out, count_in, line_send, line_recv, rel).wait_recv()
        total = total + count_in[rel]
    scale[...] = ETA / jnp.maximum(total, 1.0)
    for rel in FAR_ORDER:
        along_line(count_out, count_in, line_send, line_recv, rel).wait_send()


def send_rims(rows, rim_out, rim_in, hs, hr):
    _, _, _, y = place()
    bands = lax.axis_size("sub")
    rim_out[0] = rows[:, 0:HALO, :].astype(jnp.bfloat16)
    rim_out[1] = rows[:, HALO + HEIGHT:EXT, :].astype(jnp.bfloat16)
    up = remote(rim_out.at[0], rim_in.at[1], hs.at[0], hr.at[1], {"sub": y - 1})
    down = remote(rim_out.at[1], rim_in.at[0], hs.at[1], hr.at[0], {"sub": y + 1})

    @pl.when(y > 0)
    def _():
        up.start()

    @pl.when(y < bands - 1)
    def _():
        down.start()

    return up, down


def reduce_patches(rows, rims, select, marks, get_scale, sky, sky_new, scratch):
    (rim_in, stacked, outgoing, incoming, line_out, line_in), sems = scratch
    axs, axr, bzs, bzr = sems
    up, down = rims
    _, x, c, y = place()
    bands = lax.axis_size("sub")
    col = x * NC + c
    strips = range(PIECES * QCOLS)

    @pl.when(y > 0)
    def _():
        down.wait_recv()
        for n in strips:
            rows[n, HALO:2 * HALO, :] += rim_in[0, n].astype(jnp.float32)

    @pl.when(y < bands - 1)
    def _():
        up.wait_recv()
        for n in strips:
            rows[n, HEIGHT:HALO + HEIGHT, :] += rim_in[1, n].astype(jnp.float32)

    for n in strips:
        for i in range(PH):
            lines = rows[n, pl.ds(HALO + i, ROWS, stride=PH), :]
            stacked[n * ROWS:(n + 1) * ROWS, i * PW:(i + 1) * PW] = lines.astype(jnp.bfloat16)

    def exchange(chunk, dx, dc, back):
        return across(
            outgoing.at[chunk], incoming.at[chunk], axs.at[chunk], axr.at[chunk], dx, dc, back
        )

    for chunk in range(N_CHUNKS):
        picked = jnp.dot(select[chunk], stacked[...], preferred_element_type=jnp.float32)
        outgoing[chunk] = picked.reshape(COLS, CHUNK_ROWS, SIZE).astype(jnp.bfloat16)
        for dx, dc in PEERS:
            exchange(chunk, dx, dc, False).start()
        incoming[chunk, col] = outgoing[chunk, col]
    for chunk in range(N_CHUNKS):
        for dx, dc in PEERS[::-1]:
            exchange(chunk, dx, dc, True).wait_recv()
        arrived = incoming[chunk].astype(jnp.float32).reshape(COLS * CHUNK_ROWS, SIZE)
        totals = jnp.dot(
            marks[chunk], arrived.astype(jnp.bfloat16), preferred_element_type=jnp.float32
        )
        for pos, rel in enumerate(CHUNKS[chunk]):
            line_out[rel] = totals[pos * PER_TILE:(pos + 1) * PER_TILE].astype(jnp.bfloat16)
            if rel > 0:
                along_line(line_out, line_in, bzs, bzr, rel).start()
    scale = get_scale()
    total = line_out[0].astype(jnp.float32)
    for rel in NEAR_ORDER[1:]:
        along_line(line_out, line_in, bzs, bzr, rel).wait_recv()
        total = total + line_in[rel].astype(jnp.float32)
    for i in range(PH):
        old = sky[pl.ds(i, PER_TILE, stride=PH), :]
        sky_new[pl.ds(i, PER_TILE, stride=PH), :] = old - scale * total[:, i * PW:(i + 1) * PW]
    for chunk in range(N_CHUNKS):
        for dx, dc in PEERS:
            exchange(chunk, dx, dc, False).wait_send()
    for rel in range(1, NZ):
        along_line(line_out, line_in, bzs, bzr, rel).wait_send()

    @pl.when(y > 0)
    def _():
        up.wait_send()

    @pl.when(y < bands - 1)
    def _():
        down.wait_send()


def own_tile(sky, table):
    z, x, c, _ = place()
    start = ((x * NC + c) * NZ + z) * PER_TILE
    for k in range(PER_TILE):
        table[start + k] = sky[k * PH:(k + 1) * PH, :].astype(jnp.bfloat16)


def convolve(block, centre, edge, transposed):
    dims = (((1,), (1 if transposed else 0,)), ((), ()))
    half = BREADTH // 2

    def product(a, b):
        return lax.dot_general(a, b, dims, preferred_element_type=jnp.float32)

    left = product(block[:, :half], centre)
    right = product(block[:, half:], centre)
    seam = product(block[:, PW:PW + half], edge)
    return [left[:, :PW], left[:, PW:] + seam[:, :PW], right[:, :PW] + seam[:, PW:], right[:, PW:]]


def diagonals(row, height):
    return pltpu.roll(jnp.broadcast_to(row, (height, row.shape[1])), 0, 1, stride=1, stride_axis=0)


def lag_rows(taps, lag):
    tap = lax.broadcasted_iota(jnp.int32, (TAPS, 2 * PW), 0)
    lane = lax.broadcasted_iota(jnp.int32, (TAPS, 2 * PW), 1)
    chosen = (tap == lag(lane)).astype(jnp.bfloat16)
    return jnp.dot(taps[...], chosen, preferred_element_type=jnp.float32)


def wrapped(lane):
    return jnp.where(lane < PW, lane, lane - 2 * PW)


def build_tall(vert, base, tall):
    base[...] = lag_rows(vert, lambda lane: lane - HALO + MARGIN)

    def one(m, carry):
        rows = diagonals(base[pl.ds(m, 1), :], HEIGHT)
        tall[pl.ds(pl.multiple_of(m * HEIGHT, HEIGHT), HEIGHT), :] = rows[:, :EXT].astype(jnp.bfloat16)
        return carry

    lax.fori_loop(0, MODES, one, 0)


def build_wide(vert, base, wide):
    base[...] = lag_rows(vert, lambda lane: MARGIN - HALO - wrapped(lane))

    def one(m, carry):
        rows = diagonals(base[pl.ds(m, 1), :], EXT)
        wide[m] = rows[:, :HEIGHT].astype(jnp.bfloat16)
        return carry

    lax.fori_loop(0, MODES, one, 0)


def build_bands(horiz, base, bands, seams):
    base[...] = lag_rows(horiz, lambda lane: MARGIN - wrapped(lane))
    side = BREADTH // 2
    w = lax.broadcasted_iota(jnp.int32, (side, side), 0)
    c = lax.broadcasted_iota(jnp.int32, (side, side), 1)
    near = jnp.abs(w - c) <= MARGIN
    across = near & ((w < PW) != (c < PW))

    def one(m, carry):
        rows = diagonals(base[pl.ds(m, 1), :], side)
        bands[m] = jnp.where(near, rows, 0.0).astype(jnp.bfloat16)
        seams[m] = jnp.where(across, rows, 0.0).astype(jnp.bfloat16)
        return carry

    lax.fori_loop(0, MODES, one, 0)


def build_slots(owners, offsets, own_rows, off_rows, select, extra):
    z, _, _, _ = place()

    def one(r, carry):
        for p in range(PIECES):
            for q in range(QCOLS):
                n = (p * QCOLS + q) * ROWS + r
                own_rows[pl.ds(n, 1), :] = jnp.full((1, PW), owners[p, q, 0, r], jnp.int32)
                off_rows[pl.ds(n, 1), :] = jnp.full((1, PW), offsets[p, q, r], jnp.int32)
        return carry

    lax.fori_loop(0, ROWS, one, 0)
    count = PIECES * QCOLS * ROWS
    down = lax.broadcasted_iota(jnp.int32, (count, count), 0)
    along = lax.broadcasted_iota(jnp.int32, (count, count), 1)
    per_piece = QCOLS * ROWS
    own = own_rows[...]
    own_along = own.T
    earlier = (own == own_along) & (down < along) & ((down < per_piece) == (along < per_piece))
    rank = jnp.sum(earlier.astype(jnp.int32), axis=0, keepdims=True)
    across = own_along[0:1, :]

    def turned(owner):
        far = lax.rem(owner // COLS - z + NZ + NZ // 2, NZ)
        return jnp.where(far < NZ // 2, 2 * far, 2 * (NZ - far) - 1)

    spin = turned(across)
    chunk, pos = spin // 2, lax.rem(spin, 2)
    piece = along[0:1, :] // per_piece
    slot = ((chunk * COLS + lax.rem(across, COLS)) * 2 + pos) * 4 + piece * 2 + rank
    size = COLS * CHUNK_ROWS
    for h in range(N_CHUNKS):
        select[h] = (down[0:size] + h * size == slot).astype(jnp.bfloat16)
    mark = lax.rem(turned(own), 2) * PER_TILE + off_rows[...]
    extra[...] = (mark == along).astype(jnp.bfloat16)


def compute(ext, coeffs, observed, tables, clipped, rows, scratch):
    tall, wide, bands, seams = tables
    smooth, back, model = scratch
    for p in range(PIECES):
        for m in range(MODES):
            smooth[m, p * HEIGHT:(p + 1) * HEIGHT, :] = jnp.dot(
                tall[m * HEIGHT:(m + 1) * HEIGHT, :], ext[p], preferred_element_type=jnp.float32
            ).astype(jnp.bfloat16)
    model[...] = -observed[...]

    def forward(m, carry):
        parts = convolve(smooth[m], bands[m], seams[m], False)
        for q in range(QCOLS):
            cols = slice(q * PW, (q + 1) * PW)
            for p in range(PIECES):
                model[p, :, cols] += (
                    coeffs[p, m, :, cols].astype(jnp.float32) * parts[q][p * HEIGHT:(p + 1) * HEIGHT]
                )
        return carry

    lax.fori_loop(0, MODES, forward, 0, unroll=MODES)
    clipped[...] = jnp.clip(model[...], -DELTA, DELTA)

    def adjoint(m, carry):
        weighted = jnp.concatenate(
            [
                (coeffs[p, m].astype(jnp.float32) * clipped[p]).astype(jnp.bfloat16)
                for p in range(PIECES)
            ],
            axis=0,
        )
        parts = convolve(weighted, bands[m], seams[m], True)
        start = pl.multiple_of(m * HEIGHT, HEIGHT)
        for q in range(QCOLS):
            cols = slice(q * PW, (q + 1) * PW)
            for p in range(PIECES):
                back[p, pl.ds(start, HEIGHT), cols] = parts[q][p * HEIGHT:(p + 1) * HEIGHT].astype(
                    jnp.bfloat16
                )
        return carry

    lax.fori_loop(0, MODES, adjoint, 0, unroll=MODES)
    turned = jnp.concatenate([wide[m] for m in range(MODES)], axis=1)
    for p in range(PIECES):
        total = jnp.dot(turned, back[p], preferred_element_type=jnp.float32)
        for q in range(QCOLS):
            rows[p * QCOLS + q] = total[:, q * PW:(q + 1) * PW]


def kernel(owners, offsets, sky, coeffs_far, observed_far, vert, horiz, sky_out, clipped, *scratch):
    (
        coeffs, observed, base, tall, wide, bands, seams, own_rows, off_rows, select, extra,
        table, rim_out, rim_in, ext, smooth, back, model, rows, sky_mid,
        marks_out, marks_in, marks, count_out, count_in, scale, adj_out, *scratch
    ) = scratch
    load, mark_sems, fetch_sems = scratch[0], scratch[1:5], scratch[5:13]
    adj_in, reduce_refs, reduce_sems = scratch[13], scratch[13:19], scratch[19:]
    loads = [
        pltpu.make_async_copy(coeffs_far, coeffs, load.at[0]),
        pltpu.make_async_copy(observed_far, observed, load.at[1]),
    ]
    all_here = greet()
    for copy in loads:
        copy.start()
    own_tile(sky, table)
    build_tall(vert, base, tall)
    all_here()

    def early():
        build_wide(vert, base, wide)

    def late():
        build_bands(horiz, base, bands, seams)
        build_slots(owners, offsets, own_rows, off_rows, select, extra)

    def nothing():
        pass

    for step in range(STEPS):
        first = step == 0
        sems = [ref.at[step] for ref in fetch_sems]
        spread_tiles(table, sems[:6], early if first else nothing, late if first else nothing)
        fetch_image(owners, offsets, table, ext, rim_out, rim_in, *sems[6:])
        if first:
            send_marks(select, extra, marks_out, marks_in, *mark_sems[:2])
            for copy in loads:
                copy.wait()
        compute(ext, coeffs, observed, (tall, wide, bands, seams), clipped, rows, (smooth, back, model))
        sems = [ref.at[step] for ref in reduce_sems]
        rims = send_rims(rows, adj_out, adj_in, *sems[:2])
        if first:
            take_marks(marks_out, marks_in, marks, count_out, count_in, mark_sems)

        def get_scale():
            if first:
                take_counts(count_out, count_in, scale, mark_sems)
            return scale[...]

        before, after = (sky, sky_mid) if first else (sky_mid, sky_out)
        reduce_patches(rows, rims, select, marks, get_scale, before, after, (reduce_refs, sems[2:]))
        if first:
            own_tile(sky_mid, table)


def copy_out(sky_far, clipped_far, sky_out, clipped_out, sky, clipped, load, store):
    pairs = ((clipped_far, clipped, clipped_out), (sky_far, sky, sky_out))
    inward = [pltpu.make_async_copy(a, b, load.at[i]) for i, (a, b, _) in enumerate(pairs)]
    outward = [pltpu.make_async_copy(b, c, store.at[i]) for i, (_, b, c) in enumerate(pairs)]
    for copy in inward:
        copy.start()
    for came, goes in zip(inward, outward):
        came.wait()
        goes.start()
    for copy in outward:
        copy.wait()


def per_device(sky_map, coeffs, observed, vert_taps, horiz_taps, owner_ids, offset):
    sky = sky_map.reshape(PER_TILE * PH, PW)
    bf16, f32, i32 = jnp.bfloat16, jnp.float32, jnp.int32
    side = BREADTH // 2
    count = PIECES * QCOLS * ROWS
    dma = pltpu.SemaphoreType.DMA
    scratch = [
        pltpu.VMEM(coeffs.shape, bf16),
        pltpu.VMEM(observed.shape, f32),
        pltpu.VMEM((MODES, side), f32),
        pltpu.VMEM((MODES * HEIGHT, EXT), bf16),
        pltpu.VMEM((MODES, EXT, HEIGHT), bf16),
        pltpu.VMEM((MODES, side, side), bf16),
        pltpu.VMEM((MODES, side, side), bf16),
        pltpu.VMEM((count, PW), i32),
        pltpu.VMEM((count, PW), i32),
        pltpu.VMEM((N_CHUNKS, COLS * CHUNK_ROWS, count), bf16),
        pltpu.VMEM((count, PW), bf16),
        pltpu.VMEM((COLS * NZ * PER_TILE, PH, PW), bf16),
        pltpu.VMEM((2, PIECES, HALO, BREADTH), bf16),
        pltpu.VMEM((2, PIECES, HALO, BREADTH), bf16),
        pltpu.VMEM((PIECES, EXT, BREADTH), bf16),
        pltpu.VMEM((MODES, PIECES * HEIGHT, BREADTH), bf16),
        pltpu.VMEM((PIECES, MODES * HEIGHT, BREADTH), bf16),
        pltpu.VMEM((PIECES, HEIGHT, BREADTH), f32),
        pltpu.VMEM((PIECES * QCOLS, EXT, PW), f32),
        pltpu.VMEM((PER_TILE * PH, PW), f32),
        pltpu.VMEM((N_CHUNKS, COLS, CHUNK_ROWS, PW), bf16),
        pltpu.VMEM((N_CHUNKS, COLS, CHUNK_ROWS, PW), bf16),
        pltpu.VMEM((N_CHUNKS, 2 * PER_TILE, COLS * CHUNK_ROWS), bf16),
        pltpu.VMEM((NZ, PER_TILE, PW), f32),
        pltpu.VMEM((NZ, PER_TILE, PW), f32),
        pltpu.VMEM((PER_TILE, PW), f32),
        pltpu.VMEM((2, PIECES * QCOLS, HALO, PW), bf16),
        dma((2,)),
        dma((NX, NC)),
        dma((NX, NC)),
        dma((NZ,)),
        dma((NZ,)),
        dma((STEPS, NZ)),
        dma((STEPS, NZ)),
        dma((STEPS, NZ, NX)),
        dma((STEPS, NZ, NX)),
        dma((STEPS, NZ, NX)),
        dma((STEPS, NZ, NX)),
        dma((STEPS, 2)),
        dma((STEPS, 2)),
        pltpu.VMEM((2, PIECES * QCOLS, HALO, PW), bf16),
        pltpu.VMEM((count, SIZE), bf16),
        pltpu.VMEM((N_CHUNKS, COLS, CHUNK_ROWS, SIZE), bf16),
        pltpu.VMEM((N_CHUNKS, COLS, CHUNK_ROWS, SIZE), bf16),
        pltpu.VMEM((NZ, PER_TILE, SIZE), bf16),
        pltpu.VMEM((NZ, PER_TILE, SIZE), bf16),
        dma((STEPS, 2)),
        dma((STEPS, 2)),
        dma((STEPS, N_CHUNKS, NX, NC)),
        dma((STEPS, N_CHUNKS, NX, NC)),
        dma((STEPS, NZ)),
        dma((STEPS, NZ)),
    ]
    smem, vmem, far = pltpu.SMEM, pltpu.VMEM, pl.ANY
    sky_new, clipped = pl.pallas_call(
        kernel,
        out_shape=(
            jax.ShapeDtypeStruct(sky.shape, f32),
            jax.ShapeDtypeStruct(observed.shape, f32),
        ),
        in_specs=[pl.BlockSpec(memory_space=m) for m in (smem, smem, vmem, far, far, vmem, vmem)],
        out_specs=(pl.BlockSpec(memory_space=vmem), pl.BlockSpec(memory_space=vmem)),
        scratch_shapes=scratch,
        compiler_params=pltpu.CompilerParams(
            vmem_limit_bytes=VMEM_LIMIT, collective_id=0, has_side_effects=True
        ),
    )(owner_ids.transpose(0, 2, 3, 1), offset.transpose(0, 2, 1), sky, coeffs, observed, vert_taps, horiz_taps)
    sky_new, clipped = pl.pallas_call(
        copy_out,
        out_shape=(
            jax.ShapeDtypeStruct(sky.shape, f32),
            jax.ShapeDtypeStruct(observed.shape, f32),
        ),
        in_specs=[pl.BlockSpec(memory_space=far)] * 2,
        out_specs=(pl.BlockSpec(memory_space=far), pl.BlockSpec(memory_space=far)),
        scratch_shapes=[pltpu.VMEM(sky.shape, f32), pltpu.VMEM(observed.shape, f32), dma((2,)), dma((2,))],
        compiler_params=pltpu.CompilerParams(vmem_limit_bytes=VMEM_LIMIT),
    )(sky_new, clipped)
    return sky_new.reshape(sky_map.shape), clipped


def solution(mesh):
    return jax.shard_map(
        per_device,
        mesh=mesh,
        in_specs=(
            P(("exp", "sub"), None, None, None),
            P("exp", None, "sub", None),
            P("exp", "sub", None),
            P(),
            P(),
            P("exp", "sub", None, None),
            P("exp", "sub", None),
        ),
        out_specs=(P(("exp", "sub"), None, None, None), P("exp", "sub", None)),
        check_vma=False,
    )
```

```python
import jax
import jax.numpy as jnp
from jax import lax
from jax.experimental import pallas as pl
from jax.experimental.pallas import tpu as pltpu
from jax.sharding import PartitionSpec as P

STEPS = 2
ETA = 0.5
DELTA = 1.0

NZ, NX, NC = 8, 4, 2
COLS = NX * NC
MODES = 12
TAPS = 21
MARGIN = 10
PIECES = 2
HEIGHT = 128
BREADTH = 512
HALO = 16
TALL = HEIGHT + 2 * HALO
REACH = 2 * HALO
EXT = HEIGHT + 2 * REACH
PER_TILE = 8
PH = 8
PW = 128
ROWS = HEIGHT // PH
QCOLS = BREADTH // PW
SIZE = PH * PW
NEAR_ORDER = (0, 1, 7, 2, 6, 3, 5, 4)
FAR_ORDER = (4, 3, 5, 2, 6, 1, 7)
CHUNKS = ((4, 3), (5, 2), (6, 1), (7, 0))
N_CHUNKS = len(CHUNKS)
CHUNK_ROWS = 4 * len(CHUNKS[0])
PEERS = ((2, 0), (2, 1), (1, 0), (1, 1), (3, 0), (3, 1), (0, 1))
VMEM_LIMIT = 60 * 1024 * 1024


def place():
    e = lax.axis_index("exp")
    y = lax.axis_index("sub")
    return e // COLS, lax.rem(e // NC, NX), lax.rem(e, NC), y


def at_exp(z, x, c):
    return {"exp": (z * NX + x) * NC + c}


def remote(src, dst, send_sem, recv_sem, device):
    return pltpu.make_async_remote_copy(
        src_ref=src, dst_ref=dst, send_sem=send_sem, recv_sem=recv_sem,
        device_id=device, device_id_type=pl.DeviceIdType.MESH,
    )


def greet():
    z, x, c, y = place()
    barrier = pltpu.get_barrier_semaphore()
    many = 0
    for dz in range(1, NZ):
        pl.semaphore_signal(barrier, inc=1, device_id=at_exp(lax.rem(z + dz, NZ), x, c))
        many += 1
    for dx in range(NX):
        for dc in range(NC):
            if dx + dc > 0:
                pl.semaphore_signal(
                    barrier, inc=1, device_id=at_exp(z, lax.rem(x + dx, NX), lax.rem(c + dc, NC))
                )
                many += 1
    bands = lax.axis_size("sub")

    @pl.when(y > 0)
    def _():
        pl.semaphore_signal(barrier, inc=1, device_id={"sub": y - 1})

    @pl.when(y < bands - 1)
    def _():
        pl.semaphore_signal(barrier, inc=1, device_id={"sub": y + 1})

    return lambda: pl.semaphore_wait(
        barrier, many + jnp.minimum(y, 1) + jnp.minimum(bands - 1 - y, 1)
    )


def spread_tiles(table, sems, early, late):
    (zs, zr, xs, xr, cs, cr) = sems
    z, x, c, _ = place()
    col = x * NC + c

    def tile(col_at, z_at):
        return table.at[pl.ds((col_at * NZ + z_at) * PER_TILE, PER_TILE)]

    def along_z(dz, back):
        z_from = lax.rem(z - dz + NZ, NZ) if back else z
        block = tile(col, z_from)
        return remote(block, block, zs.at[dz], zr.at[dz], at_exp(lax.rem(z + dz, NZ), x, c))

    def along_x(dz, dx, back):
        x_from = lax.rem(x - dx + NX, NX) if back else x
        block = tile(x_from * NC + c, lax.rem(z - dz + NZ, NZ))
        return remote(block, block, xs.at[dz, dx], xr.at[dz, dx], at_exp(z, lax.rem(x + dx, NX), c))

    def to_twin(dz, dx, back):
        c_from = 1 - c if back else c
        block = tile(lax.rem(x - dx + NX, NX) * NC + c_from, lax.rem(z - dz + NZ, NZ))
        return remote(block, block, cs.at[dz, dx], cr.at[dz, dx], at_exp(z, x, 1 - c))

    for dz in FAR_ORDER:
        along_z(dz, False).start()
    early()
    for dz in NEAR_ORDER:
        if dz > 0:
            along_z(dz, True).wait_recv()
        for dx in (2, 1, 3):
            along_x(dz, dx, False).start()
        to_twin(dz, 0, False).start()
    late()
    for dz in NEAR_ORDER:
        for dx in (1, 3, 2):
            along_x(dz, dx, True).wait_recv()
            to_twin(dz, dx, False).start()
    for dz in NEAR_ORDER:
        for dx in range(NX):
            to_twin(dz, dx, True).wait_recv()
    for dz in range(NZ):
        if dz > 0:
            along_z(dz, False).wait_send()
        for dx in range(NX):
            if dx > 0:
                along_x(dz, dx, False).wait_send()
            to_twin(dz, dx, False).wait_send()


def gather_rows(owners, offsets, table, ext, pair):
    for p in range(PIECES):
        for q in range(QCOLS):
            both = []
            for half in range(2):
                r = pair * 2 + half
                owner = owners[p, q, 0, r]
                tile = lax.rem(owner, COLS) * NZ + owner // COLS
                both.append(table[tile * PER_TILE + offsets[p, q, r]].astype(jnp.float32))
            block = jnp.concatenate(both, axis=0).astype(jnp.bfloat16)
            if isinstance(pair, int):
                start = REACH + pair * 2 * PH
            else:
                start = pl.multiple_of(REACH + pair * 2 * PH, 2 * PH)
            ext[p, pl.ds(start, 2 * PH), q * PW:(q + 1) * PW] = block


def fetch_image(owners, offsets, table, ext, rim_out, rim_in, hs, hr):
    _, _, _, y = place()
    bands = lax.axis_size("sub")
    pairs = ROWS // 2
    for pair in (0, 1, pairs - 2, pairs - 1):
        gather_rows(owners, offsets, table, ext, pair)
    rim_out[0] = ext[:, REACH:2 * REACH, :]
    rim_out[1] = ext[:, HEIGHT:HEIGHT + REACH, :]
    up = remote(rim_out.at[0], rim_in.at[1], hs.at[0], hr.at[1], {"sub": y - 1})
    down = remote(rim_out.at[1], rim_in.at[0], hs.at[1], hr.at[0], {"sub": y + 1})

    @pl.when(y > 0)
    def _():
        up.start()

    @pl.when(y < bands - 1)
    def _():
        down.start()

    def more(pair, carry):
        gather_rows(owners, offsets, table, ext, pair)
        return carry

    lax.fori_loop(2, pairs - 2, more, 0)
    none = jnp.zeros((PIECES, REACH, BREADTH), jnp.bfloat16)

    @pl.when(y > 0)
    def _():
        down.wait_recv()
        ext[:, 0:REACH, :] = rim_in[0]

    @pl.when(y == 0)
    def _():
        ext[:, 0:REACH, :] = none

    @pl.when(y < bands - 1)
    def _():
        up.wait_recv()
        ext[:, REACH + HEIGHT:EXT, :] = rim_in[1]

    @pl.when(y == bands - 1)
    def _():
        ext[:, REACH + HEIGHT:EXT, :] = none

    @pl.when(y > 0)
    def _():
        up.wait_send()

    @pl.when(y < bands - 1)
    def _():
        down.wait_send()


def across(outgoing, incoming, send_sem, recv_sem, dx, dc, back, every=False):
    z, x, c, _ = place()
    x_to, c_to = lax.rem(x + dx, NX), lax.rem(c + dc, NC)
    x_from, c_from = (lax.rem(x - dx + NX, NX), c_to) if back else (x, c)
    to_at, from_at = x_to * NC + c_to, x_from * NC + c_from
    return remote(
        outgoing.at[:, to_at] if every else outgoing.at[to_at],
        incoming.at[:, from_at] if every else incoming.at[from_at],
        send_sem.at[dx, dc], recv_sem.at[dx, dc], at_exp(z, x_to, c_to),
    )


def along_line(outgoing, incoming, send_sem, recv_sem, rel):
    z, x, c, _ = place()
    return remote(
        outgoing.at[rel], incoming.at[rel], send_sem.at[rel], recv_sem.at[rel],
        at_exp(lax.rem(z + rel, NZ), x, c),
    )


def send_marks(select, extra, marks_out, marks_in, send_sem, recv_sem):
    z, x, c, _ = place()
    col = x * NC + c
    for chunk in range(N_CHUNKS):
        picked = jnp.dot(select[chunk], extra[...], preferred_element_type=jnp.float32)
        marks_out[chunk] = picked.reshape(COLS, CHUNK_ROWS, PW).astype(jnp.bfloat16)
    for dx, dc in PEERS:
        across(marks_out, marks_in, send_sem, recv_sem, dx, dc, False, True).start()
    marks_in[:, col] = marks_out[:, col]


def take_marks(marks_out, marks_in, marks, count_out, count_in, sems):
    send_sem, recv_sem, line_send, line_recv = sems
    for dx, dc in PEERS:
        across(marks_out, marks_in, send_sem, recv_sem, dx, dc, True, True).wait_recv()
    for chunk in range(N_CHUNKS):
        arrived = marks_in[chunk].astype(jnp.float32).reshape(COLS * CHUNK_ROWS, PW)
        turned = arrived.T[0:2 * PER_TILE].astype(jnp.bfloat16)
        marks[chunk] = turned
        many = jnp.dot(
            turned, jnp.ones((COLS * CHUNK_ROWS, PW), jnp.bfloat16), preferred_element_type=jnp.float32
        )
        for pos, rel in enumerate(CHUNKS[chunk]):
            count_out[rel] = many[pos * PER_TILE:(pos + 1) * PER_TILE]
    for rel in FAR_ORDER:
        along_line(count_out, count_in, line_send, line_recv, rel).start()
    for dx, dc in PEERS:
        across(marks_out, marks_in, send_sem, recv_sem, dx, dc, False, True).wait_send()


def take_counts(count_out, count_in, scale, sems):
    _, _, line_send, line_recv = sems
    total = count_out[0]
    for rel in NEAR_ORDER[1:]:
        along_line(count_out, count_in, line_send, line_recv, rel).wait_recv()
        total = total + count_in[rel]
    scale[...] = ETA / jnp.maximum(total, 1.0)
    for rel in FAR_ORDER:
        along_line(count_out, count_in, line_send, line_recv, rel).wait_send()


def share_rows(coeffs_far, observed_far, coeffs, observed, hs, hr):
    _, _, _, y = place()
    bands = lax.axis_size("sub")
    ends = (pl.ds(0, HALO), pl.ds(HALO + HEIGHT, HALO))
    edges = (pl.ds(0, HALO), pl.ds(HEIGHT - HALO, HALO))

    def pair(side, to):
        coming = ends[1 - side]
        return (
            remote(
                coeffs_far.at[:, :, edges[side]], coeffs.at[:, :, coming],
                hs.at[side, 0], hr.at[1 - side, 0], {"sub": to},
            ),
            remote(
                observed_far.at[:, edges[side]], observed.at[:, coming],
                hs.at[side, 1], hr.at[1 - side, 1], {"sub": to},
            ),
        )

    up, down = pair(0, y - 1), pair(1, y + 1)

    def start():
        @pl.when(y > 0)
        def _():
            for copy in up:
                copy.start()

        @pl.when(y < bands - 1)
        def _():
            for copy in down:
                copy.start()

        @pl.when(y == 0)
        def _():
            coeffs[:, :, ends[0]] = jnp.zeros((PIECES, MODES, HALO, BREADTH), jnp.bfloat16)
            observed[:, ends[0]] = jnp.zeros((PIECES, HALO, BREADTH), jnp.float32)

        @pl.when(y == bands - 1)
        def _():
            coeffs[:, :, ends[1]] = jnp.zeros((PIECES, MODES, HALO, BREADTH), jnp.bfloat16)
            observed[:, ends[1]] = jnp.zeros((PIECES, HALO, BREADTH), jnp.float32)

    def wait():
        @pl.when(y > 0)
        def _():
            for copy in down:
                copy.wait_recv()
            for copy in up:
                copy.wait_send()

        @pl.when(y < bands - 1)
        def _():
            for copy in up:
                copy.wait_recv()
            for copy in down:
                copy.wait_send()

    return start, wait


def reduce_patches(rows, select, marks, get_scale, sky, sky_new, scratch):
    (stacked, outgoing, incoming, line_out, line_in), sems = scratch
    axs, axr, bzs, bzr = sems
    _, x, c, _ = place()
    col = x * NC + c
    for n in range(PIECES * QCOLS):
        for i in range(PH):
            lines = rows[n, pl.ds(i, ROWS, stride=PH), :]
            stacked[n * ROWS:(n + 1) * ROWS, i * PW:(i + 1) * PW] = lines.astype(jnp.bfloat16)

    def exchange(chunk, dx, dc, back):
        return across(
            outgoing.at[chunk], incoming.at[chunk], axs.at[chunk], axr.at[chunk], dx, dc, back
        )

    for chunk in range(N_CHUNKS):
        picked = jnp.dot(select[chunk], stacked[...], preferred_element_type=jnp.float32)
        outgoing[chunk] = picked.reshape(COLS, CHUNK_ROWS, SIZE).astype(jnp.bfloat16)
        for dx, dc in PEERS:
            exchange(chunk, dx, dc, False).start()
        incoming[chunk, col] = outgoing[chunk, col]
    for chunk in range(N_CHUNKS):
        for dx, dc in PEERS[::-1]:
            exchange(chunk, dx, dc, True).wait_recv()
        arrived = incoming[chunk].astype(jnp.float32).reshape(COLS * CHUNK_ROWS, SIZE)
        totals = jnp.dot(
            marks[chunk], arrived.astype(jnp.bfloat16), preferred_element_type=jnp.float32
        )
        for pos, rel in enumerate(CHUNKS[chunk]):
            line_out[rel] = totals[pos * PER_TILE:(pos + 1) * PER_TILE].astype(jnp.bfloat16)
            if rel > 0:
                along_line(line_out, line_in, bzs, bzr, rel).start()
    scale = get_scale()
    total = line_out[0].astype(jnp.float32)
    for rel in NEAR_ORDER[1:]:
        along_line(line_out, line_in, bzs, bzr, rel).wait_recv()
        total = total + line_in[rel].astype(jnp.float32)
    for i in range(PH):
        old = sky[pl.ds(i, PER_TILE, stride=PH), :]
        sky_new[pl.ds(i, PER_TILE, stride=PH), :] = old - scale * total[:, i * PW:(i + 1) * PW]
    for chunk in range(N_CHUNKS):
        for dx, dc in PEERS:
            exchange(chunk, dx, dc, False).wait_send()
    for rel in range(1, NZ):
        along_line(line_out, line_in, bzs, bzr, rel).wait_send()


def own_tile(sky, table):
    z, x, c, _ = place()
    start = ((x * NC + c) * NZ + z) * PER_TILE
    for k in range(PER_TILE):
        table[start + k] = sky[k * PH:(k + 1) * PH, :].astype(jnp.bfloat16)


def convolve(block, centre, edge, transposed):
    dims = (((1,), (1 if transposed else 0,)), ((), ()))
    half = BREADTH // 2

    def product(a, b):
        return lax.dot_general(a, b, dims, preferred_element_type=jnp.float32)

    left = product(block[:, :half], centre)
    right = product(block[:, half:], centre)
    seam = product(block[:, PW:PW + half], edge)
    return [left[:, :PW], left[:, PW:] + seam[:, :PW], right[:, :PW] + seam[:, PW:], right[:, PW:]]


def diagonals(row, height):
    return pltpu.roll(jnp.broadcast_to(row, (height, row.shape[1])), 0, 1, stride=1, stride_axis=0)


def lag_rows(taps, lag):
    tap = lax.broadcasted_iota(jnp.int32, (TAPS, 2 * PW), 0)
    lane = lax.broadcasted_iota(jnp.int32, (TAPS, 2 * PW), 1)
    chosen = (tap == lag(lane)).astype(jnp.bfloat16)
    return jnp.dot(taps[...], chosen, preferred_element_type=jnp.float32)


def wrapped(lane):
    return jnp.where(lane < PW, lane, lane - 2 * PW)


def build_tall(vert, base, tall):
    base[...] = lag_rows(vert, lambda lane: lane - HALO + MARGIN)

    def one(m, carry):
        rows = diagonals(base[pl.ds(m, 1), :], TALL)
        tall[pl.ds(pl.multiple_of(m * TALL, TALL), TALL), :] = rows[:, :EXT].astype(jnp.bfloat16)
        return carry

    lax.fori_loop(0, MODES, one, 0)


def build_wide(vert, base, wide):
    base[...] = lag_rows(vert, lambda lane: HALO + MARGIN - lane)
    for m in range(MODES):
        rows = diagonals(base[m:m + 1, :], HEIGHT)
        wide[:, m * TALL:(m + 1) * TALL] = rows[:, :TALL].astype(jnp.bfloat16)


def build_bands(horiz, base, bands, seams):
    base[...] = lag_rows(horiz, lambda lane: MARGIN - wrapped(lane))
    side = BREADTH // 2
    w = lax.broadcasted_iota(jnp.int32, (side, side), 0)
    c = lax.broadcasted_iota(jnp.int32, (side, side), 1)
    near = jnp.abs(w - c) <= MARGIN
    across = near & ((w < PW) != (c < PW))

    def one(m, carry):
        rows = diagonals(base[pl.ds(m, 1), :], side)
        bands[m] = jnp.where(near, rows, 0.0).astype(jnp.bfloat16)
        seams[m] = jnp.where(across, rows, 0.0).astype(jnp.bfloat16)
        return carry

    lax.fori_loop(0, MODES, one, 0)


def build_slots(owners, offsets, own_rows, off_rows, select, extra):
    z, _, _, _ = place()

    def one(r, carry):
        for p in range(PIECES):
            for q in range(QCOLS):
                n = (p * QCOLS + q) * ROWS + r
                own_rows[pl.ds(n, 1), :] = jnp.full((1, PW), owners[p, q, 0, r], jnp.int32)
                off_rows[pl.ds(n, 1), :] = jnp.full((1, PW), offsets[p, q, r], jnp.int32)
        return carry

    lax.fori_loop(0, ROWS, one, 0)
    count = PIECES * QCOLS * ROWS
    down = lax.broadcasted_iota(jnp.int32, (count, count), 0)
    along = lax.broadcasted_iota(jnp.int32, (count, count), 1)
    per_piece = QCOLS * ROWS
    own = own_rows[...]
    own_along = own.T
    earlier = (own == own_along) & (down < along) & ((down < per_piece) == (along < per_piece))
    rank = jnp.sum(earlier.astype(jnp.int32), axis=0, keepdims=True)
    across = own_along[0:1, :]

    def turned(owner):
        far = lax.rem(owner // COLS - z + NZ + NZ // 2, NZ)
        return jnp.where(far < NZ // 2, 2 * far, 2 * (NZ - far) - 1)

    spin = turned(across)
    chunk, pos = spin // 2, lax.rem(spin, 2)
    piece = along[0:1, :] // per_piece
    slot = ((chunk * COLS + lax.rem(across, COLS)) * 2 + pos) * 4 + piece * 2 + rank
    size = COLS * CHUNK_ROWS
    for h in range(N_CHUNKS):
        select[h] = (down[0:size] + h * size == slot).astype(jnp.bfloat16)
    mark = lax.rem(turned(own), 2) * PER_TILE + off_rows[...]
    extra[...] = (mark == along).astype(jnp.bfloat16)


def compute(ext, coeffs, observed, tables, clipped, rows, scratch):
    tall, wide, bands, seams = tables
    smooth, back, model = scratch
    for p in range(PIECES):
        for m in range(MODES):
            smooth[m, p * TALL:(p + 1) * TALL, :] = jnp.dot(
                tall[m * TALL:(m + 1) * TALL, :], ext[p], preferred_element_type=jnp.float32
            ).astype(jnp.bfloat16)
    model[...] = -observed[...]

    def forward(m, carry):
        parts = convolve(smooth[m], bands[m], seams[m], False)
        for q in range(QCOLS):
            cols = slice(q * PW, (q + 1) * PW)
            for p in range(PIECES):
                model[p, :, cols] += (
                    coeffs[p, m, :, cols].astype(jnp.float32) * parts[q][p * TALL:(p + 1) * TALL]
                )
        return carry

    lax.fori_loop(0, MODES, forward, 0, unroll=MODES)
    model[...] = jnp.clip(model[...], -DELTA, DELTA)
    if clipped is not None:
        clipped[...] = model[:, HALO:HALO + HEIGHT, :]

    def adjoint(m, carry):
        weighted = jnp.concatenate(
            [
                (coeffs[p, m].astype(jnp.float32) * model[p]).astype(jnp.bfloat16)
                for p in range(PIECES)
            ],
            axis=0,
        )
        parts = convolve(weighted, bands[m], seams[m], True)
        start = pl.multiple_of(m * TALL, TALL)
        for q in range(QCOLS):
            cols = slice(q * PW, (q + 1) * PW)
            for p in range(PIECES):
                back[p, pl.ds(start, TALL), cols] = parts[q][p * TALL:(p + 1) * TALL].astype(
                    jnp.bfloat16
                )
        return carry

    lax.fori_loop(0, MODES, adjoint, 0, unroll=MODES)
    for p in range(PIECES):
        total = jnp.dot(wide[...], back[p], preferred_element_type=jnp.float32)
        for q in range(QCOLS):
            rows[p * QCOLS + q] = total[:, q * PW:(q + 1) * PW]


def kernel(owners, offsets, sky, coeffs_far, observed_far, vert, horiz, sky_out, clipped, *scratch):
    (
        coeffs, observed, base, tall, wide, bands, seams, own_rows, off_rows, select, extra,
        table, rim_out, rim_in, ext, smooth, back, model, rows, sky_mid,
        marks_out, marks_in, marks, count_out, count_in, scale, *scratch
    ) = scratch
    load, share_sems, mark_sems, fetch_sems = scratch[0], scratch[1:3], scratch[3:7], scratch[7:15]
    reduce_refs, reduce_sems = scratch[15:20], scratch[20:]
    inner = pl.ds(HALO, HEIGHT)
    loads = [
        pltpu.make_async_copy(coeffs_far, coeffs.at[:, :, inner], load.at[0]),
        pltpu.make_async_copy(observed_far, observed.at[:, inner], load.at[1]),
    ]
    share, shared = share_rows(coeffs_far, observed_far, coeffs, observed, *share_sems)
    all_here = greet()
    for copy in loads:
        copy.start()
    own_tile(sky, table)
    build_tall(vert, base, tall)
    all_here()

    def early():
        share()
        build_wide(vert, base, wide)

    def late():
        build_bands(horiz, base, bands, seams)
        build_slots(owners, offsets, own_rows, off_rows, select, extra)

    def nothing():
        pass

    for step in range(STEPS):
        first = step == 0
        sems = [ref.at[step] for ref in fetch_sems]
        spread_tiles(table, sems[:6], early if first else nothing, late if first else nothing)
        fetch_image(owners, offsets, table, ext, rim_out, rim_in.at[step], *sems[6:])
        if first:
            send_marks(select, extra, marks_out, marks_in, *mark_sems[:2])
            for copy in loads:
                copy.wait()
            shared()
        tables = (tall, wide, bands, seams)
        compute(ext, coeffs, observed, tables, None if first else clipped, rows, (smooth, back, model))
        sems = [ref.at[step] for ref in reduce_sems]
        if first:
            take_marks(marks_out, marks_in, marks, count_out, count_in, mark_sems)

        def get_scale():
            if first:
                take_counts(count_out, count_in, scale, mark_sems)
            return scale[...]

        before, after = (sky, sky_mid) if first else (sky_mid, sky_out)
        reduce_patches(rows, select, marks, get_scale, before, after, (reduce_refs, sems))
        if first:
            own_tile(sky_mid, table)


def copy_out(sky_far, clipped_far, sky_out, clipped_out, sky, clipped, load, store):
    pairs = ((clipped_far, clipped, clipped_out), (sky_far, sky, sky_out))
    inward = [pltpu.make_async_copy(a, b, load.at[i]) for i, (a, b, _) in enumerate(pairs)]
    outward = [pltpu.make_async_copy(b, c, store.at[i]) for i, (_, b, c) in enumerate(pairs)]
    for copy in inward:
        copy.start()
    for came, goes in zip(inward, outward):
        came.wait()
        goes.start()
    for copy in outward:
        copy.wait()


def per_device(sky_map, coeffs, observed, vert_taps, horiz_taps, owner_ids, offset):
    sky = sky_map.reshape(PER_TILE * PH, PW)
    bf16, f32, i32 = jnp.bfloat16, jnp.float32, jnp.int32
    side = BREADTH // 2
    count = PIECES * QCOLS * ROWS
    dma = pltpu.SemaphoreType.DMA
    scratch = [
        pltpu.VMEM((PIECES, MODES, TALL, BREADTH), bf16),
        pltpu.VMEM((PIECES, TALL, BREADTH), f32),
        pltpu.VMEM((MODES, side), f32),
        pltpu.VMEM((MODES * TALL, EXT), bf16),
        pltpu.VMEM((HEIGHT, MODES * TALL), bf16),
        pltpu.VMEM((MODES, side, side), bf16),
        pltpu.VMEM((MODES, side, side), bf16),
        pltpu.VMEM((count, PW), i32),
        pltpu.VMEM((count, PW), i32),
        pltpu.VMEM((N_CHUNKS, COLS * CHUNK_ROWS, count), bf16),
        pltpu.VMEM((count, PW), bf16),
        pltpu.VMEM((COLS * NZ * PER_TILE, PH, PW), bf16),
        pltpu.VMEM((2, PIECES, REACH, BREADTH), bf16),
        pltpu.VMEM((STEPS, 2, PIECES, REACH, BREADTH), bf16),
        pltpu.VMEM((PIECES, EXT, BREADTH), bf16),
        pltpu.VMEM((MODES, PIECES * TALL, BREADTH), bf16),
        pltpu.VMEM((PIECES, MODES * TALL, BREADTH), bf16),
        pltpu.VMEM((PIECES, TALL, BREADTH), f32),
        pltpu.VMEM((PIECES * QCOLS, HEIGHT, PW), f32),
        pltpu.VMEM((PER_TILE * PH, PW), f32),
        pltpu.VMEM((N_CHUNKS, COLS, CHUNK_ROWS, PW), bf16),
        pltpu.VMEM((N_CHUNKS, COLS, CHUNK_ROWS, PW), bf16),
        pltpu.VMEM((N_CHUNKS, 2 * PER_TILE, COLS * CHUNK_ROWS), bf16),
        pltpu.VMEM((NZ, PER_TILE, PW), f32),
        pltpu.VMEM((NZ, PER_TILE, PW), f32),
        pltpu.VMEM((PER_TILE, PW), f32),
        dma((2,)),
        dma((2, 2)),
        dma((2, 2)),
        dma((NX, NC)),
        dma((NX, NC)),
        dma((NZ,)),
        dma((NZ,)),
        dma((STEPS, NZ)),
        dma((STEPS, NZ)),
        dma((STEPS, NZ, NX)),
        dma((STEPS, NZ, NX)),
        dma((STEPS, NZ, NX)),
        dma((STEPS, NZ, NX)),
        dma((STEPS, 2)),
        dma((STEPS, 2)),
        pltpu.VMEM((count, SIZE), bf16),
        pltpu.VMEM((N_CHUNKS, COLS, CHUNK_ROWS, SIZE), bf16),
        pltpu.VMEM((N_CHUNKS, COLS, CHUNK_ROWS, SIZE), bf16),
        pltpu.VMEM((NZ, PER_TILE, SIZE), bf16),
        pltpu.VMEM((NZ, PER_TILE, SIZE), bf16),
        dma((STEPS, N_CHUNKS, NX, NC)),
        dma((STEPS, N_CHUNKS, NX, NC)),
        dma((STEPS, NZ)),
        dma((STEPS, NZ)),
    ]
    smem, vmem, far = pltpu.SMEM, pltpu.VMEM, pl.ANY
    sky_new, clipped = pl.pallas_call(
        kernel,
        out_shape=(
            jax.ShapeDtypeStruct(sky.shape, f32),
            jax.ShapeDtypeStruct(observed.shape, f32),
        ),
        in_specs=[pl.BlockSpec(memory_space=m) for m in (smem, smem, vmem, far, far, vmem, vmem)],
        out_specs=(pl.BlockSpec(memory_space=vmem), pl.BlockSpec(memory_space=vmem)),
        scratch_shapes=scratch,
        compiler_params=pltpu.CompilerParams(
            vmem_limit_bytes=VMEM_LIMIT, collective_id=0, has_side_effects=True
        ),
    )(owner_ids.transpose(0, 2, 3, 1), offset.transpose(0, 2, 1), sky, coeffs, observed, vert_taps, horiz_taps)
    sky_new, clipped = pl.pallas_call(
        copy_out,
        out_shape=(
            jax.ShapeDtypeStruct(sky.shape, f32),
            jax.ShapeDtypeStruct(observed.shape, f32),
        ),
        in_specs=[pl.BlockSpec(memory_space=far)] * 2,
        out_specs=(pl.BlockSpec(memory_space=far), pl.BlockSpec(memory_space=far)),
        scratch_shapes=[pltpu.VMEM(sky.shape, f32), pltpu.VMEM(observed.shape, f32), dma((2,)), dma((2,))],
        compiler_params=pltpu.CompilerParams(vmem_limit_bytes=VMEM_LIMIT),
    )(sky_new, clipped)
    return sky_new.reshape(sky_map.shape), clipped


def solution(mesh):
    return jax.shard_map(
        per_device,
        mesh=mesh,
        in_specs=(
            P(("exp", "sub"), None, None, None),
            P("exp", None, "sub", None),
            P("exp", "sub", None),
            P(),
            P(),
            P("exp", "sub", None, None),
            P("exp", "sub", None),
        ),
        out_specs=(P(("exp", "sub"), None, None, None), P("exp", "sub", None)),
        check_vma=False,
    )
```

```python
import jax
import jax.numpy as jnp
from jax import lax
from jax.experimental import pallas as pl
from jax.experimental.pallas import tpu as pltpu
from jax.sharding import PartitionSpec as P

STEPS = 2
ETA = 0.5
DELTA = 1.0

NZ, NX, NC = 8, 4, 2
COLS = NX * NC
MODES = 12
TAPS = 21
MARGIN = 10
PIECES = 2
HEIGHT = 128
BREADTH = 512
HALO = 16
TALL = HEIGHT + 2 * HALO
REACH = 2 * HALO
EXT = HEIGHT + 2 * REACH
PER_TILE = 8
PH = 8
PW = 128
ROWS = HEIGHT // PH
QCOLS = BREADTH // PW
SIZE = PH * PW
NEAR_ORDER = (0, 1, 7, 2, 6, 3, 5, 4)
FAR_ORDER = (4, 3, 5, 2, 6, 1, 7)
CHUNKS = ((4, 3), (5, 2), (6, 1), (7, 0))
N_CHUNKS = len(CHUNKS)
CHUNK_ROWS = 4 * len(CHUNKS[0])
PEERS = ((2, 0), (2, 1), (1, 0), (1, 1), (3, 0), (3, 1), (0, 1))
VMEM_LIMIT = 60 * 1024 * 1024


def place():
    e = lax.axis_index("exp")
    y = lax.axis_index("sub")
    return e // COLS, lax.rem(e // NC, NX), lax.rem(e, NC), y


def at_exp(z, x, c):
    return {"exp": (z * NX + x) * NC + c}


def remote(src, dst, send_sem, recv_sem, device):
    return pltpu.make_async_remote_copy(
        src_ref=src, dst_ref=dst, send_sem=send_sem, recv_sem=recv_sem,
        device_id=device, device_id_type=pl.DeviceIdType.MESH,
    )


def greet():
    z, x, c, y = place()
    barrier = pltpu.get_barrier_semaphore()
    many = 0
    for dz in range(1, NZ):
        pl.semaphore_signal(barrier, inc=1, device_id=at_exp(lax.rem(z + dz, NZ), x, c))
        many += 1
    for dx in range(NX):
        for dc in range(NC):
            if dx + dc > 0:
                pl.semaphore_signal(
                    barrier, inc=1, device_id=at_exp(z, lax.rem(x + dx, NX), lax.rem(c + dc, NC))
                )
                many += 1
    bands = lax.axis_size("sub")

    @pl.when(y > 0)
    def _():
        pl.semaphore_signal(barrier, inc=1, device_id={"sub": y - 1})

    @pl.when(y < bands - 1)
    def _():
        pl.semaphore_signal(barrier, inc=1, device_id={"sub": y + 1})

    return lambda: pl.semaphore_wait(
        barrier, many + jnp.minimum(y, 1) + jnp.minimum(bands - 1 - y, 1)
    )


def spread_tiles(table, sems, early, late):
    (zs, zr, xs, xr, cs, cr) = sems
    z, x, c, _ = place()
    col = x * NC + c

    def tile(col_at, z_at):
        return table.at[pl.ds((col_at * NZ + z_at) * PER_TILE, PER_TILE)]

    def along_z(dz, back):
        z_from = lax.rem(z - dz + NZ, NZ) if back else z
        block = tile(col, z_from)
        return remote(block, block, zs.at[dz], zr.at[dz], at_exp(lax.rem(z + dz, NZ), x, c))

    def along_x(dz, dx, back):
        x_from = lax.rem(x - dx + NX, NX) if back else x
        block = tile(x_from * NC + c, lax.rem(z - dz + NZ, NZ))
        return remote(block, block, xs.at[dz, dx], xr.at[dz, dx], at_exp(z, lax.rem(x + dx, NX), c))

    def to_twin(dz, dx, back):
        c_from = 1 - c if back else c
        block = tile(lax.rem(x - dx + NX, NX) * NC + c_from, lax.rem(z - dz + NZ, NZ))
        return remote(block, block, cs.at[dz, dx], cr.at[dz, dx], at_exp(z, x, 1 - c))

    for dz in FAR_ORDER:
        along_z(dz, False).start()
    early()
    for dz in NEAR_ORDER:
        if dz > 0:
            along_z(dz, True).wait_recv()
        for dx in (2, 1, 3):
            along_x(dz, dx, False).start()
        to_twin(dz, 0, False).start()
    late()
    for dz in NEAR_ORDER:
        for dx in (1, 3, 2):
            along_x(dz, dx, True).wait_recv()
            to_twin(dz, dx, False).start()
    for dz in NEAR_ORDER:
        for dx in range(NX):
            to_twin(dz, dx, True).wait_recv()

    def sent():
        for dz in range(NZ):
            if dz > 0:
                along_z(dz, False).wait_send()
            for dx in range(NX):
                if dx > 0:
                    along_x(dz, dx, False).wait_send()
                to_twin(dz, dx, False).wait_send()

    return sent


def gather_rows(owners, offsets, table, ext, pair):
    for p in range(PIECES):
        for q in range(QCOLS):
            both = []
            for half in range(2):
                r = pair * 2 + half
                owner = owners[p, q, 0, r]
                tile = lax.rem(owner, COLS) * NZ + owner // COLS
                both.append(table[tile * PER_TILE + offsets[p, q, r]].astype(jnp.float32))
            block = jnp.concatenate(both, axis=0).astype(jnp.bfloat16)
            if isinstance(pair, int):
                start = REACH + pair * 2 * PH
            else:
                start = pl.multiple_of(REACH + pair * 2 * PH, 2 * PH)
            ext[p, pl.ds(start, 2 * PH), q * PW:(q + 1) * PW] = block


def fetch_image(owners, offsets, table, ext, rim_out, rim_in, hs, hr, meanwhile):
    _, _, _, y = place()
    bands = lax.axis_size("sub")
    pairs = ROWS // 2
    for pair in (0, 1, pairs - 2, pairs - 1):
        gather_rows(owners, offsets, table, ext, pair)
    rim_out[0] = ext[:, REACH:2 * REACH, :]
    rim_out[1] = ext[:, HEIGHT:HEIGHT + REACH, :]
    up = remote(rim_out.at[0], rim_in.at[1], hs.at[0], hr.at[1], {"sub": y - 1})
    down = remote(rim_out.at[1], rim_in.at[0], hs.at[1], hr.at[0], {"sub": y + 1})

    @pl.when(y > 0)
    def _():
        up.start()

    @pl.when(y < bands - 1)
    def _():
        down.start()

    def more(pair, carry):
        gather_rows(owners, offsets, table, ext, pair)
        return carry

    lax.fori_loop(2, pairs - 2, more, 0)
    for finish in meanwhile:
        finish()
    none = jnp.zeros((PIECES, REACH, BREADTH), jnp.bfloat16)

    @pl.when(y > 0)
    def _():
        down.wait_recv()
        ext[:, 0:REACH, :] = rim_in[0]

    @pl.when(y == 0)
    def _():
        ext[:, 0:REACH, :] = none

    @pl.when(y < bands - 1)
    def _():
        up.wait_recv()
        ext[:, REACH + HEIGHT:EXT, :] = rim_in[1]

    @pl.when(y == bands - 1)
    def _():
        ext[:, REACH + HEIGHT:EXT, :] = none

    @pl.when(y > 0)
    def _():
        up.wait_send()

    @pl.when(y < bands - 1)
    def _():
        down.wait_send()


def across(outgoing, incoming, send_sem, recv_sem, dx, dc, back, every=False):
    z, x, c, _ = place()
    x_to, c_to = lax.rem(x + dx, NX), lax.rem(c + dc, NC)
    x_from, c_from = (lax.rem(x - dx + NX, NX), c_to) if back else (x, c)
    to_at, from_at = x_to * NC + c_to, x_from * NC + c_from
    return remote(
        outgoing.at[:, to_at] if every else outgoing.at[to_at],
        incoming.at[:, from_at] if every else incoming.at[from_at],
        send_sem.at[dx, dc], recv_sem.at[dx, dc], at_exp(z, x_to, c_to),
    )


def along_line(outgoing, incoming, send_sem, recv_sem, rel):
    z, x, c, _ = place()
    return remote(
        outgoing.at[rel], incoming.at[rel], send_sem.at[rel], recv_sem.at[rel],
        at_exp(lax.rem(z + rel, NZ), x, c),
    )


def send_marks(select, extra, marks_out, marks_in, send_sem, recv_sem):
    z, x, c, _ = place()
    col = x * NC + c
    for chunk in range(N_CHUNKS):
        picked = jnp.dot(select[chunk], extra[...], preferred_element_type=jnp.float32)
        marks_out[chunk] = picked.reshape(COLS, CHUNK_ROWS, PW).astype(jnp.bfloat16)
    for dx, dc in PEERS:
        across(marks_out, marks_in, send_sem, recv_sem, dx, dc, False, True).start()
    marks_in[:, col] = marks_out[:, col]


def take_marks(marks_out, marks_in, marks, count_out, count_in, sems):
    send_sem, recv_sem, line_send, line_recv = sems
    for dx, dc in PEERS:
        across(marks_out, marks_in, send_sem, recv_sem, dx, dc, True, True).wait_recv()
    for chunk in range(N_CHUNKS):
        arrived = marks_in[chunk].astype(jnp.float32).reshape(COLS * CHUNK_ROWS, PW)
        turned = arrived.T[0:2 * PER_TILE].astype(jnp.bfloat16)
        marks[chunk] = turned
        many = jnp.dot(
            turned, jnp.ones((COLS * CHUNK_ROWS, PW), jnp.bfloat16), preferred_element_type=jnp.float32
        )
        for pos, rel in enumerate(CHUNKS[chunk]):
            count_out[rel] = many[pos * PER_TILE:(pos + 1) * PER_TILE]
    for rel in FAR_ORDER:
        along_line(count_out, count_in, line_send, line_recv, rel).start()


def take_counts(marks_out, marks_in, count_out, count_in, scale, sems):
    send_sem, recv_sem, line_send, line_recv = sems
    for dx, dc in PEERS:
        across(marks_out, marks_in, send_sem, recv_sem, dx, dc, False, True).wait_send()
    total = count_out[0]
    for rel in NEAR_ORDER[1:]:
        along_line(count_out, count_in, line_send, line_recv, rel).wait_recv()
        total = total + count_in[rel]
    scale[...] = ETA / jnp.maximum(total, 1.0)
    for rel in FAR_ORDER:
        along_line(count_out, count_in, line_send, line_recv, rel).wait_send()


def share_rows(coeffs_far, observed_far, coeffs, observed, hs, hr):
    _, _, _, y = place()
    bands = lax.axis_size("sub")
    ends = (pl.ds(0, HALO), pl.ds(HALO + HEIGHT, HALO))
    edges = (pl.ds(0, HALO), pl.ds(HEIGHT - HALO, HALO))

    def pair(side, to):
        coming = ends[1 - side]
        return (
            remote(
                coeffs_far.at[:, :, edges[side]], coeffs.at[:, :, coming],
                hs.at[side, 0], hr.at[1 - side, 0], {"sub": to},
            ),
            remote(
                observed_far.at[:, edges[side]], observed.at[:, coming],
                hs.at[side, 1], hr.at[1 - side, 1], {"sub": to},
            ),
        )

    up, down = pair(0, y - 1), pair(1, y + 1)

    def start():
        @pl.when(y > 0)
        def _():
            for copy in up:
                copy.start()

        @pl.when(y < bands - 1)
        def _():
            for copy in down:
                copy.start()

        @pl.when(y == 0)
        def _():
            coeffs[:, :, ends[0]] = jnp.zeros((PIECES, MODES, HALO, BREADTH), jnp.bfloat16)
            observed[:, ends[0]] = jnp.zeros((PIECES, HALO, BREADTH), jnp.float32)

        @pl.when(y == bands - 1)
        def _():
            coeffs[:, :, ends[1]] = jnp.zeros((PIECES, MODES, HALO, BREADTH), jnp.bfloat16)
            observed[:, ends[1]] = jnp.zeros((PIECES, HALO, BREADTH), jnp.float32)

    def wait():
        @pl.when(y > 0)
        def _():
            for copy in down:
                copy.wait_recv()
            for copy in up:
                copy.wait_send()

        @pl.when(y < bands - 1)
        def _():
            for copy in up:
                copy.wait_recv()
            for copy in down:
                copy.wait_send()

    return start, wait


def reduce_patches(rows, select, marks, get_scale, sky, sky_new, scratch):
    (stacked, outgoing, incoming, line_out, line_in), sems = scratch
    axs, axr, bzs, bzr = sems
    _, x, c, _ = place()
    col = x * NC + c
    for n in range(PIECES * QCOLS):
        for i in range(PH):
            lines = rows[n, pl.ds(i, ROWS, stride=PH), :]
            stacked[n * ROWS:(n + 1) * ROWS, i * PW:(i + 1) * PW] = lines.astype(jnp.bfloat16)

    def exchange(chunk, dx, dc, back):
        return across(
            outgoing.at[chunk], incoming.at[chunk], axs.at[chunk], axr.at[chunk], dx, dc, back
        )

    for chunk in range(N_CHUNKS):
        picked = jnp.dot(select[chunk], stacked[...], preferred_element_type=jnp.float32)
        outgoing[chunk] = picked.reshape(COLS, CHUNK_ROWS, SIZE).astype(jnp.bfloat16)
        for dx, dc in PEERS:
            exchange(chunk, dx, dc, False).start()
        incoming[chunk, col] = outgoing[chunk, col]
    for chunk in range(N_CHUNKS):
        for dx, dc in PEERS[::-1]:
            exchange(chunk, dx, dc, True).wait_recv()
        arrived = incoming[chunk].astype(jnp.float32).reshape(COLS * CHUNK_ROWS, SIZE)
        totals = jnp.dot(
            marks[chunk], arrived.astype(jnp.bfloat16), preferred_element_type=jnp.float32
        )
        for pos, rel in enumerate(CHUNKS[chunk]):
            line_out[rel] = totals[pos * PER_TILE:(pos + 1) * PER_TILE].astype(jnp.bfloat16)
            if rel > 0:
                along_line(line_out, line_in, bzs, bzr, rel).start()
    scale = get_scale()
    for chunk in range(N_CHUNKS):
        for dx, dc in PEERS:
            exchange(chunk, dx, dc, False).wait_send()
    total = line_out[0].astype(jnp.float32)
    for rel in NEAR_ORDER[1:]:
        along_line(line_out, line_in, bzs, bzr, rel).wait_recv()
        total = total + line_in[rel].astype(jnp.float32)
    for i in range(PH):
        old = sky[pl.ds(i, PER_TILE, stride=PH), :]
        sky_new[pl.ds(i, PER_TILE, stride=PH), :] = old - scale * total[:, i * PW:(i + 1) * PW]

    def sent():
        for rel in range(1, NZ):
            along_line(line_out, line_in, bzs, bzr, rel).wait_send()

    return sent


def own_tile(sky, table):
    z, x, c, _ = place()
    start = ((x * NC + c) * NZ + z) * PER_TILE
    for k in range(PER_TILE):
        table[start + k] = sky[k * PH:(k + 1) * PH, :].astype(jnp.bfloat16)


def convolve(block, centre, edge, transposed):
    dims = (((1,), (1 if transposed else 0,)), ((), ()))
    half = BREADTH // 2

    def product(a, b):
        return lax.dot_general(a, b, dims, preferred_element_type=jnp.float32)

    left = product(block[:, :half], centre)
    right = product(block[:, half:], centre)
    seam = product(block[:, PW:PW + half], edge)
    return [left[:, :PW], left[:, PW:] + seam[:, :PW], right[:, :PW] + seam[:, PW:], right[:, PW:]]


def diagonals(row, height):
    return pltpu.roll(jnp.broadcast_to(row, (height, row.shape[1])), 0, 1, stride=1, stride_axis=0)


def lag_rows(taps, lag):
    tap = lax.broadcasted_iota(jnp.int32, (TAPS, 2 * PW), 0)
    lane = lax.broadcasted_iota(jnp.int32, (TAPS, 2 * PW), 1)
    chosen = (tap == lag(lane)).astype(jnp.bfloat16)
    return jnp.dot(taps[...], chosen, preferred_element_type=jnp.float32)


def wrapped(lane):
    return jnp.where(lane < PW, lane, lane - 2 * PW)


def build_tall(vert, base, tall):
    base[...] = lag_rows(vert, lambda lane: lane - HALO + MARGIN)

    def one(m, carry):
        rows = diagonals(base[pl.ds(m, 1), :], TALL)
        tall[pl.ds(pl.multiple_of(m * TALL, TALL), TALL), :] = rows[:, :EXT].astype(jnp.bfloat16)
        return carry

    lax.fori_loop(0, MODES, one, 0)


def build_wide(vert, base, wide):
    base[...] = lag_rows(vert, lambda lane: HALO + MARGIN - lane)
    for m in range(MODES):
        rows = diagonals(base[m:m + 1, :], HEIGHT)
        wide[:, m * TALL:(m + 1) * TALL] = rows[:, :TALL].astype(jnp.bfloat16)


def build_bands(horiz, base, bands, seams):
    base[...] = lag_rows(horiz, lambda lane: MARGIN - wrapped(lane))
    side = BREADTH // 2
    w = lax.broadcasted_iota(jnp.int32, (side, side), 0)
    c = lax.broadcasted_iota(jnp.int32, (side, side), 1)
    near = jnp.abs(w - c) <= MARGIN
    across = near & ((w < PW) != (c < PW))

    def one(m, carry):
        rows = diagonals(base[pl.ds(m, 1), :], side)
        bands[m] = jnp.where(near, rows, 0.0).astype(jnp.bfloat16)
        seams[m] = jnp.where(across, rows, 0.0).astype(jnp.bfloat16)
        return carry

    lax.fori_loop(0, MODES, one, 0)


def build_slots(owners, offsets, own_rows, off_rows, select, extra):
    z, _, _, _ = place()

    def one(r, carry):
        for p in range(PIECES):
            for q in range(QCOLS):
                n = (p * QCOLS + q) * ROWS + r
                own_rows[pl.ds(n, 1), :] = jnp.full((1, PW), owners[p, q, 0, r], jnp.int32)
                off_rows[pl.ds(n, 1), :] = jnp.full((1, PW), offsets[p, q, r], jnp.int32)
        return carry

    lax.fori_loop(0, ROWS, one, 0)
    count = PIECES * QCOLS * ROWS
    down = lax.broadcasted_iota(jnp.int32, (count, count), 0)
    along = lax.broadcasted_iota(jnp.int32, (count, count), 1)
    per_piece = QCOLS * ROWS
    own = own_rows[...]
    own_along = own.T
    earlier = (own == own_along) & (down < along) & ((down < per_piece) == (along < per_piece))
    rank = jnp.sum(earlier.astype(jnp.int32), axis=0, keepdims=True)
    across = own_along[0:1, :]

    def turned(owner):
        far = lax.rem(owner // COLS - z + NZ + NZ // 2, NZ)
        return jnp.where(far < NZ // 2, 2 * far, 2 * (NZ - far) - 1)

    spin = turned(across)
    chunk, pos = spin // 2, lax.rem(spin, 2)
    piece = along[0:1, :] // per_piece
    slot = ((chunk * COLS + lax.rem(across, COLS)) * 2 + pos) * 4 + piece * 2 + rank
    size = COLS * CHUNK_ROWS
    for h in range(N_CHUNKS):
        select[h] = (down[0:size] + h * size == slot).astype(jnp.bfloat16)
    mark = lax.rem(turned(own), 2) * PER_TILE + off_rows[...]
    extra[...] = (mark == along).astype(jnp.bfloat16)


def compute(ext, coeffs, observed, tables, clipped, rows, scratch):
    tall, wide, bands, seams = tables
    smooth, back, model = scratch
    for p in range(PIECES):
        for m in range(MODES):
            smooth[m, p * TALL:(p + 1) * TALL, :] = jnp.dot(
                tall[m * TALL:(m + 1) * TALL, :], ext[p], preferred_element_type=jnp.float32
            ).astype(jnp.bfloat16)
    model[...] = -observed[...]

    def forward(m, carry):
        parts = convolve(smooth[m], bands[m], seams[m], False)
        for q in range(QCOLS):
            cols = slice(q * PW, (q + 1) * PW)
            for p in range(PIECES):
                model[p, :, cols] += (
                    coeffs[p, m, :, cols].astype(jnp.float32) * parts[q][p * TALL:(p + 1) * TALL]
                )
        return carry

    lax.fori_loop(0, MODES, forward, 0, unroll=MODES)
    model[...] = jnp.clip(model[...], -DELTA, DELTA)
    if clipped is not None:
        clipped[...] = model[:, HALO:HALO + HEIGHT, :]

    def adjoint(m, carry):
        weighted = jnp.concatenate(
            [
                (coeffs[p, m].astype(jnp.float32) * model[p]).astype(jnp.bfloat16)
                for p in range(PIECES)
            ],
            axis=0,
        )
        parts = convolve(weighted, bands[m], seams[m], True)
        start = pl.multiple_of(m * TALL, TALL)
        for q in range(QCOLS):
            cols = slice(q * PW, (q + 1) * PW)
            for p in range(PIECES):
                back[p, pl.ds(start, TALL), cols] = parts[q][p * TALL:(p + 1) * TALL].astype(
                    jnp.bfloat16
                )
        return carry

    lax.fori_loop(0, MODES, adjoint, 0, unroll=MODES)
    for p in range(PIECES):
        total = jnp.dot(wide[...], back[p], preferred_element_type=jnp.float32)
        for q in range(QCOLS):
            rows[p * QCOLS + q] = total[:, q * PW:(q + 1) * PW]


def kernel(owners, offsets, sky, coeffs_far, observed_far, vert, horiz, sky_out, clipped, *scratch):
    (
        coeffs, observed, base, tall, wide, bands, seams, own_rows, off_rows, select, extra,
        table, rim_out, rim_in, ext, smooth, back, model, rows, sky_mid,
        marks_out, marks_in, marks, count_out, count_in, scale, *scratch
    ) = scratch
    load, share_sems, mark_sems, fetch_sems = scratch[0], scratch[1:3], scratch[3:7], scratch[7:15]
    reduce_refs, reduce_sems = scratch[15:20], scratch[20:]
    inner = pl.ds(HALO, HEIGHT)
    loads = [
        pltpu.make_async_copy(coeffs_far, coeffs.at[:, :, inner], load.at[0]),
        pltpu.make_async_copy(observed_far, observed.at[:, inner], load.at[1]),
    ]
    share, shared = share_rows(coeffs_far, observed_far, coeffs, observed, *share_sems)
    all_here = greet()
    for copy in loads:
        copy.start()
    own_tile(sky, table)
    build_tall(vert, base, tall)
    all_here()

    def early():
        share()
        build_wide(vert, base, wide)

    def late():
        build_bands(horiz, base, bands, seams)
        build_slots(owners, offsets, own_rows, off_rows, select, extra)

    def nothing():
        pass

    meanwhile = []
    for step in range(STEPS):
        first = step == 0
        sems = [ref.at[step] for ref in fetch_sems]
        sent = spread_tiles(table, sems[:6], early if first else nothing, late if first else nothing)
        fetch_image(owners, offsets, table, ext, rim_out, rim_in.at[step], *sems[6:], meanwhile + [sent])
        if first:
            send_marks(select, extra, marks_out, marks_in, *mark_sems[:2])
            for copy in loads:
                copy.wait()
            shared()
        tables = (tall, wide, bands, seams)
        compute(ext, coeffs, observed, tables, None if first else clipped, rows, (smooth, back, model))
        sems = [ref.at[step] for ref in reduce_sems]
        if first:
            take_marks(marks_out, marks_in, marks, count_out, count_in, mark_sems)

        def get_scale():
            if first:
                take_counts(marks_out, marks_in, count_out, count_in, scale, mark_sems)
            return scale[...]

        before, after = (sky, sky_mid) if first else (sky_mid, sky_out)
        sent = reduce_patches(rows, select, marks, get_scale, before, after, (reduce_refs, sems))
        if first:
            own_tile(sky_mid, table)
            meanwhile = [sent]
        else:
            sent()


def copy_out(sky_far, clipped_far, sky_out, clipped_out, sky, clipped, load, store):
    pairs = ((clipped_far, clipped, clipped_out), (sky_far, sky, sky_out))
    inward = [pltpu.make_async_copy(a, b, load.at[i]) for i, (a, b, _) in enumerate(pairs)]
    outward = [pltpu.make_async_copy(b, c, store.at[i]) for i, (_, b, c) in enumerate(pairs)]
    for copy in inward:
        copy.start()
    for came, goes in zip(inward, outward):
        came.wait()
        goes.start()
    for copy in outward:
        copy.wait()


def per_device(sky_map, coeffs, observed, vert_taps, horiz_taps, owner_ids, offset):
    sky = sky_map.reshape(PER_TILE * PH, PW)
    bf16, f32, i32 = jnp.bfloat16, jnp.float32, jnp.int32
    side = BREADTH // 2
    count = PIECES * QCOLS * ROWS
    dma = pltpu.SemaphoreType.DMA
    scratch = [
        pltpu.VMEM((PIECES, MODES, TALL, BREADTH), bf16),
        pltpu.VMEM((PIECES, TALL, BREADTH), f32),
        pltpu.VMEM((MODES, side), f32),
        pltpu.VMEM((MODES * TALL, EXT), bf16),
        pltpu.VMEM((HEIGHT, MODES * TALL), bf16),
        pltpu.VMEM((MODES, side, side), bf16),
        pltpu.VMEM((MODES, side, side), bf16),
        pltpu.VMEM((count, PW), i32),
        pltpu.VMEM((count, PW), i32),
        pltpu.VMEM((N_CHUNKS, COLS * CHUNK_ROWS, count), bf16),
        pltpu.VMEM((count, PW), bf16),
        pltpu.VMEM((COLS * NZ * PER_TILE, PH, PW), bf16),
        pltpu.VMEM((2, PIECES, REACH, BREADTH), bf16),
        pltpu.VMEM((STEPS, 2, PIECES, REACH, BREADTH), bf16),
        pltpu.VMEM((PIECES, EXT, BREADTH), bf16),
        pltpu.VMEM((MODES, PIECES * TALL, BREADTH), bf16),
        pltpu.VMEM((PIECES, MODES * TALL, BREADTH), bf16),
        pltpu.VMEM((PIECES, TALL, BREADTH), f32),
        pltpu.VMEM((PIECES * QCOLS, HEIGHT, PW), f32),
        pltpu.VMEM((PER_TILE * PH, PW), f32),
        pltpu.VMEM((N_CHUNKS, COLS, CHUNK_ROWS, PW), bf16),
        pltpu.VMEM((N_CHUNKS, COLS, CHUNK_ROWS, PW), bf16),
        pltpu.VMEM((N_CHUNKS, 2 * PER_TILE, COLS * CHUNK_ROWS), bf16),
        pltpu.VMEM((NZ, PER_TILE, PW), f32),
        pltpu.VMEM((NZ, PER_TILE, PW), f32),
        pltpu.VMEM((PER_TILE, PW), f32),
        dma((2,)),
        dma((2, 2)),
        dma((2, 2)),
        dma((NX, NC)),
        dma((NX, NC)),
        dma((NZ,)),
        dma((NZ,)),
        dma((STEPS, NZ)),
        dma((STEPS, NZ)),
        dma((STEPS, NZ, NX)),
        dma((STEPS, NZ, NX)),
        dma((STEPS, NZ, NX)),
        dma((STEPS, NZ, NX)),
        dma((STEPS, 2)),
        dma((STEPS, 2)),
        pltpu.VMEM((count, SIZE), bf16),
        pltpu.VMEM((N_CHUNKS, COLS, CHUNK_ROWS, SIZE), bf16),
        pltpu.VMEM((N_CHUNKS, COLS, CHUNK_ROWS, SIZE), bf16),
        pltpu.VMEM((NZ, PER_TILE, SIZE), bf16),
        pltpu.VMEM((NZ, PER_TILE, SIZE), bf16),
        dma((STEPS, N_CHUNKS, NX, NC)),
        dma((STEPS, N_CHUNKS, NX, NC)),
        dma((STEPS, NZ)),
        dma((STEPS, NZ)),
    ]
    smem, vmem, far = pltpu.SMEM, pltpu.VMEM, pl.ANY
    sky_new, clipped = pl.pallas_call(
        kernel,
        out_shape=(
            jax.ShapeDtypeStruct(sky.shape, f32),
            jax.ShapeDtypeStruct(observed.shape, f32),
        ),
        in_specs=[pl.BlockSpec(memory_space=m) for m in (smem, smem, vmem, far, far, vmem, vmem)],
        out_specs=(pl.BlockSpec(memory_space=vmem), pl.BlockSpec(memory_space=vmem)),
        scratch_shapes=scratch,
        compiler_params=pltpu.CompilerParams(
            vmem_limit_bytes=VMEM_LIMIT, collective_id=0, has_side_effects=True
        ),
    )(owner_ids.transpose(0, 2, 3, 1), offset.transpose(0, 2, 1), sky, coeffs, observed, vert_taps, horiz_taps)
    sky_new, clipped = pl.pallas_call(
        copy_out,
        out_shape=(
            jax.ShapeDtypeStruct(sky.shape, f32),
            jax.ShapeDtypeStruct(observed.shape, f32),
        ),
        in_specs=[pl.BlockSpec(memory_space=far)] * 2,
        out_specs=(pl.BlockSpec(memory_space=far), pl.BlockSpec(memory_space=far)),
        scratch_shapes=[pltpu.VMEM(sky.shape, f32), pltpu.VMEM(observed.shape, f32), dma((2,)), dma((2,))],
        compiler_params=pltpu.CompilerParams(vmem_limit_bytes=VMEM_LIMIT),
    )(sky_new, clipped)
    return sky_new.reshape(sky_map.shape), clipped


def solution(mesh):
    return jax.shard_map(
        per_device,
        mesh=mesh,
        in_specs=(
            P(("exp", "sub"), None, None, None),
            P("exp", None, "sub", None),
            P("exp", "sub", None),
            P(),
            P(),
            P("exp", "sub", None, None),
            P("exp", "sub", None),
        ),
        out_specs=(P(("exp", "sub"), None, None, None), P("exp", "sub", None)),
        check_vma=False,
    )
```

```python
import jax
import jax.numpy as jnp
from jax import lax
from jax.experimental import pallas as pl
from jax.experimental.pallas import tpu as pltpu
from jax.sharding import PartitionSpec as P

STEPS = 2
ETA = 0.5
DELTA = 1.0

NZ, NX, NC = 8, 4, 2
COLS = NX * NC
MODES = 12
TAPS = 21
MARGIN = 10
PIECES = 2
HEIGHT = 128
BREADTH = 512
HALO = 16
TALL = HEIGHT + 2 * HALO
REACH = 2 * HALO
EXT = HEIGHT + 2 * REACH
PER_TILE = 8
PH = 8
PW = 128
ROWS = HEIGHT // PH
QCOLS = BREADTH // PW
SIZE = PH * PW
NEAR_ORDER = (0, 1, 7, 2, 6, 3, 5, 4)
FAR_ORDER = (4, 3, 5, 2, 6, 1, 7)
CHUNKS = ((4, 3), (5, 2), (6, 1), (7, 0))
N_CHUNKS = len(CHUNKS)
CHUNK_ROWS = 4 * len(CHUNKS[0])
PEERS = ((2, 0), (2, 1), (1, 0), (1, 1), (3, 0), (3, 1), (0, 1))
VMEM_LIMIT = 60 * 1024 * 1024


def place():
    e = lax.axis_index("exp")
    y = lax.axis_index("sub")
    return e // COLS, lax.rem(e // NC, NX), lax.rem(e, NC), y


def at_exp(z, x, c):
    return {"exp": (z * NX + x) * NC + c}


def remote(src, dst, send_sem, recv_sem, device):
    return pltpu.make_async_remote_copy(
        src_ref=src, dst_ref=dst, send_sem=send_sem, recv_sem=recv_sem,
        device_id=device, device_id_type=pl.DeviceIdType.MESH,
    )


def greet():
    z, x, c, y = place()
    barrier = pltpu.get_barrier_semaphore()
    many = 0
    for dz in range(1, NZ):
        pl.semaphore_signal(barrier, inc=1, device_id=at_exp(lax.rem(z + dz, NZ), x, c))
        many += 1
    for dx in range(NX):
        for dc in range(NC):
            if dx + dc > 0:
                pl.semaphore_signal(
                    barrier, inc=1, device_id=at_exp(z, lax.rem(x + dx, NX), lax.rem(c + dc, NC))
                )
                many += 1
    bands = lax.axis_size("sub")

    @pl.when(y > 0)
    def _():
        pl.semaphore_signal(barrier, inc=1, device_id={"sub": y - 1})

    @pl.when(y < bands - 1)
    def _():
        pl.semaphore_signal(barrier, inc=1, device_id={"sub": y + 1})

    return lambda: pl.semaphore_wait(
        barrier, many + jnp.minimum(y, 1) + jnp.minimum(bands - 1 - y, 1)
    )


def spread_tiles(table, sems, early, late):
    (zs, zr, xs, xr, cs, cr) = sems
    z, x, c, _ = place()
    col = x * NC + c

    def tile(col_at, z_at):
        return table.at[pl.ds((col_at * NZ + z_at) * PER_TILE, PER_TILE)]

    def along_z(dz, back):
        z_from = lax.rem(z - dz + NZ, NZ) if back else z
        block = tile(col, z_from)
        return remote(block, block, zs.at[dz], zr.at[dz], at_exp(lax.rem(z + dz, NZ), x, c))

    def along_x(dz, dx, back):
        x_from = lax.rem(x - dx + NX, NX) if back else x
        block = tile(x_from * NC + c, lax.rem(z - dz + NZ, NZ))
        return remote(block, block, xs.at[dz, dx], xr.at[dz, dx], at_exp(z, lax.rem(x + dx, NX), c))

    def to_twin(dz, dx, back):
        c_from = 1 - c if back else c
        block = tile(lax.rem(x - dx + NX, NX) * NC + c_from, lax.rem(z - dz + NZ, NZ))
        return remote(block, block, cs.at[dz, dx], cr.at[dz, dx], at_exp(z, x, 1 - c))

    for dz in FAR_ORDER:
        along_z(dz, False).start()
    early()
    for dz in NEAR_ORDER:
        if dz > 0:
            along_z(dz, True).wait_recv()
        for dx in (2, 1, 3):
            along_x(dz, dx, False).start()
        to_twin(dz, 0, False).start()
    late()
    for dz in NEAR_ORDER:
        for dx in (1, 3, 2):
            along_x(dz, dx, True).wait_recv()
            to_twin(dz, dx, False).start()
    for dz in NEAR_ORDER:
        for dx in range(NX):
            to_twin(dz, dx, True).wait_recv()

    def sent():
        for dz in range(NZ):
            if dz > 0:
                along_z(dz, False).wait_send()
            for dx in range(NX):
                if dx > 0:
                    along_x(dz, dx, False).wait_send()
                to_twin(dz, dx, False).wait_send()

    return sent


def gather_rows(owners, offsets, table, ext, pair):
    for p in range(PIECES):
        for q in range(QCOLS):
            both = []
            for half in range(2):
                r = pair * 2 + half
                owner = owners[p, q, 0, r]
                tile = lax.rem(owner, COLS) * NZ + owner // COLS
                both.append(table[tile * PER_TILE + offsets[p, q, r]].astype(jnp.float32))
            block = jnp.concatenate(both, axis=0).astype(jnp.bfloat16)
            if isinstance(pair, int):
                start = REACH + pair * 2 * PH
            else:
                start = pl.multiple_of(REACH + pair * 2 * PH, 2 * PH)
            ext[p, pl.ds(start, 2 * PH), q * PW:(q + 1) * PW] = block


def fetch_image(owners, offsets, table, ext, rim_out, rim_in, hs, hr, meanwhile):
    _, _, _, y = place()
    bands = lax.axis_size("sub")
    pairs = ROWS // 2
    for pair in (0, 1, pairs - 2, pairs - 1):
        gather_rows(owners, offsets, table, ext, pair)
    rim_out[0] = ext[:, REACH:2 * REACH, :]
    rim_out[1] = ext[:, HEIGHT:HEIGHT + REACH, :]
    up = remote(rim_out.at[0], rim_in.at[1], hs.at[0], hr.at[1], {"sub": y - 1})
    down = remote(rim_out.at[1], rim_in.at[0], hs.at[1], hr.at[0], {"sub": y + 1})

    @pl.when(y > 0)
    def _():
        up.start()

    @pl.when(y < bands - 1)
    def _():
        down.start()

    def more(pair, carry):
        gather_rows(owners, offsets, table, ext, pair)
        return carry

    lax.fori_loop(2, pairs - 2, more, 0)
    for finish in meanwhile:
        finish()

    def arrive():
        none = jnp.zeros((PIECES, REACH, BREADTH), jnp.bfloat16)

        @pl.when(y > 0)
        def _():
            down.wait_recv()
            ext[:, 0:REACH, :] = rim_in[0]

        @pl.when(y == 0)
        def _():
            ext[:, 0:REACH, :] = none

        @pl.when(y < bands - 1)
        def _():
            up.wait_recv()
            ext[:, REACH + HEIGHT:EXT, :] = rim_in[1]

        @pl.when(y == bands - 1)
        def _():
            ext[:, REACH + HEIGHT:EXT, :] = none

        @pl.when(y > 0)
        def _():
            up.wait_send()

        @pl.when(y < bands - 1)
        def _():
            down.wait_send()

    return arrive


def across(outgoing, incoming, send_sem, recv_sem, dx, dc, back, every=False):
    z, x, c, _ = place()
    x_to, c_to = lax.rem(x + dx, NX), lax.rem(c + dc, NC)
    x_from, c_from = (lax.rem(x - dx + NX, NX), c_to) if back else (x, c)
    to_at, from_at = x_to * NC + c_to, x_from * NC + c_from
    return remote(
        outgoing.at[:, to_at] if every else outgoing.at[to_at],
        incoming.at[:, from_at] if every else incoming.at[from_at],
        send_sem.at[dx, dc], recv_sem.at[dx, dc], at_exp(z, x_to, c_to),
    )


def along_line(outgoing, incoming, send_sem, recv_sem, rel):
    z, x, c, _ = place()
    return remote(
        outgoing.at[rel], incoming.at[rel], send_sem.at[rel], recv_sem.at[rel],
        at_exp(lax.rem(z + rel, NZ), x, c),
    )


def send_marks(select, extra, marks_out, marks_in, send_sem, recv_sem):
    z, x, c, _ = place()
    col = x * NC + c
    for chunk in range(N_CHUNKS):
        picked = jnp.dot(select[chunk], extra[...], preferred_element_type=jnp.float32)
        marks_out[chunk] = picked.reshape(COLS, CHUNK_ROWS, PW).astype(jnp.bfloat16)
    for dx, dc in PEERS:
        across(marks_out, marks_in, send_sem, recv_sem, dx, dc, False, True).start()
    marks_in[:, col] = marks_out[:, col]


def take_marks(marks_out, marks_in, marks, count_out, count_in, sems):
    send_sem, recv_sem, line_send, line_recv = sems
    for dx, dc in PEERS:
        across(marks_out, marks_in, send_sem, recv_sem, dx, dc, True, True).wait_recv()
    for chunk in range(N_CHUNKS):
        arrived = marks_in[chunk].astype(jnp.float32).reshape(COLS * CHUNK_ROWS, PW)
        turned = arrived.T[0:2 * PER_TILE].astype(jnp.bfloat16)
        marks[chunk] = turned
        many = jnp.dot(
            turned, jnp.ones((COLS * CHUNK_ROWS, PW), jnp.bfloat16), preferred_element_type=jnp.float32
        )
        for pos, rel in enumerate(CHUNKS[chunk]):
            count_out[rel] = many[pos * PER_TILE:(pos + 1) * PER_TILE]
    for rel in FAR_ORDER:
        along_line(count_out, count_in, line_send, line_recv, rel).start()


def take_counts(marks_out, marks_in, count_out, count_in, scale, sems):
    send_sem, recv_sem, line_send, line_recv = sems
    for dx, dc in PEERS:
        across(marks_out, marks_in, send_sem, recv_sem, dx, dc, False, True).wait_send()
    total = count_out[0]
    for rel in NEAR_ORDER[1:]:
        along_line(count_out, count_in, line_send, line_recv, rel).wait_recv()
        total = total + count_in[rel]
    scale[...] = ETA / jnp.maximum(total, 1.0)
    for rel in FAR_ORDER:
        along_line(count_out, count_in, line_send, line_recv, rel).wait_send()


def share_rows(coeffs_far, observed_far, coeffs, observed, hs, hr):
    _, _, _, y = place()
    bands = lax.axis_size("sub")
    ends = (pl.ds(0, HALO), pl.ds(HALO + HEIGHT, HALO))
    edges = (pl.ds(0, HALO), pl.ds(HEIGHT - HALO, HALO))

    def pair(side, to):
        coming = ends[1 - side]
        return (
            remote(
                coeffs_far.at[:, :, edges[side]], coeffs.at[:, :, coming],
                hs.at[side, 0], hr.at[1 - side, 0], {"sub": to},
            ),
            remote(
                observed_far.at[:, edges[side]], observed.at[:, coming],
                hs.at[side, 1], hr.at[1 - side, 1], {"sub": to},
            ),
        )

    up, down = pair(0, y - 1), pair(1, y + 1)

    def start():
        @pl.when(y > 0)
        def _():
            for copy in up:
                copy.start()

        @pl.when(y < bands - 1)
        def _():
            for copy in down:
                copy.start()

        @pl.when(y == 0)
        def _():
            coeffs[:, :, ends[0]] = jnp.zeros((PIECES, MODES, HALO, BREADTH), jnp.bfloat16)
            observed[:, ends[0]] = jnp.zeros((PIECES, HALO, BREADTH), jnp.float32)

        @pl.when(y == bands - 1)
        def _():
            coeffs[:, :, ends[1]] = jnp.zeros((PIECES, MODES, HALO, BREADTH), jnp.bfloat16)
            observed[:, ends[1]] = jnp.zeros((PIECES, HALO, BREADTH), jnp.float32)

    def wait():
        @pl.when(y > 0)
        def _():
            for copy in down:
                copy.wait_recv()
            for copy in up:
                copy.wait_send()

        @pl.when(y < bands - 1)
        def _():
            for copy in up:
                copy.wait_recv()
            for copy in down:
                copy.wait_send()

    return start, wait


def reduce_patches(rows, select, marks, get_scale, sky, sky_new, scratch):
    (stacked, outgoing, incoming, line_out, line_in), sems = scratch
    axs, axr, bzs, bzr = sems
    _, x, c, _ = place()
    col = x * NC + c
    for n in range(PIECES * QCOLS):
        for i in range(PH):
            lines = rows[n, pl.ds(i, ROWS, stride=PH), :]
            stacked[n * ROWS:(n + 1) * ROWS, i * PW:(i + 1) * PW] = lines.astype(jnp.bfloat16)

    def exchange(chunk, dx, dc, back):
        return across(
            outgoing.at[chunk], incoming.at[chunk], axs.at[chunk], axr.at[chunk], dx, dc, back
        )

    for chunk in range(N_CHUNKS):
        picked = jnp.dot(select[chunk], stacked[...], preferred_element_type=jnp.float32)
        outgoing[chunk] = picked.reshape(COLS, CHUNK_ROWS, SIZE).astype(jnp.bfloat16)
        for dx, dc in PEERS:
            exchange(chunk, dx, dc, False).start()
        incoming[chunk, col] = outgoing[chunk, col]
    for chunk in range(N_CHUNKS):
        for dx, dc in PEERS[::-1]:
            exchange(chunk, dx, dc, True).wait_recv()
        arrived = incoming[chunk].astype(jnp.float32).reshape(COLS * CHUNK_ROWS, SIZE)
        totals = jnp.dot(
            marks[chunk], arrived.astype(jnp.bfloat16), preferred_element_type=jnp.float32
        )
        for pos, rel in enumerate(CHUNKS[chunk]):
            line_out[rel] = totals[pos * PER_TILE:(pos + 1) * PER_TILE].astype(jnp.bfloat16)
            if rel > 0:
                along_line(line_out, line_in, bzs, bzr, rel).start()
    scale = get_scale()
    for chunk in range(N_CHUNKS):
        for dx, dc in PEERS:
            exchange(chunk, dx, dc, False).wait_send()
    total = line_out[0].astype(jnp.float32)
    for rel in NEAR_ORDER[1:]:
        along_line(line_out, line_in, bzs, bzr, rel).wait_recv()
        total = total + line_in[rel].astype(jnp.float32)
    for i in range(PH):
        old = sky[pl.ds(i, PER_TILE, stride=PH), :]
        sky_new[pl.ds(i, PER_TILE, stride=PH), :] = old - scale * total[:, i * PW:(i + 1) * PW]

    def sent():
        for rel in range(1, NZ):
            along_line(line_out, line_in, bzs, bzr, rel).wait_send()

    return sent


def own_tile(sky, table):
    z, x, c, _ = place()
    start = ((x * NC + c) * NZ + z) * PER_TILE
    for k in range(PER_TILE):
        table[start + k] = sky[k * PH:(k + 1) * PH, :].astype(jnp.bfloat16)


def convolve(block, centre, edge, transposed):
    dims = (((1,), (1 if transposed else 0,)), ((), ()))
    half = BREADTH // 2

    def product(a, b):
        return lax.dot_general(a, b, dims, preferred_element_type=jnp.float32)

    left = product(block[:, :half], centre)
    right = product(block[:, half:], centre)
    seam = product(block[:, PW:PW + half], edge)
    return [left[:, :PW], left[:, PW:] + seam[:, :PW], right[:, :PW] + seam[:, PW:], right[:, PW:]]


def diagonals(row, height):
    return pltpu.roll(jnp.broadcast_to(row, (height, row.shape[1])), 0, 1, stride=1, stride_axis=0)


def lag_rows(taps, lag):
    tap = lax.broadcasted_iota(jnp.int32, (TAPS, 2 * PW), 0)
    lane = lax.broadcasted_iota(jnp.int32, (TAPS, 2 * PW), 1)
    chosen = (tap == lag(lane)).astype(jnp.bfloat16)
    return jnp.dot(taps[...], chosen, preferred_element_type=jnp.float32)


def wrapped(lane):
    return jnp.where(lane < PW, lane, lane - 2 * PW)


def build_tall(vert, base, tall):
    base[...] = lag_rows(vert, lambda lane: lane - HALO + MARGIN)

    def one(m, carry):
        rows = diagonals(base[pl.ds(m, 1), :], TALL)
        tall[pl.ds(pl.multiple_of(m * TALL, TALL), TALL), :] = rows[:, :EXT].astype(jnp.bfloat16)
        return carry

    lax.fori_loop(0, MODES, one, 0)


def build_wide(vert, base, wide):
    base[...] = lag_rows(vert, lambda lane: HALO + MARGIN - lane)
    for m in range(MODES):
        rows = diagonals(base[m:m + 1, :], HEIGHT)
        wide[:, m * TALL:(m + 1) * TALL] = rows[:, :TALL].astype(jnp.bfloat16)


def build_bands(horiz, base, bands, seams):
    base[...] = lag_rows(horiz, lambda lane: MARGIN - wrapped(lane))
    side = BREADTH // 2
    w = lax.broadcasted_iota(jnp.int32, (side, side), 0)
    c = lax.broadcasted_iota(jnp.int32, (side, side), 1)
    near = jnp.abs(w - c) <= MARGIN
    across = near & ((w < PW) != (c < PW))

    def one(m, carry):
        rows = diagonals(base[pl.ds(m, 1), :], side)
        bands[m] = jnp.where(near, rows, 0.0).astype(jnp.bfloat16)
        seams[m] = jnp.where(across, rows, 0.0).astype(jnp.bfloat16)
        return carry

    lax.fori_loop(0, MODES, one, 0)


def build_slots(owners, offsets, own_rows, off_rows, select, extra):
    z, _, _, _ = place()

    def one(r, carry):
        for p in range(PIECES):
            for q in range(QCOLS):
                n = (p * QCOLS + q) * ROWS + r
                own_rows[pl.ds(n, 1), :] = jnp.full((1, PW), owners[p, q, 0, r], jnp.int32)
                off_rows[pl.ds(n, 1), :] = jnp.full((1, PW), offsets[p, q, r], jnp.int32)
        return carry

    lax.fori_loop(0, ROWS, one, 0)
    count = PIECES * QCOLS * ROWS
    down = lax.broadcasted_iota(jnp.int32, (count, count), 0)
    along = lax.broadcasted_iota(jnp.int32, (count, count), 1)
    per_piece = QCOLS * ROWS
    own = own_rows[...]
    own_along = own.T
    earlier = (own == own_along) & (down < along) & ((down < per_piece) == (along < per_piece))
    rank = jnp.sum(earlier.astype(jnp.int32), axis=0, keepdims=True)
    across = own_along[0:1, :]

    def turned(owner):
        far = lax.rem(owner // COLS - z + NZ + NZ // 2, NZ)
        return jnp.where(far < NZ // 2, 2 * far, 2 * (NZ - far) - 1)

    spin = turned(across)
    chunk, pos = spin // 2, lax.rem(spin, 2)
    piece = along[0:1, :] // per_piece
    slot = ((chunk * COLS + lax.rem(across, COLS)) * 2 + pos) * 4 + piece * 2 + rank
    size = COLS * CHUNK_ROWS
    for h in range(N_CHUNKS):
        select[h] = (down[0:size] + h * size == slot).astype(jnp.bfloat16)
    mark = lax.rem(turned(own), 2) * PER_TILE + off_rows[...]
    extra[...] = (mark == along).astype(jnp.bfloat16)


def compute(ext, coeffs, observed, tables, clipped, rows, scratch, arrive):
    tall, wide, bands, seams = tables
    smooth, back, model = scratch
    model[...] = -observed[...]

    def ahead(ranges):
        lengths = [b - a for a, b in ranges]
        starts = [sum(lengths[:i]) for i in range(len(ranges))]
        for p in range(PIECES):
            for m in range(MODES):
                lines = [tall[m * TALL + a:m * TALL + b, :] for a, b in ranges]
                result = jnp.dot(
                    jnp.concatenate(lines, axis=0), ext[p], preferred_element_type=jnp.float32
                ).astype(jnp.bfloat16)
                for (a, b), at in zip(ranges, starts):
                    smooth[m, p * TALL + a:p * TALL + b, :] = result[at:at + b - a]

        def forward(m, carry):
            block = jnp.concatenate(
                [smooth[m, p * TALL + a:p * TALL + b, :] for p in range(PIECES) for a, b in ranges],
                axis=0,
            )
            parts = convolve(block, bands[m], seams[m], False)
            for q in range(QCOLS):
                cols = slice(q * PW, (q + 1) * PW)
                for p in range(PIECES):
                    for (a, b), at in zip(ranges, starts):
                        at = at + p * sum(lengths)
                        model[p, a:b, cols] += (
                            coeffs[p, m, a:b, cols].astype(jnp.float32) * parts[q][at:at + b - a]
                        )
            return carry

        lax.fori_loop(0, MODES, forward, 0, unroll=MODES)

    ahead(((REACH, HEIGHT),))
    arrive()
    ahead(((0, REACH), (HEIGHT, TALL)))
    model[...] = jnp.clip(model[...], -DELTA, DELTA)
    if clipped is not None:
        clipped[...] = model[:, HALO:HALO + HEIGHT, :]

    def adjoint(m, carry):
        weighted = jnp.concatenate(
            [
                (coeffs[p, m].astype(jnp.float32) * model[p]).astype(jnp.bfloat16)
                for p in range(PIECES)
            ],
            axis=0,
        )
        parts = convolve(weighted, bands[m], seams[m], True)
        start = pl.multiple_of(m * TALL, TALL)
        for q in range(QCOLS):
            cols = slice(q * PW, (q + 1) * PW)
            for p in range(PIECES):
                back[p, pl.ds(start, TALL), cols] = parts[q][p * TALL:(p + 1) * TALL].astype(
                    jnp.bfloat16
                )
        return carry

    lax.fori_loop(0, MODES, adjoint, 0, unroll=MODES)
    for p in range(PIECES):
        total = jnp.dot(wide[...], back[p], preferred_element_type=jnp.float32)
        for q in range(QCOLS):
            rows[p * QCOLS + q] = total[:, q * PW:(q + 1) * PW]


def kernel(owners, offsets, sky, coeffs_far, observed_far, vert, horiz, sky_out, clipped, *scratch):
    (
        coeffs, observed, base, tall, wide, bands, seams, own_rows, off_rows, select, extra,
        table, rim_out, rim_in, ext, smooth, back, model, rows, sky_mid,
        marks_out, marks_in, marks, count_out, count_in, scale, *scratch
    ) = scratch
    load, share_sems, mark_sems, fetch_sems = scratch[0], scratch[1:3], scratch[3:7], scratch[7:15]
    reduce_refs, reduce_sems = scratch[15:20], scratch[20:]
    inner = pl.ds(HALO, HEIGHT)
    loads = [
        pltpu.make_async_copy(coeffs_far, coeffs.at[:, :, inner], load.at[0]),
        pltpu.make_async_copy(observed_far, observed.at[:, inner], load.at[1]),
    ]
    share, shared = share_rows(coeffs_far, observed_far, coeffs, observed, *share_sems)
    all_here = greet()
    for copy in loads:
        copy.start()
    own_tile(sky, table)
    for rim in (slice(0, REACH), slice(REACH + HEIGHT, EXT)):
        ext[:, rim, :] = jnp.zeros((PIECES, REACH, BREADTH), jnp.bfloat16)
    build_tall(vert, base, tall)
    all_here()

    def early():
        share()
        build_wide(vert, base, wide)

    def late():
        build_bands(horiz, base, bands, seams)
        build_slots(owners, offsets, own_rows, off_rows, select, extra)

    def nothing():
        pass

    meanwhile = []
    for step in range(STEPS):
        first = step == 0
        sems = [ref.at[step] for ref in fetch_sems]
        sent = spread_tiles(table, sems[:6], early if first else nothing, late if first else nothing)
        arrive = fetch_image(owners, offsets, table, ext, rim_out, rim_in.at[step], *sems[6:], meanwhile + [sent])
        if first:
            send_marks(select, extra, marks_out, marks_in, *mark_sems[:2])
            for copy in loads:
                copy.wait()
            shared()
        tables = (tall, wide, bands, seams)
        compute(ext, coeffs, observed, tables, None if first else clipped, rows, (smooth, back, model), arrive)
        sems = [ref.at[step] for ref in reduce_sems]
        if first:
            take_marks(marks_out, marks_in, marks, count_out, count_in, mark_sems)

        def get_scale():
            if first:
                take_counts(marks_out, marks_in, count_out, count_in, scale, mark_sems)
            return scale[...]

        before, after = (sky, sky_mid) if first else (sky_mid, sky_out)
        sent = reduce_patches(rows, select, marks, get_scale, before, after, (reduce_refs, sems))
        if first:
            own_tile(sky_mid, table)
            meanwhile = [sent]
        else:
            sent()


def copy_out(sky_far, clipped_far, sky_out, clipped_out, sky, clipped, load, store):
    pairs = ((clipped_far, clipped, clipped_out), (sky_far, sky, sky_out))
    inward = [pltpu.make_async_copy(a, b, load.at[i]) for i, (a, b, _) in enumerate(pairs)]
    outward = [pltpu.make_async_copy(b, c, store.at[i]) for i, (_, b, c) in enumerate(pairs)]
    for copy in inward:
        copy.start()
    for came, goes in zip(inward, outward):
        came.wait()
        goes.start()
    for copy in outward:
        copy.wait()


def per_device(sky_map, coeffs, observed, vert_taps, horiz_taps, owner_ids, offset):
    sky = sky_map.reshape(PER_TILE * PH, PW)
    bf16, f32, i32 = jnp.bfloat16, jnp.float32, jnp.int32
    side = BREADTH // 2
    count = PIECES * QCOLS * ROWS
    dma = pltpu.SemaphoreType.DMA
    scratch = [
        pltpu.VMEM((PIECES, MODES, TALL, BREADTH), bf16),
        pltpu.VMEM((PIECES, TALL, BREADTH), f32),
        pltpu.VMEM((MODES, side), f32),
        pltpu.VMEM((MODES * TALL, EXT), bf16),
        pltpu.VMEM((HEIGHT, MODES * TALL), bf16),
        pltpu.VMEM((MODES, side, side), bf16),
        pltpu.VMEM((MODES, side, side), bf16),
        pltpu.VMEM((count, PW), i32),
        pltpu.VMEM((count, PW), i32),
        pltpu.VMEM((N_CHUNKS, COLS * CHUNK_ROWS, count), bf16),
        pltpu.VMEM((count, PW), bf16),
        pltpu.VMEM((COLS * NZ * PER_TILE, PH, PW), bf16),
        pltpu.VMEM((2, PIECES, REACH, BREADTH), bf16),
        pltpu.VMEM((STEPS, 2, PIECES, REACH, BREADTH), bf16),
        pltpu.VMEM((PIECES, EXT, BREADTH), bf16),
        pltpu.VMEM((MODES, PIECES * TALL, BREADTH), bf16),
        pltpu.VMEM((PIECES, MODES * TALL, BREADTH), bf16),
        pltpu.VMEM((PIECES, TALL, BREADTH), f32),
        pltpu.VMEM((PIECES * QCOLS, HEIGHT, PW), f32),
        pltpu.VMEM((PER_TILE * PH, PW), f32),
        pltpu.VMEM((N_CHUNKS, COLS, CHUNK_ROWS, PW), bf16),
        pltpu.VMEM((N_CHUNKS, COLS, CHUNK_ROWS, PW), bf16),
        pltpu.VMEM((N_CHUNKS, 2 * PER_TILE, COLS * CHUNK_ROWS), bf16),
        pltpu.VMEM((NZ, PER_TILE, PW), f32),
        pltpu.VMEM((NZ, PER_TILE, PW), f32),
        pltpu.VMEM((PER_TILE, PW), f32),
        dma((2,)),
        dma((2, 2)),
        dma((2, 2)),
        dma((NX, NC)),
        dma((NX, NC)),
        dma((NZ,)),
        dma((NZ,)),
        dma((STEPS, NZ)),
        dma((STEPS, NZ)),
        dma((STEPS, NZ, NX)),
        dma((STEPS, NZ, NX)),
        dma((STEPS, NZ, NX)),
        dma((STEPS, NZ, NX)),
        dma((STEPS, 2)),
        dma((STEPS, 2)),
        pltpu.VMEM((count, SIZE), bf16),
        pltpu.VMEM((N_CHUNKS, COLS, CHUNK_ROWS, SIZE), bf16),
        pltpu.VMEM((N_CHUNKS, COLS, CHUNK_ROWS, SIZE), bf16),
        pltpu.VMEM((NZ, PER_TILE, SIZE), bf16),
        pltpu.VMEM((NZ, PER_TILE, SIZE), bf16),
        dma((STEPS, N_CHUNKS, NX, NC)),
        dma((STEPS, N_CHUNKS, NX, NC)),
        dma((STEPS, NZ)),
        dma((STEPS, NZ)),
    ]
    smem, vmem, far = pltpu.SMEM, pltpu.VMEM, pl.ANY
    sky_new, clipped = pl.pallas_call(
        kernel,
        out_shape=(
            jax.ShapeDtypeStruct(sky.shape, f32),
            jax.ShapeDtypeStruct(observed.shape, f32),
        ),
        in_specs=[pl.BlockSpec(memory_space=m) for m in (smem, smem, vmem, far, far, vmem, vmem)],
        out_specs=(pl.BlockSpec(memory_space=vmem), pl.BlockSpec(memory_space=vmem)),
        scratch_shapes=scratch,
        compiler_params=pltpu.CompilerParams(
            vmem_limit_bytes=VMEM_LIMIT, collective_id=0, has_side_effects=True
        ),
    )(owner_ids.transpose(0, 2, 3, 1), offset.transpose(0, 2, 1), sky, coeffs, observed, vert_taps, horiz_taps)
    sky_new, clipped = pl.pallas_call(
        copy_out,
        out_shape=(
            jax.ShapeDtypeStruct(sky.shape, f32),
            jax.ShapeDtypeStruct(observed.shape, f32),
        ),
        in_specs=[pl.BlockSpec(memory_space=far)] * 2,
        out_specs=(pl.BlockSpec(memory_space=far), pl.BlockSpec(memory_space=far)),
        scratch_shapes=[pltpu.VMEM(sky.shape, f32), pltpu.VMEM(observed.shape, f32), dma((2,)), dma((2,))],
        compiler_params=pltpu.CompilerParams(vmem_limit_bytes=VMEM_LIMIT),
    )(sky_new, clipped)
    return sky_new.reshape(sky_map.shape), clipped


def solution(mesh):
    return jax.shard_map(
        per_device,
        mesh=mesh,
        in_specs=(
            P(("exp", "sub"), None, None, None),
            P("exp", None, "sub", None),
            P("exp", "sub", None),
            P(),
            P(),
            P("exp", "sub", None, None),
            P("exp", "sub", None),
        ),
        out_specs=(P(("exp", "sub"), None, None, None), P("exp", "sub", None)),
        check_vma=False,
    )
```
